128 devices in a mesh: req: 8 (over x, core), seq: 16 (over y, z).
Axes of the slice: x: 4, y: 4, z: 4, core: 2. Of those that a mesh axis runs over, the one named last changes fastest.
Arguments:
- conv_input: bfloat16 [8, 8192, 5120], P('req', 'seq'), may hold values from -6 to 6
- gate_projected: bfloat16 [8, 8192, 4096], P('req', 'seq'), may hold values from -6 to 6
- step_raw: float32 [8, 8192, 64], P('req', 'seq'), may hold values from -1.5 to 6.5
- step_bias: float32 [64], replicated, may hold values from -16 to -3
- decay_log: float32 [64], replicated, may hold values from -0.35 to 0.35
- head_direct_gain: float32 [64], replicated, may hold values from 0.2 to 1
- conv_weight: float32 [4, 5120], replicated, may hold values from -3 to 3
- convolution_bias: float32 [5120], replicated, may hold values from -0.5 to 0.5
- norm_weight: float32 [4096], replicated, may hold values from 0.5 to 1.5
- lengths: int32 [8, 4], P('req'), may hold values from 1 to 4096, 8192 in all within a row
- out_weight: bfloat16 [4096, 4096], P(('req', 'seq')), may hold values from -0.375 to 0.375
- residual_last: bfloat16 [8, 4, 4096], replicated, may hold values from -6 to 6
- final_gain: float32 [4096], replicated, may hold values from 0.5 to 1.5
- vocab_weight: bfloat16 [131072, 4096], P(('req', 'seq')), may hold values from -0.25 to 0.25
Outputs:
- y_gated: bfloat16 [8, 8192, 4096], P('req', 'seq')
- final_states: float32 [8, 4, 64, 64, 128], P('req', None, 'seq')
- last_hidden: bfloat16 [8, 4, 4096], P('req')
- max_logit: float32 [8, 4], P('req')
The draws below stay inside these ranges and needn't reach their ends.
Inputs may be any that keep to these rules, and one draw needn't show every extreme that they name: The 4 lengths of a row sum to 8192.
All inputs are finite; a program needn't handle non-finite values.
Results may differ from the reference program's by a relative error of at most 0.0046.
Values may be sent and summed in bfloat16 or wider, within the bound.
A program may use at most 256 MiB of HBM per device.

```python
import math
import jax
import jax.numpy as jnp
import numpy as np
from jax import lax

D = 4096
HEADS = 64
CHANNEL_WIDTH = 64
GROUPS = 4
STATE = 128
KERNEL = 4
BLOCK = 256
VOCAB = 131072
SEQS = 4
INNER = 4096
CONV = 5120
ROWS = 8
LEN = 8192


def draw_step_bias(key, part):
    first_key, second_key, third_key = jax.random.split(key, 3)
    share = 0.5
    quick = jax.random.uniform(first_key, (HEADS,)) < share
    fast = 1.0 / 40.0 * jnp.exp(jax.random.uniform(second_key, (HEADS,), minval=-0.3, maxval=0.3))
    slow = jnp.exp(jax.random.uniform(third_key, (HEADS,), minval=-0.7, maxval=0.2)) / LEN
    rate = jnp.where(quick, fast, slow)
    return jnp.log(jnp.expm1(rate)).astype(jnp.float32)


def draw_step_raw(key, part):
    first_key, second_key = jax.random.split(key, 2)
    gaussian_jitter = jnp.clip(0.3 * jax.random.normal(first_key, (ROWS, LEN, HEADS)), -1.5, 1.5)
    opening_offsets = jax.random.randint(second_key, (ROWS, 3), 0, LEN)
    run_length = max(LEN // 256, 1)
    places = jnp.arange(LEN)
    within_tile = (places[None, None, :] >= opening_offsets[:, :, None]) & (places[None, None, :] < opening_offsets[:, :, None] + run_length)
    packed_stretch = jnp.any(within_tile, axis=1).astype(jnp.float32)
    return (gaussian_jitter + 5.0 * packed_stretch[:, :, None]).astype(jnp.float32)


def raised(drawn, rng, source, target, parts, factor):
    def block_of(position):
        return (jnp.arange(drawn.shape[position]) // (drawn.shape[position] // parts)).reshape((-1,) + (1,) * (drawn.ndim - 1 - position))

    near = jax.random.permutation(rng, parts)[block_of(target)]
    other_side = (block_of(target) + parts // 2) % parts
    return jnp.where((block_of(source) == near) | (block_of(source) == other_side), factor * drawn, drawn)


def steps_of(stream_key, shape, cuts, low, high):
    def one(axis_at, shards_of):
        heights = jax.random.uniform(jax.random.fold_in(jax.random.fold_in(stream_key, 6), axis_at), (shards_of,), jnp.float32, low / len(cuts), high / len(cuts))
        return jnp.repeat(jnp.exp(heights), shape[axis_at] // shards_of).reshape((-1,) + (1,) * (len(shape) - axis_at - 1))

    loudness = one(*cuts[0])
    for cut in cuts[1:]:
        loudness = loudness * one(*cut)
    return loudness


def length_profile(amount, total, most, skew):
    weights = [(1 << 20) // math.isqrt(standing ** skew) + 1 for standing in range(2, amount + 1)]
    rest, holding = total - most - (amount - 1), [1] * (amount - 1)
    while rest > 0:
        candidates = [i for i in range(amount - 1) if holding[i] < most]
        mass, remaining = sum([weights[i] for i in candidates]), rest
        for i in candidates:
            addition = min(most - holding[i], max(1, remaining * weights[i] // mass), rest)
            holding[i] = holding[i] + addition
            rest = rest - addition
    return np.array([most] + holding)


def uneven_parts(stream_key, number_of, total, limit, lean):
    if number_of == 2:
        one = jax.random.randint(stream_key, (), max(1, total - limit), min(limit, total - 1) + 1)
        return jnp.stack([one, total - one])
    sizes = jnp.asarray(length_profile(number_of, total, limit, lean), jnp.int32)
    twos = (number_of - 1) // 2
    giver, sink = sizes[1:1 + 2 * twos:2], sizes[2:2 + 2 * twos:2]
    slack = jnp.minimum(giver - 1, limit - sink)
    shifted = jax.random.randint(jax.random.fold_in(stream_key, 1), (twos,), 0, 1 << 20) % (slack + 1)
    sizes = sizes.at[1:1 + 2 * twos:2].set(giver - shifted).at[2:2 + 2 * twos:2].set(sink + shifted)
    return sizes[jax.random.permutation(jax.random.fold_in(stream_key, 2), number_of)]


def bell_draw(key, extent, scale, bound, cuts=(), kind=jnp.bfloat16):
    result = jax.random.normal(key, extent, jnp.float32) * scale
    if len(cuts) > 0:
        result = steps_of(key, extent, cuts, -0.22, 0.18) * result
    return jnp.clip(result, min=-bound, max=bound).astype(kind)


def heavy_noise(own_key, dims, scale, bound, cuts, heavy, held_as=jnp.bfloat16):
    result = scale * jax.random.normal(own_key, dims, jnp.float32)
    if cuts:
        result = result * steps_of(own_key, dims, cuts, -0.22, 0.18)
    return jnp.clip(raised(result, jax.random.fold_in(own_key, 3), *heavy), -bound, bound).astype(held_as)


def setup_inputs(seed: int = 0) -> dict:
    seeds = jax.random.split(jax.random.key(seed), 15)
    conv_input = bell_draw(seeds[0], (ROWS, LEN, CONV), 1.0, 6.0, ((0, 8), (1, 16)))
    gate_projected = bell_draw(seeds[1], (ROWS, LEN, INNER), 1.0, 6.0, ((0, 8), (1, 16)))
    step_raw = draw_step_raw(jax.random.fold_in(seeds[14], 71), 0)
    step_bias = draw_step_bias(jax.random.fold_in(seeds[14], 71), 0)
    decay_log = jnp.clip(jax.random.uniform(seeds[4], (HEADS,), jnp.float32, -0.35, 0.35), -0.35, 0.35)
    head_direct_gain = jnp.clip(jax.random.uniform(seeds[5], (HEADS,), jnp.float32, 0.2, 1.0), 0.2, 1.0)
    conv_weight = bell_draw(seeds[6], (KERNEL, CONV), KERNEL ** -0.5, 3.0, (), jnp.float32)
    convolution_bias = jnp.clip(jax.random.uniform(seeds[7], (CONV,), jnp.float32, -0.5, 0.5), -0.5, 0.5)
    norm_weight = jnp.clip(1.0 + 0.1 * jax.random.normal(seeds[8], (INNER,), jnp.float32), 0.5, 1.5)
    lengths = jax.vmap(lambda own: uneven_parts(own, SEQS, LEN, LEN // 2, 2))(jax.random.split(seeds[9], ROWS)).reshape((ROWS, SEQS)).astype(jnp.int32)
    out_weight = heavy_noise(seeds[10], (INNER, D), INNER ** -0.5, 0.375, ((0, 128),), (0, 1, 128, 5.5))
    residual_last = bell_draw(seeds[11], (ROWS, SEQS, D), 1.0, 6.0)
    final_gain = jnp.clip(1.0 + 0.1 * jax.random.normal(seeds[12], (D,), jnp.float32), 0.5, 1.5)
    vocab_weight = bell_draw(seeds[13], (VOCAB, D), (D // 9) ** -0.5, 0.25, ((0, 128),))
    return dict(conv_input=conv_input, gate_projected=gate_projected, step_raw=step_raw, step_bias=step_bias, decay_log=decay_log, head_direct_gain=head_direct_gain, conv_weight=conv_weight, convolution_bias=convolution_bias, norm_weight=norm_weight, lengths=lengths, out_weight=out_weight, residual_last=residual_last, final_gain=final_gain, vocab_weight=vocab_weight)


TINY_FLOOR = 1e-05

def segment_of(places, lengths):
    bounds = jnp.cumsum(lengths).astype(jnp.int32)[:-1]
    return lax.optimization_barrier(jnp.sum((places[:, None] >= bounds[None, :]).astype(jnp.int32), axis=1)).astype(jnp.int32)

def convolve(padded, padded_seg, conv_weight, convolution_bias, count):
    target = padded_seg[KERNEL - 1:]
    total = jnp.zeros((count, padded.shape[1]), jnp.float32) + convolution_bias
    for kernel_tap in range(KERNEL):
        same_seg = (padded_seg[kernel_tap:kernel_tap + count] == target).astype(jnp.float32)
        total = total + conv_weight[kernel_tap] * padded[kernel_tap:kernel_tap + count].astype(jnp.float32) * same_seg[:, None]
    return jax.nn.silu(total)

def block_parts(feature_matrix, state_inputs, input_map, state_map, output_map, step_size, decays, segment, before):
    length = feature_matrix.shape[0]
    per_group = HEADS // GROUPS
    cum_decay = jnp.cumsum(decays, axis=0)
    places = jnp.arange(length)
    allowed = (places[:, None] >= places[None, :]) & (segment[:, None] == segment[None, :])
    spread = cum_decay.T[:, :, None] - cum_decay.T[:, None, :]
    weights = jnp.exp(jnp.where(allowed[None], spread, -jnp.inf)) * step_size.T[:, None, :]
    scores = jnp.einsum('tgn,sgn->gts', output_map.astype(jnp.float32), input_map.astype(jnp.float32))
    mixing = (weights.reshape(GROUPS, per_group, length, length) * scores[:, None]).astype(jnp.bfloat16)
    grouped = feature_matrix.reshape(length, GROUPS, per_group, CHANNEL_WIDTH)
    y_intra = jnp.einsum('gjts,sgjp->tgjp', mixing.astype(jnp.float32), grouped.astype(jnp.float32)).reshape(length, HEADS, CHANNEL_WIDTH)
    tail_seg = (segment == segment[length - 1]).astype(jnp.float32)
    tail_weight = jnp.exp(cum_decay[length - 1][None, :] - cum_decay) * step_size * tail_seg[:, None]
    scaled = state_inputs * tail_weight[:, :, None]
    state = jnp.einsum('sgjp,sgn->gjpn', scaled.reshape(length, GROUPS, per_group, CHANNEL_WIDTH), state_map, precision=lax.Precision.HIGHEST).reshape(HEADS, CHANNEL_WIDTH, STATE)
    within_tile = (segment == before).astype(jnp.float32)
    lead = jnp.exp(cum_decay) * within_tile[:, None]
    carry = jnp.exp(cum_decay[length - 1]) * within_tile[length - 1]
    return (y_intra, lead, state, carry)

def block_output(y_intra, lead, entering, output_map, feature_matrix, head_direct_gain):
    length = feature_matrix.shape[0]
    per_group = HEADS // GROUPS
    inter = jnp.einsum('tgn,gjpn->tgjp', output_map.astype(jnp.float32), entering.reshape(GROUPS, per_group, CHANNEL_WIDTH, STATE), precision=lax.Precision.HIGHEST).reshape(length, HEADS, CHANNEL_WIDTH)
    return y_intra + lead[:, :, None] * inter + head_direct_gain[None, :, None] * feature_matrix.astype(jnp.float32)

def gate_norm(values, gate, norm_weight):
    length = values.shape[0]
    flat = values.reshape(length, -1) * jax.nn.silu(gate.astype(jnp.float32))
    grouped = flat.reshape(length, GROUPS, -1)
    scale = lax.rsqrt(lax.optimization_barrier(jnp.mean(grouped * grouped, axis=-1, keepdims=True)) + TINY_FLOOR)
    return ((grouped * scale).reshape(length, -1) * norm_weight).astype(jnp.bfloat16)

def state_at(state_inputs, state_map, step_size, decays, segment, before, within, entering):
    length = state_inputs.shape[0]
    per_group = HEADS // GROUPS
    cum_decay = jnp.cumsum(decays, axis=0)
    places = jnp.arange(length)
    allowed = (segment == segment[within]) & (places <= within)
    tail_weight = jnp.exp(jnp.where(allowed[:, None], cum_decay[within][None, :] - cum_decay, -jnp.inf)) * step_size
    scaled = state_inputs * tail_weight[:, :, None]
    state = jnp.einsum('sgjp,sgn->gjpn', scaled.reshape(length, GROUPS, per_group, CHANNEL_WIDTH), state_map, precision=lax.Precision.HIGHEST).reshape(HEADS, CHANNEL_WIDTH, STATE)
    lead = jnp.exp(cum_decay[within]) * (segment[within] == before).astype(jnp.float32)
    return lead[:, None, None] * entering + state

def reference(conv_input, gate_projected, step_raw, step_bias, decay_log, head_direct_gain, conv_weight, convolution_bias, norm_weight, lengths, out_weight, residual_last, final_gain, vocab_weight):
    total_len = conv_input.shape[1]
    inner = HEADS * CHANNEL_WIDTH
    count = total_len // BLOCK
    split_at = inner + GROUPS * STATE

    def one_row(items):
        conv_row, gate_row, raw_row, length_row = items
        places = jnp.arange(total_len, dtype=jnp.int32)
        segment = segment_of(places, length_row)
        padded = jnp.concatenate([jnp.zeros((KERNEL - 1, conv_row.shape[1]), jnp.bfloat16), conv_row], axis=0)
        padded_seg = jnp.concatenate([jnp.full((KERNEL - 1,), -1, jnp.int32), segment], axis=0)
        mixed_full = convolve(padded, padded_seg, conv_weight, convolution_bias, total_len)
        mixed = mixed_full.astype(jnp.bfloat16)
        feature_matrix = mixed[:, :inner].reshape(total_len, HEADS, CHANNEL_WIDTH)
        input_map = mixed[:, inner:split_at].reshape(total_len, GROUPS, STATE)
        output_map = mixed[:, split_at:].reshape(total_len, GROUPS, STATE)
        state_inputs = mixed_full[:, :inner].reshape(total_len, HEADS, CHANNEL_WIDTH)
        state_map = mixed_full[:, inner:split_at].reshape(total_len, GROUPS, STATE)
        step_size = jax.nn.softplus(raw_row + step_bias)
        decays = -jnp.exp(decay_log) * step_size
        befores = segment_of(jnp.arange(count, dtype=jnp.int32) * BLOCK - 1, length_row)
        blocks = (feature_matrix.reshape(count, BLOCK, HEADS, CHANNEL_WIDTH), state_inputs.reshape(count, BLOCK, HEADS, CHANNEL_WIDTH), input_map.reshape(count, BLOCK, GROUPS, STATE), state_map.reshape(count, BLOCK, GROUPS, STATE), output_map.reshape(count, BLOCK, GROUPS, STATE), step_size.reshape(count, BLOCK, HEADS), decays.reshape(count, BLOCK, HEADS), segment.reshape(count, BLOCK), befores, gate_row.reshape(count, BLOCK, inner))

        def advance(entering, block):
            block_inputs, block_state_inputs, block_in_map, block_state_map, block_out_map, block_step, block_decay, block_seg, before, block_gate = block
            y_intra, lead, state, carry = block_parts(block_inputs, block_state_inputs, block_in_map, block_state_map, block_out_map, block_step, block_decay, block_seg, before)
            values = block_output(y_intra, lead, entering, block_out_map, block_inputs, head_direct_gain)
            gated = gate_norm(values, block_gate, norm_weight)
            return (carry[:, None, None] * entering + state, (gated, entering))
        _, (gated, entering) = lax.scan(advance, jnp.zeros((HEADS, CHANNEL_WIDTH, STATE), jnp.float32), blocks)
        gated = gated.reshape(total_len, inner)
        ends = jnp.cumsum(length_row).astype(jnp.int32) - 1
        finals = []
        lasts = []
        for request in range(SEQS):
            spot = ends[request]
            index = spot // BLOCK
            start = (index * BLOCK).astype(jnp.int32)
            within = spot - start
            finals.append(state_at(lax.dynamic_slice_in_dim(state_inputs, start, BLOCK, 0), lax.dynamic_slice_in_dim(state_map, start, BLOCK, 0), lax.dynamic_slice_in_dim(step_size, start, BLOCK, 0), lax.dynamic_slice_in_dim(decays, start, BLOCK, 0), lax.dynamic_slice_in_dim(segment, start, BLOCK, 0), befores[index], within, entering[index]))
            lasts.append(gated[spot])
        return (gated, jnp.stack(finals), jnp.stack(lasts))
    y_gated, final_states, last_rows = lax.map(one_row, (conv_input, gate_projected, step_raw, lengths))
    flat_rows = last_rows.reshape(-1, inner)
    hidden = residual_last.reshape(-1, D).astype(jnp.float32) + jnp.dot(flat_rows, out_weight, preferred_element_type=jnp.float32)
    last_hidden = hidden.astype(jnp.bfloat16).reshape(residual_last.shape)
    scale = lax.rsqrt(lax.optimization_barrier(jnp.mean(hidden * hidden, axis=-1, keepdims=True)) + TINY_FLOOR)
    normed = (hidden * scale * final_gain).astype(jnp.bfloat16)
    pieces = vocab_weight.reshape(16, -1, D)

    def top_of(piece):
        logits = lax.dot_general(normed, piece, (((1,), (1,)), ((), ())), preferred_element_type=jnp.float32)
        return lax.optimization_barrier(jnp.max(logits, axis=1))
    tops = lax.map(top_of, pieces)
    max_logit = lax.optimization_barrier(jnp.max(tops, axis=0)).reshape(lengths.shape)
    return (y_gated, final_states, last_hidden, max_logit)
```

```python
import functools

import jax
import jax.numpy as jnp
from jax import lax
from jax.experimental import pallas as pl
from jax.experimental.pallas import tpu as pltpu
from jax.sharding import PartitionSpec as P

D = 4096
HEADS = 64
CHANNEL_WIDTH = 64
GROUPS = 4
STATE = 128
KERNEL = 4
BLOCK = 256
SEQS = 4
PER_GROUP = HEADS // GROUPS
GW = PER_GROUP * CHANNEL_WIDTH
TINY_FLOOR = 1e-05
LOG2E = 1.4426950408889634
MESH = pl.DeviceIdType.MESH
F32 = jnp.float32
BF16 = jnp.bfloat16
VMEM_LIMIT = 60 * 1024 * 1024


def dot(a, b):
    return lax.dot_general(a, b, (((1,), (0,)), ((), ())), preferred_element_type=F32)


def dot_nt(a, b):
    return lax.dot_general(a, b, (((1,), (1,)), ((), ())), preferred_element_type=F32)


def split2(x):
    hi = x.astype(BF16)
    return hi, (x - hi.astype(F32)).astype(BF16)


def split3(x):
    hi = x.astype(BF16)
    rest = x - hi.astype(F32)
    mid = rest.astype(BF16)
    return hi, mid, (rest - mid.astype(F32)).astype(BF16)


def seg_of(place, b1, b2, b3):
    one = lambda b: (place >= b).astype(jnp.int32)
    return one(b1) + one(b2) + one(b3)


def spread_matrix():
    lane = lax.broadcasted_iota(jnp.int32, (128, GW), 0)
    col = lax.broadcasted_iota(jnp.int32, (128, GW), 1)
    hit = (lane < 48) & (lane % PER_GROUP == col // CHANNEL_WIDTH)
    return jnp.where(hit, 1.0, 0.0).astype(BF16)


def spread(v, spread_ref):
    hi, mid, lo = split3(v)
    lane = lax.broadcasted_iota(jnp.int32, v.shape, 1)
    parts = jnp.where(
        lane < 16, hi.astype(F32), jnp.where(lane < 32, mid.astype(F32), lo.astype(F32))
    ).astype(BF16)
    return dot(parts, spread_ref[...])


def silu(x):
    return x * jax.nn.sigmoid(x)


def local_kernel(
    meta,
    x_ref,
    b_ref,
    c_ref,
    xh_ref,
    bh_ref,
    ch_ref,
    wx_ref,
    wb_ref,
    wc_ref,
    vx_ref,
    vb_ref,
    vc_ref,
    dt_ref,
    dtt_ref,
    a_ref,
    at_ref,
    dx_ref,
    y_ref,
    st_ref,
    pt_ref,
    aux_ref,
    co_ref,
    ld_ref,
    xext,
    xf,
    s0,
    c0,
    cumr,
    sp,
):
    g = pl.program_id(0)
    j = pl.program_id(1)
    first = meta[0]
    b1, b2, b3 = meta[1], meta[2], meta[3]
    start = first + j * BLOCK

    @pl.when((g == 0) & (j == 0))
    def _():
        sp[...] = spread_matrix()

    @pl.when(j == 0)
    def _():
        xext[0:8, 0:GW] = xh_ref[...].astype(F32)
        xext[0:8, GW : GW + 128] = bh_ref[...].astype(F32)
        xext[0:8, GW + 128 : GW + 256] = ch_ref[...].astype(F32)
        pt_ref[...] = jnp.zeros_like(pt_ref)
        aux_ref[...] = jnp.zeros_like(aux_ref)

    @pl.when(j == 1)
    def _():
        xext[0:8, :] = xext[BLOCK : BLOCK + 8, :]

    xext[8 : BLOCK + 8, 0:GW] = x_ref[...].astype(F32)
    xext[8 : BLOCK + 8, GW : GW + 128] = b_ref[...].astype(F32)
    xext[8 : BLOCK + 8, GW + 128 : GW + 256] = c_ref[...].astype(F32)

    row = lax.broadcasted_iota(jnp.int32, (BLOCK, 128), 0) + start
    seg = seg_of(row, b1, b2, b3)
    same = [(seg_of(row - k, b1, b2, b3) == seg).astype(F32) for k in (3, 2, 1)]
    for c in range(10):
        cols = slice(c * 128, c * 128 + 128)
        w_ref, v_ref, lo = (
            (wx_ref, vx_ref, c * 128) if c < 8 else ((wb_ref, vb_ref, 0) if c == 8 else (wc_ref, vc_ref, 0))
        )
        part = slice(lo, lo + 128)
        total = jnp.broadcast_to(v_ref[0:1, part], (BLOCK, 128))
        for k in range(3):
            total = total + w_ref[k : k + 1, part] * xext[5 + k : 5 + k + BLOCK, cols] * same[k]
        total = total + w_ref[3:4, part] * xext[8 : 8 + BLOCK, cols]
        xf[:, cols] = silu(total)

    bf = xf[:, GW : GW + 128]
    cb = xf[:, GW + 128 : GW + 256].astype(BF16)
    co_ref[...] = cb

    i0 = lax.broadcasted_iota(jnp.int32, (BLOCK, BLOCK), 0)
    i1 = lax.broadcasted_iota(jnp.int32, (BLOCK, BLOCK), 1)
    tri = jnp.where(i0 >= i1, 1.0, 0.0).astype(BF16)
    triu = jnp.where(i0 <= i1, 1.0, 0.0).astype(BF16)
    dt = dt_ref[0, 0]
    dh, dm, dl = split3(dt * a_ref[0])
    cum = (dot(tri, dl) + dot(tri, dm)) + dot(tri, dh)
    logdt = jnp.log(dt) * LOG2E
    dtt = dtt_ref[0, 0]
    th, tm, tl = split3(dtt * at_ref[0])
    cumt = (dot(tl, triu) + dot(tm, triu)) + dot(th, triu)
    rt = jnp.log(dtt) * LOG2E - cumt
    cumr[...] = cum
    last = cum[BLOCK - 1 : BLOCK, :]

    seg_before_span = seg_of(first - 1, b1, b2, b3)
    seg_before = seg_of(start - 1, b1, b2, b3)
    seg_end = seg_of(start + BLOCK - 1, b1, b2, b3)

    @pl.when(j == 0)
    def _():
        c0[...] = jnp.zeros_like(c0)

    prior = c0[0:1, :]
    ld_ref[0, 0] = jnp.where(seg == seg_before_span, jnp.exp2(cum + prior), 0.0)

    bh, bl = split2(bf)
    sc = dot_nt(cb, bh)
    t_seg = seg_of(i0 + start, b1, b2, b3)
    s_seg = seg_of(i1 + start, b1, b2, b3)
    sc = jnp.where((i0 >= i1) & (t_seg == s_seg), sc, 0.0)

    @pl.when(j == 0)
    def _():
        y_ref[...] = jnp.zeros_like(y_ref)

    @pl.when(j == 1)
    def _():
        lead = jnp.where(seg == seg_before, jnp.exp2(cum), 0.0)
        sh, sl = split2(s0[...])
        y_ref[...] = spread(lead, sp) * (dot(cb, sh) + dot(cb, sl))

    lane = lax.broadcasted_iota(jnp.int32, (BLOCK, 128), 1)
    half = BLOCK // 2
    sc_t = sc[:half, :half]
    sc_l = sc[half:, :half]
    sc_r = sc[half:, half:]
    for pair in range(PER_GROUP // 2):
        cols = slice(pair * 128, pair * 128 + 128)
        xb = xf[:, cols].astype(BF16)
        res = []
        for h in (2 * pair, 2 * pair + 1):
            col = cum[:, h : h + 1]
            r = rt[h : h + 1, :]
            top = jnp.exp2(jnp.minimum(col[:half] + r[:, :half], 100.0)) * sc_t
            left = jnp.exp2(col[half:] + r[:, :half]) * sc_l
            right = jnp.exp2(jnp.minimum(col[half:] + r[:, half:], 100.0)) * sc_r
            bottom = jnp.concatenate([left.astype(BF16), right.astype(BF16)], axis=1)
            res.append(
                jnp.concatenate([dot(top.astype(BF16), xb[:half]), dot(bottom, xb)], axis=0)
            )
        intra = jnp.where(lane < CHANNEL_WIDTH, res[0], res[1])
        y_ref[:, cols] = y_ref[:, cols] + (intra + dx_ref[0:1, cols] * xb.astype(F32))

    bht, blt = split2(bf.T)

    def state_of(weights):
        xs = xf[:, 0:GW] * spread(weights, sp)
        xs_h, xs_l = split2(xs)
        return dot(bht, xs_h) + (dot(blt, xs_h) + dot(bht, xs_l))

    def at_end(seg_e):
        return jnp.where(seg == seg_e, jnp.exp2(last - cum + logdt), 0.0)

    own = state_of(at_end(seg_end))

    for r in range(SEQS - 1):
        end = meta[1 + r] - 1
        local = end - start
        owned = (local >= 0) & (local < BLOCK)

        @pl.when(owned)
        def _():
            ce = cumr[pl.ds(jnp.clip(local, 0, BLOCK - 1), 1), :]
            inside = (row <= end) & (seg == r)
            w = jnp.exp2(jnp.where(inside, ce - cum + logdt, -1e30))
            reach = jnp.where(seg_before == r, jnp.exp2(ce), 0.0)
            tail = state_of(w)
            keep = jnp.where(j == 1, 1.0, 0.0)
            reach8 = spread(jnp.broadcast_to(reach * keep, (8, 128)), sp)
            tail = tail + jnp.where(j == 1, reach8[0:1] * s0[...], 0.0)
            pt_ref[r] = tail.astype(BF16)
            full = jnp.where(seg_before_span == r, jnp.exp2(ce + prior), 0.0)
            aux_ref[1 + r : 2 + r, :] = spread(jnp.broadcast_to(full, (8, 128)), sp)[0:1]

    @pl.when(j == 0)
    def _():
        s0[...] = own
        c0[...] = jnp.broadcast_to(last, c0.shape)

    @pl.when(j == 1)
    def _():
        carry = jnp.where(seg_end == seg_before, jnp.exp2(last), 0.0)
        whole = jnp.where(seg_end == seg_before_span, jnp.exp2(last + prior), 0.0)
        carry8 = spread(jnp.broadcast_to(carry, (8, 128)), sp)
        whole8 = spread(jnp.broadcast_to(whole, (8, 128)), sp)
        st_ref[...] = (carry8[0:1] * s0[...] + own).astype(BF16)
        aux_ref[0:1, :] = whole8[0:1]


def local_pass(meta, conv, halo, conv_weight, conv_bias, dt, dtt, a, at, dx):
    length = conv.shape[0]
    blocks = length // BLOCK
    maps = D // 128
    grid = (GROUPS, blocks)
    xs = lambda rows: [
        pl.BlockSpec((rows, GW), lambda g, j: (0, g)),
        pl.BlockSpec((rows, 128), lambda g, j: (0, maps + g)),
        pl.BlockSpec((rows, 128), lambda g, j: (0, maps + GROUPS + g)),
    ]
    in_specs = (
        [
            pl.BlockSpec(memory_space=pltpu.SMEM),
            pl.BlockSpec((BLOCK, GW), lambda g, j: (j, g)),
            pl.BlockSpec((BLOCK, 128), lambda g, j: (j, maps + g)),
            pl.BlockSpec((BLOCK, 128), lambda g, j: (j, maps + GROUPS + g)),
        ]
        + xs(8)
        + xs(KERNEL)
        + xs(1)
        + [
            pl.BlockSpec((1, 1, BLOCK, 128), lambda g, j: (g, j, 0, 0)),
            pl.BlockSpec((1, 1, PER_GROUP, BLOCK), lambda g, j: (g, j, 0, 0)),
            pl.BlockSpec((1, 1, 128), lambda g, j: (g, 0, 0)),
            pl.BlockSpec((1, PER_GROUP, 1), lambda g, j: (g, 0, 0)),
            pl.BlockSpec((1, GW), lambda g, j: (0, g)),
        ]
    )
    out_specs = [
        pl.BlockSpec((BLOCK, GW), lambda g, j: (j, g)),
        pl.BlockSpec((STATE, GW), lambda g, j: (0, g)),
        pl.BlockSpec((SEQS - 1, STATE, GW), lambda g, j: (0, 0, g)),
        pl.BlockSpec((8, GW), lambda g, j: (0, g)),
        pl.BlockSpec((BLOCK, 128), lambda g, j: (j, g)),
        pl.BlockSpec((1, 1, BLOCK, 128), lambda g, j: (g, j, 0, 0)),
    ]
    out_shape = [
        jax.ShapeDtypeStruct((length, D), F32),
        jax.ShapeDtypeStruct((STATE, D), BF16),
        jax.ShapeDtypeStruct((SEQS - 1, STATE, D), BF16),
        jax.ShapeDtypeStruct((8, D), F32),
        jax.ShapeDtypeStruct((length, GROUPS * STATE), BF16),
        jax.ShapeDtypeStruct((GROUPS, blocks, BLOCK, 128), F32),
    ]
    return pl.pallas_call(
        local_kernel,
        grid=grid,
        in_specs=in_specs,
        out_specs=out_specs,
        out_shape=out_shape,
        scratch_shapes=[
            pltpu.VMEM((BLOCK + 8, GW + 256), F32),
            pltpu.VMEM((BLOCK, GW + 256), F32),
            pltpu.VMEM((STATE, GW), F32),
            pltpu.VMEM((8, 128), F32),
            pltpu.VMEM((BLOCK, 128), F32),
            pltpu.VMEM((128, GW), BF16),
        ],
        compiler_params=pltpu.CompilerParams(
            vmem_limit_bytes=VMEM_LIMIT, dimension_semantics=("arbitrary", "arbitrary")
        ),
        name="local_pass",
    )(
        meta, conv, conv, conv, halo, halo, halo, conv_weight, conv_weight, conv_weight,
        conv_bias, conv_bias, conv_bias, dt, dtt, a, at, dx,
    )


def exchange_kernel(
    n,
    st_ref,
    aux_ref,
    ent_ref,
    fin_ref,
    rs,
    ra,
    eb,
    send1,
    recv1,
    send2,
    recv2,
    send3,
    recv3,
):
    me = lax.axis_index("seq")
    width = D // n
    barrier = pltpu.get_barrier_semaphore()

    def peer(i):
        return lax.rem(me + i, n)

    def cols(p):
        return pl.ds(pl.multiple_of(p * width, width), width)

    def greet(i, _):
        pl.semaphore_signal(barrier, inc=1, device_id={"seq": peer(i)}, device_id_type=MESH)
        return 0

    lax.fori_loop(1, n, greet, 0)
    pl.semaphore_wait(barrier, n - 1)

    def out(p, slot):
        return (
            pltpu.make_async_remote_copy(
                src_ref=st_ref.at[:, cols(p)],
                dst_ref=rs.at[slot],
                send_sem=send1.at[p],
                recv_sem=recv1.at[slot],
                device_id={"seq": p},
                device_id_type=MESH,
            ),
            pltpu.make_async_remote_copy(
                src_ref=aux_ref.at[:, cols(p)],
                dst_ref=ra.at[slot],
                send_sem=send2.at[p],
                recv_sem=recv2.at[slot],
                device_id={"seq": p},
                device_id_type=MESH,
            ),
        )

    def back(p, slot):
        return pltpu.make_async_remote_copy(
            src_ref=eb.at[p],
            dst_ref=ent_ref.at[:, cols(slot)],
            send_sem=send3.at[p],
            recv_sem=recv3.at[slot],
            device_id={"seq": p},
            device_id_type=MESH,
        )

    def begin(i, _):
        for copy in out(peer(i), me):
            copy.start()
        return 0

    lax.fori_loop(1, n, begin, 0)
    rs[me] = st_ref[:, cols(me)]
    ra[me] = aux_ref[:, cols(me)]

    def arrive(i, _):
        for copy in out(peer(i), peer(i)):
            copy.wait_recv()
        return 0

    lax.fori_loop(1, n, arrive, 0)

    fin_ref[...] = jnp.zeros_like(fin_ref)

    def scan(d, _):
        now = fin_ref[SEQS - 1]
        eb[d] = now.astype(BF16)
        for r in range(SEQS - 1):
            fin_ref[r] = fin_ref[r] + ra[d, 1 + r : 2 + r, :] * now
        fin_ref[SEQS - 1] = ra[d, 0:1, :] * now + rs[d].astype(F32)
        return 0

    lax.fori_loop(0, n, scan, 0)

    def reply(i, _):
        back(peer(i), me).start()
        return 0

    lax.fori_loop(1, n, reply, 0)
    ent_ref[:, cols(me)] = eb[me]

    def done(i, _):
        back(peer(i), peer(i)).wait_recv()
        return 0

    lax.fori_loop(1, n, done, 0)

    def drain(i, _):
        for copy in out(peer(i), me):
            copy.wait_send()
        back(peer(i), me).wait_send()
        return 0

    lax.fori_loop(1, n, drain, 0)


def exchange(states, aux, n):
    width = D // n
    vmem = pl.BlockSpec(memory_space=pltpu.VMEM)
    return pl.pallas_call(
        functools.partial(exchange_kernel, n),
        in_specs=[vmem, vmem],
        out_specs=[vmem, vmem],
        out_shape=[
            jax.ShapeDtypeStruct((STATE, D), BF16),
            jax.ShapeDtypeStruct((SEQS, STATE, width), F32),
        ],
        scratch_shapes=[
            pltpu.VMEM((n, STATE, width), BF16),
            pltpu.VMEM((n, 8, width), F32),
            pltpu.VMEM((n, STATE, width), BF16),
        ]
        + [pltpu.SemaphoreType.DMA((n,)) for _ in range(6)],
        compiler_params=pltpu.CompilerParams(
            collective_id=0, has_side_effects=True, vmem_limit_bytes=VMEM_LIMIT
        ),
        name="exchange",
    )(states, aux)


def finish_kernel(y_ref, c_ref, e_ref, ld_ref, gate_ref, nw_ref, out_ref, sp):
    @pl.when((pl.program_id(0) == 0) & (pl.program_id(1) == 0))
    def _():
        sp[...] = spread_matrix()

    v = y_ref[...] + spread(ld_ref[0, 0], sp) * dot(c_ref[...], e_ref[...])
    v = v * silu(gate_ref[...].astype(F32))
    scale = lax.rsqrt(jnp.mean(v * v, axis=1, keepdims=True) + TINY_FLOOR)
    out_ref[...] = (v * scale * nw_ref[...]).astype(BF16)


def finish(y, c, entering, lead, gate, norm_weight):
    length = y.shape[0]
    block = lambda width: pl.BlockSpec((BLOCK, width), lambda g, j: (j, g))
    return pl.pallas_call(
        finish_kernel,
        grid=(GROUPS, length // BLOCK),
        in_specs=[
            block(GW),
            block(STATE),
            pl.BlockSpec((STATE, GW), lambda g, j: (0, g)),
            pl.BlockSpec((1, 1, BLOCK, 128), lambda g, j: (g, j, 0, 0)),
            block(GW),
            pl.BlockSpec((1, GW), lambda g, j: (0, g)),
        ],
        out_specs=block(GW),
        out_shape=jax.ShapeDtypeStruct((length, D), BF16),
        scratch_shapes=[pltpu.VMEM((128, GW), BF16)],
        compiler_params=pltpu.CompilerParams(
            vmem_limit_bytes=VMEM_LIMIT, dimension_semantics=("arbitrary", "arbitrary")
        ),
        name="finish",
    )(y, c, entering, lead, gate, norm_weight)


def body(
    conv_input,
    gate_projected,
    step_raw,
    step_bias,
    decay_log,
    head_direct_gain,
    conv_weight,
    convolution_bias,
    norm_weight,
    lengths,
    out_weight,
    residual_last,
    final_gain,
    vocab_weight,
):
    local_len = conv_input.shape[1]
    inner = HEADS * CHANNEL_WIDTH
    count = local_len // BLOCK
    seq_count = lax.axis_size("seq")
    seq_place = lax.axis_index("seq")
    req_place = lax.axis_index("req")
    first = seq_place * local_len
    conv = conv_input[0]
    route = [(i, i + 1) for i in range(seq_count - 1)]
    halo = lax.ppermute(conv[local_len - 8 :], "seq", route)
    bounds = jnp.cumsum(lengths[0]).astype(jnp.int32)
    meta = jnp.concatenate([first.astype(jnp.int32)[None], bounds])

    step = jax.nn.softplus(step_raw[0] + step_bias)
    step = step.reshape(count, BLOCK, GROUPS, PER_GROUP)
    dt = jnp.tile(step.transpose(2, 0, 1, 3), (1, 1, 1, 128 // PER_GROUP))
    dtt = step.transpose(2, 0, 3, 1)
    rate = (-jnp.exp(decay_log) * LOG2E).reshape(GROUPS, PER_GROUP)
    a = jnp.tile(rate, (1, 128 // PER_GROUP))[:, None, :]
    at = rate[:, :, None]
    dx = jnp.repeat(head_direct_gain, CHANNEL_WIDTH)[None]

    y, states, tails, aux, c, lead = local_pass(
        meta, conv, halo, conv_weight, convolution_bias[None], dt, dtt, a, at, dx
    )
    tail_share = lax.psum_scatter(tails, "seq", scatter_dimension=2, tiled=True)
    entering, reached = exchange(states, aux, seq_count)
    gated = finish(y, c, entering, lead, gate_projected[0], norm_weight[None])

    final = jnp.concatenate(
        [reached[: SEQS - 1] + tail_share.astype(F32), reached[SEQS - 1 :]], axis=0
    )
    final_states = final.reshape(SEQS, STATE, HEADS // seq_count, CHANNEL_WIDTH)
    final_states = final_states.transpose(0, 2, 3, 1)[None]

    lasts = []
    for request in range(SEQS):
        local_end = bounds[request] - 1 - first
        owned = (local_end >= 0) & (local_end < local_len)
        spot = jnp.clip(local_end, 0, local_len - 1)
        lasts.append(jnp.where(owned, gated[spot].astype(jnp.float32), 0.0))
    last_local = jnp.stack(lasts)
    rows_total = residual_last.shape[0]
    group_rows = lax.psum(last_local.astype(jnp.bfloat16), "seq")[None]
    all_rows = lax.all_gather(group_rows, "req", axis=0, tiled=True)
    share = out_weight.shape[0]
    flat_place = req_place * seq_count + seq_place
    columns = lax.dynamic_slice_in_dim(all_rows.reshape(-1, inner), flat_place * share, share, 1)
    partial_value = jnp.dot(columns, out_weight, preferred_element_type=jnp.float32)
    summed = lax.psum(partial_value, ("req", "seq"))
    hidden = residual_last.reshape(-1, D).astype(jnp.float32) + summed
    last_hidden = hidden.astype(jnp.bfloat16).reshape(rows_total, SEQS, D)
    own_hidden = lax.dynamic_slice_in_dim(last_hidden, req_place, 1, 0)
    scale = lax.rsqrt(jnp.mean(hidden * hidden, axis=-1, keepdims=True) + TINY_FLOOR)
    normed = (hidden * scale * final_gain).astype(jnp.bfloat16)
    logits = lax.dot_general(
        normed, vocab_weight, (((1,), (1,)), ((), ())), preferred_element_type=jnp.float32
    )
    local_top = jnp.max(logits, axis=1)
    top_all = lax.pmax(local_top, ("req", "seq"))
    max_logit = lax.dynamic_slice_in_dim(top_all.reshape(rows_total, SEQS), req_place, 1, 0)
    return (gated[None], final_states, own_hidden, max_logit)


def solution(mesh):
    return jax.shard_map(
        body,
        mesh=mesh,
        in_specs=(
            P("req", "seq", None),
            P("req", "seq", None),
            P("req", "seq", None),
            P(),
            P(),
            P(),
            P(),
            P(),
            P(),
            P("req", None),
            P(("req", "seq"), None),
            P(),
            P(),
            P(("req", "seq"), None),
        ),
        out_specs=(
            P("req", "seq", None),
            P("req", None, "seq", None, None),
            P("req", None, None),
            P("req", None),
        ),
        check_vma=False,
    )
```

```python
import functools

import jax
import jax.numpy as jnp
from jax import lax
from jax.experimental import pallas as pl
from jax.experimental.pallas import tpu as pltpu
from jax.sharding import PartitionSpec as P

D = 4096
HEADS = 64
CHANNEL_WIDTH = 64
GROUPS = 4
STATE = 128
KERNEL = 4
BLOCK = 256
SEQS = 4
PER_GROUP = HEADS // GROUPS
GW = PER_GROUP * CHANNEL_WIDTH
TINY_FLOOR = 1e-05
LOG2E = 1.4426950408889634
MESH = pl.DeviceIdType.MESH
F32 = jnp.float32
BF16 = jnp.bfloat16
VMEM_LIMIT = 60 * 1024 * 1024


def dot(a, b):
    return lax.dot_general(a, b, (((1,), (0,)), ((), ())), preferred_element_type=F32)


def dot_nt(a, b):
    return lax.dot_general(a, b, (((1,), (1,)), ((), ())), preferred_element_type=F32)


def split2(x):
    hi = x.astype(BF16)
    return hi, (x - hi.astype(F32)).astype(BF16)


def split3(x):
    hi = x.astype(BF16)
    rest = x - hi.astype(F32)
    mid = rest.astype(BF16)
    return hi, mid, (rest - mid.astype(F32)).astype(BF16)


def seg_of(place, b1, b2, b3):
    one = lambda b: (place >= b).astype(jnp.int32)
    return one(b1) + one(b2) + one(b3)


def spread_matrix():
    lane = lax.broadcasted_iota(jnp.int32, (128, GW), 0)
    col = lax.broadcasted_iota(jnp.int32, (128, GW), 1)
    hit = (lane < 48) & (lane % PER_GROUP == col // CHANNEL_WIDTH)
    return jnp.where(hit, 1.0, 0.0).astype(BF16)


def spread(v, spread_ref):
    hi, mid, lo = split3(v)
    lane = lax.broadcasted_iota(jnp.int32, v.shape, 1)
    parts = jnp.where(
        lane < 16, hi.astype(F32), jnp.where(lane < 32, mid.astype(F32), lo.astype(F32))
    ).astype(BF16)
    return dot(parts, spread_ref[...])


def silu(x):
    return x * jax.nn.sigmoid(x)


def local_kernel(
    meta,
    x_ref,
    b_ref,
    c_ref,
    xh_ref,
    bh_ref,
    ch_ref,
    wx_ref,
    wb_ref,
    wc_ref,
    vx_ref,
    vb_ref,
    vc_ref,
    dt_ref,
    dtt_ref,
    a_ref,
    at_ref,
    dx_ref,
    y_ref,
    st_ref,
    pt_ref,
    aux_ref,
    co_ref,
    ld_ref,
    xext,
    xf,
    s0,
    c0,
    cumr,
    sp,
):
    g = pl.program_id(0)
    j = pl.program_id(1)
    first = meta[0]
    b1, b2, b3 = meta[1], meta[2], meta[3]
    start = first + j * BLOCK

    @pl.when((g == 0) & (j == 0))
    def _():
        sp[...] = spread_matrix()

    @pl.when(j == 0)
    def _():
        xext[0:8, 0:GW] = xh_ref[...].astype(F32)
        xext[0:8, GW : GW + 128] = bh_ref[...].astype(F32)
        xext[0:8, GW + 128 : GW + 256] = ch_ref[...].astype(F32)
        pt_ref[...] = jnp.zeros_like(pt_ref)
        aux_ref[...] = jnp.zeros_like(aux_ref)

    @pl.when(j == 1)
    def _():
        xext[0:8, :] = xext[BLOCK : BLOCK + 8, :]

    xext[8 : BLOCK + 8, 0:GW] = x_ref[...].astype(F32)
    xext[8 : BLOCK + 8, GW : GW + 128] = b_ref[...].astype(F32)
    xext[8 : BLOCK + 8, GW + 128 : GW + 256] = c_ref[...].astype(F32)

    row = lax.broadcasted_iota(jnp.int32, (BLOCK, 128), 0) + start
    seg = seg_of(row, b1, b2, b3)
    same = [(seg_of(row - k, b1, b2, b3) == seg).astype(F32) for k in (3, 2, 1)]
    for c in range(10):
        cols = slice(c * 128, c * 128 + 128)
        w_ref, v_ref, lo = (
            (wx_ref, vx_ref, c * 128) if c < 8 else ((wb_ref, vb_ref, 0) if c == 8 else (wc_ref, vc_ref, 0))
        )
        part = slice(lo, lo + 128)
        total = jnp.broadcast_to(v_ref[0:1, part], (BLOCK, 128))
        for k in range(3):
            total = total + w_ref[k : k + 1, part] * xext[5 + k : 5 + k + BLOCK, cols] * same[k]
        total = total + w_ref[3:4, part] * xext[8 : 8 + BLOCK, cols]
        xf[:, cols] = silu(total)

    bf = xf[:, GW : GW + 128]
    cb = xf[:, GW + 128 : GW + 256].astype(BF16)
    co_ref[...] = cb

    i0 = lax.broadcasted_iota(jnp.int32, (BLOCK, BLOCK), 0)
    i1 = lax.broadcasted_iota(jnp.int32, (BLOCK, BLOCK), 1)
    tri = jnp.where(i0 >= i1, 1.0, 0.0).astype(BF16)
    triu = jnp.where(i0 <= i1, 1.0, 0.0).astype(BF16)
    dt = dt_ref[0, 0]
    dh, dm, dl = split3(dt * a_ref[0])
    cum = (dot(tri, dl) + dot(tri, dm)) + dot(tri, dh)
    logdt = jnp.log(dt) * LOG2E
    dtt = dtt_ref[0, 0]
    th, tm, tl = split3(dtt * at_ref[0])
    cumt = (dot(tl, triu) + dot(tm, triu)) + dot(th, triu)
    rt = jnp.log(dtt) * LOG2E - cumt
    cumr[...] = cum
    last = cum[BLOCK - 1 : BLOCK, :]

    seg_before_span = seg_of(first - 1, b1, b2, b3)
    seg_before = seg_of(start - 1, b1, b2, b3)
    seg_end = seg_of(start + BLOCK - 1, b1, b2, b3)

    @pl.when(j == 0)
    def _():
        c0[...] = jnp.zeros_like(c0)

    prior = c0[0:1, :]
    ld_ref[0, 0] = jnp.where(seg == seg_before_span, jnp.exp2(cum + prior), 0.0)

    bh, bl = split2(bf)
    sc = dot_nt(cb, bh)
    t_seg = seg_of(i0 + start, b1, b2, b3)
    s_seg = seg_of(i1 + start, b1, b2, b3)
    sc = jnp.where((i0 >= i1) & (t_seg == s_seg), sc, 0.0)

    @pl.when(j == 0)
    def _():
        y_ref[...] = jnp.zeros_like(y_ref)

    @pl.when(j == 1)
    def _():
        lead = jnp.where(seg == seg_before, jnp.exp2(cum), 0.0)
        sh, sl = split2(s0[...])
        y_ref[...] = spread(lead, sp) * (dot(cb, sh) + dot(cb, sl))

    lane = lax.broadcasted_iota(jnp.int32, (BLOCK, 128), 1)
    half = BLOCK // 2
    sc_t = sc[:half, :half]
    sc_l = sc[half:, :half]
    sc_r = sc[half:, half:]
    for pair in range(PER_GROUP // 2):
        cols = slice(pair * 128, pair * 128 + 128)
        xb = xf[:, cols].astype(BF16)
        res = []
        for h in (2 * pair, 2 * pair + 1):
            col = cum[:, h : h + 1]
            r = rt[h : h + 1, :]
            top = jnp.exp2(jnp.minimum(col[:half] + r[:, :half], 100.0)) * sc_t
            left = jnp.exp2(col[half:] + r[:, :half]) * sc_l
            right = jnp.exp2(jnp.minimum(col[half:] + r[:, half:], 100.0)) * sc_r
            bottom = jnp.concatenate([left.astype(BF16), right.astype(BF16)], axis=1)
            res.append(
                jnp.concatenate([dot(top.astype(BF16), xb[:half]), dot(bottom, xb)], axis=0)
            )
        intra = jnp.where(lane < CHANNEL_WIDTH, res[0], res[1])
        y_ref[:, cols] = y_ref[:, cols] + (intra + dx_ref[0:1, cols] * xb.astype(F32))

    bht, blt = split2(bf.T)

    def state_of(weights):
        xs = xf[:, 0:GW] * spread(weights, sp)
        xs_h, xs_l = split2(xs)
        return dot(bht, xs_h) + (dot(blt, xs_h) + dot(bht, xs_l))

    def at_end(seg_e):
        return jnp.where(seg == seg_e, jnp.exp2(last - cum + logdt), 0.0)

    own = state_of(at_end(seg_end))

    for r in range(SEQS - 1):
        end = meta[1 + r] - 1
        local = end - start
        owned = (local >= 0) & (local < BLOCK)

        @pl.when(owned)
        def _():
            ce = cumr[pl.ds(jnp.clip(local, 0, BLOCK - 1), 1), :]
            inside = (row <= end) & (seg == r)
            w = jnp.exp2(jnp.where(inside, ce - cum + logdt, -1e30))
            reach = jnp.where(seg_before == r, jnp.exp2(ce), 0.0)
            tail = state_of(w)
            keep = jnp.where(j == 1, 1.0, 0.0)
            reach8 = spread(jnp.broadcast_to(reach * keep, (8, 128)), sp)
            tail = tail + jnp.where(j == 1, reach8[0:1] * s0[...], 0.0)
            pt_ref[r] = tail.astype(BF16)
            full = jnp.where(seg_before_span == r, jnp.exp2(ce + prior), 0.0)
            aux_ref[1 + r : 2 + r, :] = spread(jnp.broadcast_to(full, (8, 128)), sp)[0:1]

    @pl.when(j == 0)
    def _():
        s0[...] = own
        c0[...] = jnp.broadcast_to(last, c0.shape)

    @pl.when(j == 1)
    def _():
        carry = jnp.where(seg_end == seg_before, jnp.exp2(last), 0.0)
        whole = jnp.where(seg_end == seg_before_span, jnp.exp2(last + prior), 0.0)
        carry8 = spread(jnp.broadcast_to(carry, (8, 128)), sp)
        whole8 = spread(jnp.broadcast_to(whole, (8, 128)), sp)
        st_ref[...] = (carry8[0:1] * s0[...] + own).astype(BF16)
        aux_ref[0:1, :] = whole8[0:1]


def local_pass(meta, conv, halo, conv_weight, conv_bias, dt, dtt, a, at, dx):
    length = conv.shape[0]
    blocks = length // BLOCK
    maps = D // 128
    grid = (GROUPS, blocks)
    xs = lambda rows: [
        pl.BlockSpec((rows, GW), lambda g, j: (0, g)),
        pl.BlockSpec((rows, 128), lambda g, j: (0, maps + g)),
        pl.BlockSpec((rows, 128), lambda g, j: (0, maps + GROUPS + g)),
    ]
    in_specs = (
        [
            pl.BlockSpec(memory_space=pltpu.SMEM),
            pl.BlockSpec((BLOCK, GW), lambda g, j: (j, g)),
            pl.BlockSpec((BLOCK, 128), lambda g, j: (j, maps + g)),
            pl.BlockSpec((BLOCK, 128), lambda g, j: (j, maps + GROUPS + g)),
        ]
        + xs(8)
        + xs(KERNEL)
        + xs(1)
        + [
            pl.BlockSpec((1, 1, BLOCK, 128), lambda g, j: (g, j, 0, 0)),
            pl.BlockSpec((1, 1, PER_GROUP, BLOCK), lambda g, j: (g, j, 0, 0)),
            pl.BlockSpec((1, 1, 128), lambda g, j: (g, 0, 0)),
            pl.BlockSpec((1, PER_GROUP, 1), lambda g, j: (g, 0, 0)),
            pl.BlockSpec((1, GW), lambda g, j: (0, g)),
        ]
    )
    out_specs = [
        pl.BlockSpec((BLOCK, GW), lambda g, j: (j, g)),
        pl.BlockSpec((STATE, GW), lambda g, j: (0, g)),
        pl.BlockSpec((SEQS - 1, STATE, GW), lambda g, j: (0, 0, g)),
        pl.BlockSpec((8, GW), lambda g, j: (0, g)),
        pl.BlockSpec((BLOCK, 128), lambda g, j: (j, g)),
        pl.BlockSpec((1, 1, BLOCK, 128), lambda g, j: (g, j, 0, 0)),
    ]
    out_shape = [
        jax.ShapeDtypeStruct((length, D), F32),
        jax.ShapeDtypeStruct((STATE, D), BF16),
        jax.ShapeDtypeStruct((SEQS - 1, STATE, D), BF16),
        jax.ShapeDtypeStruct((8, D), F32),
        jax.ShapeDtypeStruct((length, GROUPS * STATE), BF16),
        jax.ShapeDtypeStruct((GROUPS, blocks, BLOCK, 128), F32),
    ]
    return pl.pallas_call(
        local_kernel,
        grid=grid,
        in_specs=in_specs,
        out_specs=out_specs,
        out_shape=out_shape,
        scratch_shapes=[
            pltpu.VMEM((BLOCK + 8, GW + 256), F32),
            pltpu.VMEM((BLOCK, GW + 256), F32),
            pltpu.VMEM((STATE, GW), F32),
            pltpu.VMEM((8, 128), F32),
            pltpu.VMEM((BLOCK, 128), F32),
            pltpu.VMEM((128, GW), BF16),
        ],
        compiler_params=pltpu.CompilerParams(
            vmem_limit_bytes=VMEM_LIMIT, dimension_semantics=("arbitrary", "arbitrary")
        ),
        name="local_pass",
    )(
        meta, conv, conv, conv, halo, halo, halo, conv_weight, conv_weight, conv_weight,
        conv_bias, conv_bias, conv_bias, dt, dtt, a, at, dx,
    )


def exchange_kernel(
    n,
    st_ref,
    aux_ref,
    ent_ref,
    fin_ref,
    rs,
    ra,
    eb,
    send1,
    recv1,
    send2,
    recv2,
    send3,
    recv3,
):
    me = lax.axis_index("seq")
    width = D // n
    barrier = pltpu.get_barrier_semaphore()

    def peer(i):
        return lax.rem(me + i, n)

    def cols(p):
        return pl.ds(pl.multiple_of(p * width, width), width)

    def greet(i, _):
        pl.semaphore_signal(barrier, inc=1, device_id={"seq": peer(i)}, device_id_type=MESH)
        return 0

    lax.fori_loop(1, n, greet, 0)
    pl.semaphore_wait(barrier, n - 1)

    def out(p, slot):
        return (
            pltpu.make_async_remote_copy(
                src_ref=st_ref.at[:, cols(p)],
                dst_ref=rs.at[slot],
                send_sem=send1.at[p],
                recv_sem=recv1.at[slot],
                device_id={"seq": p},
                device_id_type=MESH,
            ),
            pltpu.make_async_remote_copy(
                src_ref=aux_ref.at[:, cols(p)],
                dst_ref=ra.at[slot],
                send_sem=send2.at[p],
                recv_sem=recv2.at[slot],
                device_id={"seq": p},
                device_id_type=MESH,
            ),
        )

    def back(p, slot):
        return pltpu.make_async_remote_copy(
            src_ref=eb.at[p],
            dst_ref=ent_ref.at[:, cols(slot)],
            send_sem=send3.at[p],
            recv_sem=recv3.at[slot],
            device_id={"seq": p},
            device_id_type=MESH,
        )

    def begin(i, _):
        for copy in out(peer(i), me):
            copy.start()
        return 0

    lax.fori_loop(1, n, begin, 0)
    rs[me] = st_ref[:, cols(me)]
    ra[me] = aux_ref[:, cols(me)]

    def arrive(i, _):
        for copy in out(peer(i), peer(i)):
            copy.wait_recv()
        return 0

    lax.fori_loop(1, n, arrive, 0)

    fin_ref[...] = jnp.zeros_like(fin_ref)

    def scan(d, _):
        now = fin_ref[SEQS - 1]
        eb[d] = now.astype(BF16)
        for r in range(SEQS - 1):
            fin_ref[r] = fin_ref[r] + ra[d, 1 + r : 2 + r, :] * now
        fin_ref[SEQS - 1] = ra[d, 0:1, :] * now + rs[d].astype(F32)
        return 0

    lax.fori_loop(0, n, scan, 0)

    def reply(i, _):
        back(peer(i), me).start()
        return 0

    lax.fori_loop(1, n, reply, 0)
    ent_ref[:, cols(me)] = eb[me]

    def done(i, _):
        back(peer(i), peer(i)).wait_recv()
        return 0

    lax.fori_loop(1, n, done, 0)

    def drain(i, _):
        for copy in out(peer(i), me):
            copy.wait_send()
        back(peer(i), me).wait_send()
        return 0

    lax.fori_loop(1, n, drain, 0)


def exchange(states, aux, n):
    width = D // n
    vmem = pl.BlockSpec(memory_space=pltpu.VMEM)
    return pl.pallas_call(
        functools.partial(exchange_kernel, n),
        in_specs=[vmem, vmem],
        out_specs=[vmem, vmem],
        out_shape=[
            jax.ShapeDtypeStruct((STATE, D), BF16),
            jax.ShapeDtypeStruct((SEQS, STATE, width), F32),
        ],
        scratch_shapes=[
            pltpu.VMEM((n, STATE, width), BF16),
            pltpu.VMEM((n, 8, width), F32),
            pltpu.VMEM((n, STATE, width), BF16),
        ]
        + [pltpu.SemaphoreType.DMA((n,)) for _ in range(6)],
        compiler_params=pltpu.CompilerParams(
            collective_id=0, has_side_effects=True, vmem_limit_bytes=VMEM_LIMIT
        ),
        name="exchange",
    )(states, aux)


def finish_kernel(y_ref, c_ref, e_ref, ld_ref, gate_ref, nw_ref, out_ref, sp):
    @pl.when((pl.program_id(0) == 0) & (pl.program_id(1) == 0))
    def _():
        sp[...] = spread_matrix()

    v = y_ref[...] + spread(ld_ref[0, 0], sp) * dot(c_ref[...], e_ref[...])
    v = v * silu(gate_ref[...].astype(F32))
    scale = lax.rsqrt(jnp.mean(v * v, axis=1, keepdims=True) + TINY_FLOOR)
    out_ref[...] = (v * scale * nw_ref[...]).astype(BF16)


def finish(y, c, entering, lead, gate, norm_weight):
    length = y.shape[0]
    block = lambda width: pl.BlockSpec((BLOCK, width), lambda g, j: (j, g))
    return pl.pallas_call(
        finish_kernel,
        grid=(GROUPS, length // BLOCK),
        in_specs=[
            block(GW),
            block(STATE),
            pl.BlockSpec((STATE, GW), lambda g, j: (0, g)),
            pl.BlockSpec((1, 1, BLOCK, 128), lambda g, j: (g, j, 0, 0)),
            block(GW),
            pl.BlockSpec((1, GW), lambda g, j: (0, g)),
        ],
        out_specs=block(GW),
        out_shape=jax.ShapeDtypeStruct((length, D), BF16),
        scratch_shapes=[pltpu.VMEM((128, GW), BF16)],
        compiler_params=pltpu.CompilerParams(
            vmem_limit_bytes=VMEM_LIMIT, dimension_semantics=("arbitrary", "arbitrary")
        ),
        name="finish",
    )(y, c, entering, lead, gate, norm_weight)


def tail_kernel(
    n,
    m,
    rows_ref,
    w_ref,
    tails_ref,
    reach_ref,
    resid_ref,
    gain_ref,
    vocab_ref,
    hid_ref,
    max_ref,
    fin_ref,
    vbuf,
    rrecv,
    ragg,
    wbuf,
    part,
    precv,
    h1,
    h2,
    hf,
    mx1,
    mx2,
    trecv,
    vsem,
    rs_s,
    rs_r,
    ag_s,
    ag_r,
    w_s,
    w_r,
    pt_s,
    pt_r,
    h1_s,
    h1_r,
    h2_s,
    h2_r,
    m1_s,
    m1_r,
    m2_s,
    m2_r,
    t_s,
    t_r,
):
    s = lax.axis_index("seq")
    b = lax.axis_index("req")
    width = D // n
    depth = D // m
    w_place = 2 * b + s // 8
    w_slot = lax.rem(s, 8)
    to_self = w_place == s
    from_b = s // 2
    from_s = 8 * lax.rem(s, 2)

    load = pltpu.make_async_copy(vocab_ref, vbuf, vsem)
    load.start()

    barrier = pltpu.get_barrier_semaphore()

    def signal(where):
        pl.semaphore_signal(barrier, inc=1, device_id=where, device_id_type=MESH)

    def seq_peer(i):
        return lax.rem(s + i, n)

    def req_peer(i):
        return lax.rem(b + i, m)

    def greet_seq(i, _):
        signal({"seq": seq_peer(i)})
        return 0

    def greet_req(i, _):
        signal({"req": req_peer(i)})
        return 0

    def greet_w(i, _):
        @pl.when(jnp.logical_not(to_self & (i == b)))
        def _():
            signal({"req": i, "seq": w_place})

        @pl.when(jnp.logical_not((from_b == b) & (from_s + i == s)))
        def _():
            signal({"req": from_b, "seq": from_s + i})

        return 0

    lax.fori_loop(1, n, greet_seq, 0)
    lax.fori_loop(1, m, greet_req, 0)
    lax.fori_loop(0, m, greet_w, 0)
    pl.semaphore_wait(barrier, (n - 1) + (m - 1) + 2 * m - 2 * to_self.astype(jnp.int32))

    def remote(src, dst, send, recv, where):
        return pltpu.make_async_remote_copy(
            src_ref=src, dst_ref=dst, send_sem=send, recv_sem=recv, device_id=where, device_id_type=MESH
        )

    def over(count, peer, copy, me):
        def start(i, _):
            copy(peer(i), me).start()
            return 0

        def arrive(i, _):
            copy(peer(i), peer(i)).wait_recv()
            return 0

        def drain(i, _):
            copy(peer(i), me).wait_send()
            return 0

        return (
            lambda: lax.fori_loop(1, count, start, 0),
            lambda: lax.fori_loop(1, count, arrive, 0),
            lambda: lax.fori_loop(1, count, drain, 0),
        )

    def rows_copy(p, slot):
        return remote(rows_ref.at[p], rrecv.at[slot], rs_s.at[p], rs_r.at[slot], {"seq": p})

    def gather_copy(p, slot):
        return remote(ragg.at[b], ragg.at[slot], ag_s.at[p], ag_r.at[slot], {"req": p})

    def part_copy(p, slot):
        cols = pl.ds(pl.multiple_of(lax.rem(p, 2) * 256, 256), 256)
        return remote(part.at[p // 2, :, cols], precv.at[slot], pt_s.at[p], pt_r.at[slot], {"seq": p})

    def h1_copy(p, slot):
        return remote(h1.at[b], h1.at[slot], h1_s.at[p], h1_r.at[slot], {"req": p})

    def h2_copy(p, slot):
        return remote(h1, h2.at[slot // 2, lax.rem(slot, 2)], h2_s.at[p], h2_r.at[slot], {"seq": p})

    def m1_copy(p, slot):
        return remote(mx1.at[b], mx1.at[slot], m1_s.at[p], m1_r.at[slot], {"req": p})

    def m2_copy(p, slot):
        return remote(mx2.at[s], mx2.at[slot], m2_s.at[p], m2_r.at[slot], {"seq": p})

    def t_copy(p, slot, r):
        cols = pl.ds(pl.multiple_of(p * width, width), width)
        return remote(tails_ref.at[r, :, cols], trecv.at[slot, r], t_s.at[p, r], t_r.at[slot, r], {"seq": p})

    def send_tails(lo, hi):
        def start(i, _):
            for r in range(SEQS - 1):
                t_copy(seq_peer(i), s, r).start()
            return 0

        lax.fori_loop(lo, hi, start, 0)

    rows_go, rows_in, rows_out = over(n, seq_peer, rows_copy, s)
    ag_go, ag_in, ag_out = over(m, req_peer, gather_copy, b)
    part_go, part_in, part_out = over(n, seq_peer, part_copy, s)
    h1_go, h1_in, h1_out = over(m, req_peer, h1_copy, b)
    h2_go, h2_in, h2_out = over(n, seq_peer, h2_copy, s)
    m1_go, m1_in, m1_out = over(m, req_peer, m1_copy, b)
    m2_go, m2_in, m2_out = over(n, seq_peer, m2_copy, s)

    rows_go()

    def w_copy(p):
        cols = pl.ds(pl.multiple_of(p * depth, depth), depth)
        return remote(
            w_ref.at[:, cols], wbuf.at[w_slot], w_s.at[p], w_r.at[w_slot], {"req": p, "seq": w_place}
        )

    def w_start(i, _):
        p = lax.rem(b + i, m)

        @pl.when(jnp.logical_not(to_self & (p == b)))
        def _():
            w_copy(p).start()

        return 0

    lax.fori_loop(0, m, w_start, 0)

    @pl.when(to_self)
    def _():
        wbuf[w_slot] = w_ref[:, pl.ds(pl.multiple_of(b * depth, depth), depth)]

    rrecv[s] = rows_ref[s]
    send_tails(1, 3)
    rows_in()
    ragg[b] = jnp.sum(rrecv[...], axis=0)
    ag_go()
    send_tails(3, 4)
    ag_in()

    def w_arrive(i, _):
        @pl.when(jnp.logical_not((from_b == b) & (from_s + i == s)))
        def _():
            remote(
                w_ref.at[:, pl.ds(0, depth)], wbuf.at[i], w_s.at[i], w_r.at[i], {"req": i, "seq": w_place}
            ).wait_recv()

        return 0

    lax.fori_loop(0, m, w_arrive, 0)

    lhs = ragg[...].reshape(8 * m, 128).astype(BF16)
    weights = wbuf[...].reshape(m * 32, depth)
    place = lax.broadcasted_iota(jnp.int32, (8 * m, depth), 0)
    both = jnp.where(place % 8 < 4, dot(lhs, weights[0:128]), dot(lhs, weights[128:256]))
    both = both + pltpu.roll(both, 4, 0)
    part[...] = both.reshape(m, 8, depth)
    part_go()
    precv[s] = part[s // 2, :, pl.ds(pl.multiple_of(lax.rem(s, 2) * 256, 256), 256)]
    send_tails(4, 8)
    part_in()
    hidden = jnp.sum(precv[...], axis=0) + resid_ref[...].astype(F32)
    upper = pltpu.roll(hidden[:, 128:256], 4, 0)
    eight = lax.broadcasted_iota(jnp.int32, (8, 128), 0)
    h1[b] = jnp.where(eight < 4, upper, hidden[:, 0:128]).astype(BF16)
    h1_go()
    send_tails(8, 9)
    h1_in()
    h2_go()
    h2[s // 2, lax.rem(s, 2)] = h1[...]
    send_tails(9, n)
    h2_in()

    for k in range(m):
        for q in range(2):
            piece = h2[:, q, k].astype(F32).reshape(8 * m, 128)
            lo = k * depth + q * 256
            hf[:, lo : lo + 128] = piece
            hf[:, lo + 128 : lo + 256] = pltpu.roll(piece, 4, 0)
    h = hf[...]
    hid_ref[...] = hf[pl.ds(pl.multiple_of(b * 8, 8), 8), :].astype(BF16)
    scale = lax.rsqrt(jnp.mean(h * h, axis=1, keepdims=True) + TINY_FLOOR)
    normed = (h * scale * gain_ref[...]).astype(BF16)
    load.wait()
    top = jnp.full((1, 8 * m), -jnp.inf, F32)
    chunk = 256
    for k in range(vbuf.shape[0] // chunk):
        logits = dot_nt(vbuf[k * chunk : (k + 1) * chunk, :], normed)
        top = jnp.maximum(top, jnp.max(logits, axis=0, keepdims=True))
    top = jnp.concatenate([top, top], axis=1)
    mx1[b] = jnp.broadcast_to(top, (8, 128))
    m1_go()
    m1_in()
    mx2[s] = jnp.max(mx1[...], axis=0)
    m2_go()

    def t_arrive(i, _):
        for r in range(SEQS - 1):
            t_copy(seq_peer(i), seq_peer(i), r).wait_recv()
        return 0

    lax.fori_loop(1, n, t_arrive, 0)
    trecv[s] = tails_ref[:, :, pl.ds(pl.multiple_of(s * width, width), width)]

    def collect(r, _):
        total = reach_ref[r]
        for d in range(n):
            total = total + trecv[d, r].astype(F32)
        fin_ref[r] = total.T
        return 0

    lax.fori_loop(0, SEQS - 1, collect, 0)
    fin_ref[SEQS - 1] = reach_ref[SEQS - 1].T
    m2_in()
    max_ref[...] = jnp.max(mx2[...], axis=0)

    for drain in (rows_out, ag_out, part_out, h1_out, h2_out, m1_out, m2_out):
        drain()

    def w_drain(p, _):
        @pl.when(jnp.logical_not(to_self & (p == b)))
        def _():
            w_copy(p).wait_send()

        return 0

    lax.fori_loop(0, m, w_drain, 0)

    def t_drain(i, _):
        for r in range(SEQS - 1):
            t_copy(seq_peer(i), s, r).wait_send()
        return 0

    lax.fori_loop(1, n, t_drain, 0)


def tail(rows, out_weight, tails, reached, resid, gain, vocab, n, m):
    width = D // n
    vmem = pl.BlockSpec(memory_space=pltpu.VMEM)
    dma = pltpu.SemaphoreType.DMA
    return pl.pallas_call(
        functools.partial(tail_kernel, n, m),
        in_specs=[vmem] * 6 + [pl.BlockSpec(memory_space=pl.ANY)],
        out_specs=[vmem] * 3,
        out_shape=[
            jax.ShapeDtypeStruct((8, D), BF16),
            jax.ShapeDtypeStruct((8, 128), F32),
            jax.ShapeDtypeStruct((SEQS, width, STATE), F32),
        ],
        scratch_shapes=[
            pltpu.VMEM(vocab.shape, BF16),
            pltpu.VMEM((n, 8, 128), F32),
            pltpu.VMEM((m, 8, 128), F32),
            pltpu.VMEM((m, 32, D // m), BF16),
            pltpu.VMEM((m, 8, D // m), F32),
            pltpu.VMEM((n, 8, 256), F32),
            pltpu.VMEM((m, 8, 128), BF16),
            pltpu.VMEM((n // 2, 2, m, 8, 128), BF16),
            pltpu.VMEM((8 * m, D), F32),
            pltpu.VMEM((m, 8, 128), F32),
            pltpu.VMEM((n, 8, 128), F32),
            pltpu.VMEM((n, SEQS - 1, STATE, width), BF16),
            dma,
            dma((n,)),
            dma((n,)),
            dma((m,)),
            dma((m,)),
            dma((m,)),
            dma((m,)),
            dma((n,)),
            dma((n,)),
            dma((m,)),
            dma((m,)),
            dma((n,)),
            dma((n,)),
            dma((m,)),
            dma((m,)),
            dma((n,)),
            dma((n,)),
            dma((n, SEQS - 1)),
            dma((n, SEQS - 1)),
        ],
        compiler_params=pltpu.CompilerParams(
            collective_id=1, has_side_effects=True, vmem_limit_bytes=VMEM_LIMIT
        ),
        name="tail",
    )(rows, out_weight, tails, reached, resid, gain, vocab)


def body(
    conv_input,
    gate_projected,
    step_raw,
    step_bias,
    decay_log,
    head_direct_gain,
    conv_weight,
    convolution_bias,
    norm_weight,
    lengths,
    out_weight,
    residual_last,
    final_gain,
    vocab_weight,
):
    local_len = conv_input.shape[1]
    inner = HEADS * CHANNEL_WIDTH
    count = local_len // BLOCK
    seq_count = lax.axis_size("seq")
    seq_place = lax.axis_index("seq")
    req_place = lax.axis_index("req")
    first = seq_place * local_len
    conv = conv_input[0]
    route = [(i, i + 1) for i in range(seq_count - 1)]
    halo = lax.ppermute(conv[local_len - 8 :], "seq", route)
    bounds = jnp.cumsum(lengths[0]).astype(jnp.int32)
    meta = jnp.concatenate([first.astype(jnp.int32)[None], bounds])

    step = jax.nn.softplus(step_raw[0] + step_bias)
    step = step.reshape(count, BLOCK, GROUPS, PER_GROUP)
    dt = jnp.tile(step.transpose(2, 0, 1, 3), (1, 1, 1, 128 // PER_GROUP))
    dtt = step.transpose(2, 0, 3, 1)
    rate = (-jnp.exp(decay_log) * LOG2E).reshape(GROUPS, PER_GROUP)
    a = jnp.tile(rate, (1, 128 // PER_GROUP))[:, None, :]
    at = rate[:, :, None]
    dx = jnp.repeat(head_direct_gain, CHANNEL_WIDTH)[None]

    y, states, tails, aux, c, lead = local_pass(
        meta, conv, halo, conv_weight, convolution_bias[None], dt, dtt, a, at, dx
    )
    entering, reached = exchange(states, aux, seq_count)
    gated = finish(y, c, entering, lead, gate_projected[0], norm_weight[None])

    lasts = []
    for request in range(SEQS):
        local_end = bounds[request] - 1 - first
        owned = (local_end >= 0) & (local_end < local_len)
        spot = jnp.clip(local_end, 0, local_len - 1)
        lasts.append(jnp.where(owned, gated[spot].astype(jnp.float32), 0.0))
    last_local = jnp.stack(lasts)
    req_count = lax.axis_size("req")
    rows = last_local.reshape(SEQS, seq_count, 2, 128).transpose(1, 2, 0, 3).reshape(seq_count, 8, 128)
    resid = lax.dynamic_slice(
        residual_last,
        (seq_place // 2, 0, req_place * (D // req_count) + (seq_place % 2) * 256),
        (1, SEQS, 256),
    )[0]
    resid = jnp.concatenate([jnp.zeros_like(resid), resid], axis=0)
    hid, top, final = tail(
        rows, out_weight, tails, reached, resid, final_gain[None], vocab_weight, seq_count, req_count
    )
    own_hidden = hid[None, SEQS:]
    max_logit = lax.dynamic_slice(top, (0, req_place * 8 + SEQS), (1, SEQS))
    final_states = final.reshape(SEQS, HEADS // seq_count, CHANNEL_WIDTH, STATE)[None]
    return (gated[None], final_states, own_hidden, max_logit)


def solution(mesh):
    return jax.shard_map(
        body,
        mesh=mesh,
        in_specs=(
            P("req", "seq", None),
            P("req", "seq", None),
            P("req", "seq", None),
            P(),
            P(),
            P(),
            P(),
            P(),
            P(),
            P("req", None),
            P(("req", "seq"), None),
            P(),
            P(),
            P(("req", "seq"), None),
        ),
        out_specs=(
            P("req", "seq", None),
            P("req", None, "seq", None, None),
            P("req", None, None),
            P("req", None),
        ),
        check_vma=False,
    )
```

```python
import functools

import jax
import jax.numpy as jnp
from jax import lax
from jax.experimental import pallas as pl
from jax.experimental.pallas import tpu as pltpu
from jax.sharding import PartitionSpec as P

D = 4096
HEADS = 64
CHANNEL_WIDTH = 64
GROUPS = 4
STATE = 128
KERNEL = 4
BLOCK = 256
SEQS = 4
PER_GROUP = HEADS // GROUPS
GW = PER_GROUP * CHANNEL_WIDTH
TINY_FLOOR = 1e-05
LOG2E = 1.4426950408889634
MESH = pl.DeviceIdType.MESH
F32 = jnp.float32
BF16 = jnp.bfloat16
VMEM_LIMIT = 60 * 1024 * 1024


def dot(a, b):
    return lax.dot_general(a, b, (((1,), (0,)), ((), ())), preferred_element_type=F32)


def dot_nt(a, b):
    return lax.dot_general(a, b, (((1,), (1,)), ((), ())), preferred_element_type=F32)


def split2(x):
    hi = x.astype(BF16)
    return hi, (x - hi.astype(F32)).astype(BF16)


def split3(x):
    hi = x.astype(BF16)
    rest = x - hi.astype(F32)
    mid = rest.astype(BF16)
    return hi, mid, (rest - mid.astype(F32)).astype(BF16)


def seg_of(place, b1, b2, b3):
    one = lambda b: (place >= b).astype(jnp.int32)
    return one(b1) + one(b2) + one(b3)


def spread_matrix():
    lane = lax.broadcasted_iota(jnp.int32, (128, GW), 0)
    col = lax.broadcasted_iota(jnp.int32, (128, GW), 1)
    hit = (lane < 48) & (lane % PER_GROUP == col // CHANNEL_WIDTH)
    return jnp.where(hit, 1.0, 0.0).astype(BF16)


def spread(v, spread_ref):
    hi, mid, lo = split3(v)
    lane = lax.broadcasted_iota(jnp.int32, v.shape, 1)
    parts = jnp.where(
        lane < 16, hi.astype(F32), jnp.where(lane < 32, mid.astype(F32), lo.astype(F32))
    ).astype(BF16)
    return dot(parts, spread_ref[...])


def silu(x):
    return x * jax.nn.sigmoid(x)


def local_kernel(
    meta,
    x_ref,
    b_ref,
    c_ref,
    xh_ref,
    bh_ref,
    ch_ref,
    wx_ref,
    wb_ref,
    wc_ref,
    vx_ref,
    vb_ref,
    vc_ref,
    dt_ref,
    dtt_ref,
    a_ref,
    at_ref,
    dx_ref,
    y_ref,
    st_ref,
    pt_ref,
    aux_ref,
    co_ref,
    ld_ref,
    xext,
    xf,
    s0,
    c0,
    cumr,
    sp,
):
    g = pl.program_id(0)
    j = pl.program_id(1)
    first = meta[0]
    b1, b2, b3 = meta[1], meta[2], meta[3]
    start = first + j * BLOCK

    @pl.when((g == 0) & (j == 0))
    def _():
        sp[...] = spread_matrix()

    @pl.when(j == 0)
    def _():
        xext[0:8, 0:GW] = xh_ref[...].astype(F32)
        xext[0:8, GW : GW + 128] = bh_ref[...].astype(F32)
        xext[0:8, GW + 128 : GW + 256] = ch_ref[...].astype(F32)
        pt_ref[...] = jnp.zeros_like(pt_ref)
        aux_ref[...] = jnp.zeros_like(aux_ref)

    @pl.when(j == 1)
    def _():
        xext[0:8, :] = xext[BLOCK : BLOCK + 8, :]

    xext[8 : BLOCK + 8, 0:GW] = x_ref[...].astype(F32)
    xext[8 : BLOCK + 8, GW : GW + 128] = b_ref[...].astype(F32)
    xext[8 : BLOCK + 8, GW + 128 : GW + 256] = c_ref[...].astype(F32)

    row = lax.broadcasted_iota(jnp.int32, (BLOCK, 128), 0) + start
    seg = seg_of(row, b1, b2, b3)
    same = [(seg_of(row - k, b1, b2, b3) == seg).astype(F32) for k in (3, 2, 1)]
    for c in range(10):
        cols = slice(c * 128, c * 128 + 128)
        w_ref, v_ref, lo = (
            (wx_ref, vx_ref, c * 128) if c < 8 else ((wb_ref, vb_ref, 0) if c == 8 else (wc_ref, vc_ref, 0))
        )
        part = slice(lo, lo + 128)
        total = jnp.broadcast_to(v_ref[0:1, part], (BLOCK, 128))
        for k in range(3):
            total = total + w_ref[k : k + 1, part] * xext[5 + k : 5 + k + BLOCK, cols] * same[k]
        total = total + w_ref[3:4, part] * xext[8 : 8 + BLOCK, cols]
        xf[:, cols] = silu(total)

    bf = xf[:, GW : GW + 128]
    cb = xf[:, GW + 128 : GW + 256].astype(BF16)
    co_ref[...] = cb

    i0 = lax.broadcasted_iota(jnp.int32, (BLOCK, BLOCK), 0)
    i1 = lax.broadcasted_iota(jnp.int32, (BLOCK, BLOCK), 1)
    tri = jnp.where(i0 >= i1, 1.0, 0.0).astype(BF16)
    triu = jnp.where(i0 <= i1, 1.0, 0.0).astype(BF16)
    dt = dt_ref[0, 0]
    dh, dm, dl = split3(dt * a_ref[0])
    cum = (dot(tri, dl) + dot(tri, dm)) + dot(tri, dh)
    logdt = jnp.log(dt) * LOG2E
    dtt = dtt_ref[0, 0]
    th, tm, tl = split3(dtt * at_ref[0])
    cumt = (dot(tl, triu) + dot(tm, triu)) + dot(th, triu)
    rt = jnp.log(dtt) * LOG2E - cumt
    cumr[...] = cum
    last = cum[BLOCK - 1 : BLOCK, :]

    seg_before_span = seg_of(first - 1, b1, b2, b3)
    seg_before = seg_of(start - 1, b1, b2, b3)
    seg_end = seg_of(start + BLOCK - 1, b1, b2, b3)

    @pl.when(j == 0)
    def _():
        c0[...] = jnp.zeros_like(c0)

    prior = c0[0:1, :]
    ld_ref[0, 0] = jnp.where(seg == seg_before_span, jnp.exp2(cum + prior), 0.0)

    bh, bl = split2(bf)
    sc = dot_nt(cb, bh)
    t_seg = seg_of(i0 + start, b1, b2, b3)
    s_seg = seg_of(i1 + start, b1, b2, b3)
    sc = jnp.where((i0 >= i1) & (t_seg == s_seg), sc, 0.0)

    @pl.when(j == 0)
    def _():
        y_ref[...] = jnp.zeros_like(y_ref)

    @pl.when(j == 1)
    def _():
        lead = jnp.where(seg == seg_before, jnp.exp2(cum), 0.0)
        sh, sl = split2(s0[...])
        y_ref[...] = spread(lead, sp) * (dot(cb, sh) + dot(cb, sl))

    lane = lax.broadcasted_iota(jnp.int32, (BLOCK, 128), 1)
    half = BLOCK // 2
    sc_t = sc[:half, :half]
    sc_l = sc[half:, :half]
    sc_r = sc[half:, half:]
    for pair in range(PER_GROUP // 2):
        cols = slice(pair * 128, pair * 128 + 128)
        xb = xf[:, cols].astype(BF16)
        res = []
        for h in (2 * pair, 2 * pair + 1):
            col = cum[:, h : h + 1]
            r = rt[h : h + 1, :]
            top = jnp.exp2(jnp.minimum(col[:half] + r[:, :half], 100.0)) * sc_t
            left = jnp.exp2(col[half:] + r[:, :half]) * sc_l
            right = jnp.exp2(jnp.minimum(col[half:] + r[:, half:], 100.0)) * sc_r
            bottom = jnp.concatenate([left.astype(BF16), right.astype(BF16)], axis=1)
            res.append(
                jnp.concatenate([dot(top.astype(BF16), xb[:half]), dot(bottom, xb)], axis=0)
            )
        intra = jnp.where(lane < CHANNEL_WIDTH, res[0], res[1])
        y_ref[:, cols] = y_ref[:, cols] + (intra + dx_ref[0:1, cols] * xb.astype(F32))

    bht, blt = split2(bf.T)

    def state_of(weights):
        xs = xf[:, 0:GW] * spread(weights, sp)
        xs_h, xs_l = split2(xs)
        return dot(bht, xs_h) + (dot(blt, xs_h) + dot(bht, xs_l))

    def at_end(seg_e):
        return jnp.where(seg == seg_e, jnp.exp2(last - cum + logdt), 0.0)

    own = state_of(at_end(seg_end))

    for r in range(SEQS - 1):
        end = meta[1 + r] - 1
        local = end - start
        owned = (local >= 0) & (local < BLOCK)

        @pl.when(owned)
        def _():
            ce = cumr[pl.ds(jnp.clip(local, 0, BLOCK - 1), 1), :]
            inside = (row <= end) & (seg == r)
            w = jnp.exp2(jnp.where(inside, ce - cum + logdt, -1e30))
            reach = jnp.where(seg_before == r, jnp.exp2(ce), 0.0)
            tail = state_of(w)
            keep = jnp.where(j == 1, 1.0, 0.0)
            reach8 = spread(jnp.broadcast_to(reach * keep, (8, 128)), sp)
            tail = tail + jnp.where(j == 1, reach8[0:1] * s0[...], 0.0)
            pt_ref[r] = tail.astype(BF16)
            full = jnp.where(seg_before_span == r, jnp.exp2(ce + prior), 0.0)
            aux_ref[1 + r : 2 + r, :] = spread(jnp.broadcast_to(full, (8, 128)), sp)[0:1]

    @pl.when(j == 0)
    def _():
        s0[...] = own
        c0[...] = jnp.broadcast_to(last, c0.shape)

    @pl.when(j == 1)
    def _():
        carry = jnp.where(seg_end == seg_before, jnp.exp2(last), 0.0)
        whole = jnp.where(seg_end == seg_before_span, jnp.exp2(last + prior), 0.0)
        carry8 = spread(jnp.broadcast_to(carry, (8, 128)), sp)
        whole8 = spread(jnp.broadcast_to(whole, (8, 128)), sp)
        st_ref[...] = (carry8[0:1] * s0[...] + own).astype(BF16)
        aux_ref[0:1, :] = whole8[0:1]


def local_pass(meta, conv, halo, conv_weight, conv_bias, dt, dtt, a, at, dx):
    length = conv.shape[0]
    blocks = length // BLOCK
    maps = D // 128
    grid = (GROUPS, blocks)
    xs = lambda rows: [
        pl.BlockSpec((rows, GW), lambda g, j: (0, g)),
        pl.BlockSpec((rows, 128), lambda g, j: (0, maps + g)),
        pl.BlockSpec((rows, 128), lambda g, j: (0, maps + GROUPS + g)),
    ]
    in_specs = (
        [
            pl.BlockSpec(memory_space=pltpu.SMEM),
            pl.BlockSpec((BLOCK, GW), lambda g, j: (j, g)),
            pl.BlockSpec((BLOCK, 128), lambda g, j: (j, maps + g)),
            pl.BlockSpec((BLOCK, 128), lambda g, j: (j, maps + GROUPS + g)),
        ]
        + xs(8)
        + xs(KERNEL)
        + xs(1)
        + [
            pl.BlockSpec((1, 1, BLOCK, 128), lambda g, j: (g, j, 0, 0)),
            pl.BlockSpec((1, 1, PER_GROUP, BLOCK), lambda g, j: (g, j, 0, 0)),
            pl.BlockSpec((1, 1, 128), lambda g, j: (g, 0, 0)),
            pl.BlockSpec((1, PER_GROUP, 1), lambda g, j: (g, 0, 0)),
            pl.BlockSpec((1, GW), lambda g, j: (0, g)),
        ]
    )
    out_specs = [
        pl.BlockSpec((BLOCK, GW), lambda g, j: (j, g)),
        pl.BlockSpec((STATE, GW), lambda g, j: (0, g)),
        pl.BlockSpec((SEQS - 1, STATE, GW), lambda g, j: (0, 0, g)),
        pl.BlockSpec((8, GW), lambda g, j: (0, g)),
        pl.BlockSpec((BLOCK, 128), lambda g, j: (j, g)),
        pl.BlockSpec((1, 1, BLOCK, 128), lambda g, j: (g, j, 0, 0)),
    ]
    out_shape = [
        jax.ShapeDtypeStruct((length, D), F32),
        jax.ShapeDtypeStruct((STATE, D), BF16),
        jax.ShapeDtypeStruct((SEQS - 1, STATE, D), BF16),
        jax.ShapeDtypeStruct((8, D), F32),
        jax.ShapeDtypeStruct((length, GROUPS * STATE), BF16),
        jax.ShapeDtypeStruct((GROUPS, blocks, BLOCK, 128), F32),
    ]
    return pl.pallas_call(
        local_kernel,
        grid=grid,
        in_specs=in_specs,
        out_specs=out_specs,
        out_shape=out_shape,
        scratch_shapes=[
            pltpu.VMEM((BLOCK + 8, GW + 256), F32),
            pltpu.VMEM((BLOCK, GW + 256), F32),
            pltpu.VMEM((STATE, GW), F32),
            pltpu.VMEM((8, 128), F32),
            pltpu.VMEM((BLOCK, 128), F32),
            pltpu.VMEM((128, GW), BF16),
        ],
        compiler_params=pltpu.CompilerParams(
            vmem_limit_bytes=VMEM_LIMIT, dimension_semantics=("arbitrary", "arbitrary")
        ),
        name="local_pass",
    )(
        meta, conv, conv, conv, halo, halo, halo, conv_weight, conv_weight, conv_weight,
        conv_bias, conv_bias, conv_bias, dt, dtt, a, at, dx,
    )


def exchange_kernel(
    n,
    st_ref,
    aux_ref,
    ent_ref,
    fin_ref,
    rs,
    ra,
    eb,
    send1,
    recv1,
    send2,
    recv2,
    send3,
    recv3,
):
    me = lax.axis_index("seq")
    width = D // n
    barrier = pltpu.get_barrier_semaphore()

    def peer(i):
        return lax.rem(me + i, n)

    def cols(p):
        return pl.ds(pl.multiple_of(p * width, width), width)

    def greet(i, _):
        pl.semaphore_signal(barrier, inc=1, device_id={"seq": peer(i)}, device_id_type=MESH)
        return 0

    lax.fori_loop(1, n, greet, 0)
    pl.semaphore_wait(barrier, n - 1)

    def out(p, slot):
        return (
            pltpu.make_async_remote_copy(
                src_ref=st_ref.at[:, cols(p)],
                dst_ref=rs.at[slot],
                send_sem=send1.at[p],
                recv_sem=recv1.at[slot],
                device_id={"seq": p},
                device_id_type=MESH,
            ),
            pltpu.make_async_remote_copy(
                src_ref=aux_ref.at[:, cols(p)],
                dst_ref=ra.at[slot],
                send_sem=send2.at[p],
                recv_sem=recv2.at[slot],
                device_id={"seq": p},
                device_id_type=MESH,
            ),
        )

    def back(p, slot):
        return pltpu.make_async_remote_copy(
            src_ref=eb.at[p],
            dst_ref=ent_ref.at[:, cols(slot)],
            send_sem=send3.at[p],
            recv_sem=recv3.at[slot],
            device_id={"seq": p},
            device_id_type=MESH,
        )

    def begin(i, _):
        for copy in out(peer(i), me):
            copy.start()
        return 0

    lax.fori_loop(1, n, begin, 0)
    rs[me] = st_ref[:, cols(me)]
    ra[me] = aux_ref[:, cols(me)]

    def arrive(i, _):
        for copy in out(peer(i), peer(i)):
            copy.wait_recv()
        return 0

    lax.fori_loop(1, n, arrive, 0)

    fin_ref[...] = jnp.zeros_like(fin_ref)

    def scan(d, _):
        now = fin_ref[SEQS - 1]
        eb[d] = now.astype(BF16)
        for r in range(SEQS - 1):
            fin_ref[r] = fin_ref[r] + ra[d, 1 + r : 2 + r, :] * now
        fin_ref[SEQS - 1] = ra[d, 0:1, :] * now + rs[d].astype(F32)
        return 0

    lax.fori_loop(0, n, scan, 0)

    def reply(i, _):
        back(peer(i), me).start()
        return 0

    lax.fori_loop(1, n, reply, 0)
    ent_ref[:, cols(me)] = eb[me]

    def done(i, _):
        back(peer(i), peer(i)).wait_recv()
        return 0

    lax.fori_loop(1, n, done, 0)

    def drain(i, _):
        for copy in out(peer(i), me):
            copy.wait_send()
        back(peer(i), me).wait_send()
        return 0

    lax.fori_loop(1, n, drain, 0)


def exchange(states, aux, n):
    width = D // n
    vmem = pl.BlockSpec(memory_space=pltpu.VMEM)
    return pl.pallas_call(
        functools.partial(exchange_kernel, n),
        in_specs=[vmem, vmem],
        out_specs=[vmem, vmem],
        out_shape=[
            jax.ShapeDtypeStruct((STATE, D), BF16),
            jax.ShapeDtypeStruct((SEQS, STATE, width), F32),
        ],
        scratch_shapes=[
            pltpu.VMEM((n, STATE, width), BF16),
            pltpu.VMEM((n, 8, width), F32),
            pltpu.VMEM((n, STATE, width), BF16),
        ]
        + [pltpu.SemaphoreType.DMA((n,)) for _ in range(6)],
        compiler_params=pltpu.CompilerParams(
            collective_id=0, has_side_effects=True, vmem_limit_bytes=VMEM_LIMIT
        ),
        name="exchange",
    )(states, aux)


def finish_kernel(y_ref, c_ref, e_ref, ld_ref, gate_ref, nw_ref, out_ref, sp):
    @pl.when((pl.program_id(0) == 0) & (pl.program_id(1) == 0))
    def _():
        sp[...] = spread_matrix()

    v = y_ref[...] + spread(ld_ref[0, 0], sp) * dot(c_ref[...], e_ref[...])
    v = v * silu(gate_ref[...].astype(F32))
    scale = lax.rsqrt(jnp.mean(v * v, axis=1, keepdims=True) + TINY_FLOOR)
    out_ref[...] = (v * scale * nw_ref[...]).astype(BF16)


def finish(y, c, entering, lead, gate, norm_weight):
    length = y.shape[0]
    block = lambda width: pl.BlockSpec((BLOCK, width), lambda g, j: (j, g))
    return pl.pallas_call(
        finish_kernel,
        grid=(GROUPS, length // BLOCK),
        in_specs=[
            block(GW),
            block(STATE),
            pl.BlockSpec((STATE, GW), lambda g, j: (0, g)),
            pl.BlockSpec((1, 1, BLOCK, 128), lambda g, j: (g, j, 0, 0)),
            block(GW),
            pl.BlockSpec((1, GW), lambda g, j: (0, g)),
        ],
        out_specs=block(GW),
        out_shape=jax.ShapeDtypeStruct((length, D), BF16),
        scratch_shapes=[pltpu.VMEM((128, GW), BF16)],
        compiler_params=pltpu.CompilerParams(
            vmem_limit_bytes=VMEM_LIMIT, dimension_semantics=("arbitrary", "arbitrary")
        ),
        name="finish",
    )(y, c, entering, lead, gate, norm_weight)


def tail_kernel(
    n,
    m,
    rows_ref,
    w_ref,
    tails_ref,
    reach_ref,
    resid_ref,
    gain_ref,
    vocab_ref,
    hid_ref,
    max_ref,
    fin_ref,
    vbuf,
    rrecv,
    ragg,
    wbuf,
    part,
    precv,
    h1,
    h2,
    hf,
    mx1,
    mx2,
    p1,
    p2,
    p3,
    p4,
    vsem,
    rs_s,
    rs_r,
    ag_s,
    ag_r,
    w_s,
    w_r,
    pt_s,
    pt_r,
    h1_s,
    h1_r,
    h2_s,
    h2_r,
    m1_s,
    m1_r,
    m2_s,
    m2_r,
    p1_s,
    p1_r,
    p2_s,
    p2_r,
    p3_s,
    p3_r,
    p4_s,
    p4_r,
):
    s = lax.axis_index("seq")
    b = lax.axis_index("req")
    width = D // n
    depth = D // m
    w_place = 2 * b + s // 8
    w_slot = lax.rem(s, 8)
    to_self = w_place == s
    from_b = s // 2
    from_s = 8 * lax.rem(s, 2)

    load = pltpu.make_async_copy(vocab_ref, vbuf, vsem)
    load.start()

    barrier = pltpu.get_barrier_semaphore()

    def signal(where):
        pl.semaphore_signal(barrier, inc=1, device_id=where, device_id_type=MESH)

    def seq_peer(i):
        return lax.rem(s + i, n)

    def req_peer(i):
        return lax.rem(b + i, m)

    def greet_seq(i, _):
        signal({"seq": seq_peer(i)})
        return 0

    def greet_req(i, _):
        signal({"req": req_peer(i)})
        return 0

    def greet_w(i, _):
        @pl.when(jnp.logical_not(to_self & (i == b)))
        def _():
            signal({"req": i, "seq": w_place})

        @pl.when(jnp.logical_not((from_b == b) & (from_s + i == s)))
        def _():
            signal({"req": from_b, "seq": from_s + i})

        return 0

    lax.fori_loop(1, n, greet_seq, 0)
    lax.fori_loop(1, m, greet_req, 0)
    lax.fori_loop(0, m, greet_w, 0)
    pl.semaphore_wait(barrier, (n - 1) + (m - 1) + 2 * m - 2 * to_self.astype(jnp.int32))

    def remote(src, dst, send, recv, where):
        return pltpu.make_async_remote_copy(
            src_ref=src, dst_ref=dst, send_sem=send, recv_sem=recv, device_id=where, device_id_type=MESH
        )

    def over(count, peer, copy, me):
        def start(i, _):
            copy(peer(i), me).start()
            return 0

        def arrive(i, _):
            copy(peer(i), peer(i)).wait_recv()
            return 0

        def drain(i, _):
            copy(peer(i), me).wait_send()
            return 0

        return (
            lambda: lax.fori_loop(1, count, start, 0),
            lambda: lax.fori_loop(1, count, arrive, 0),
            lambda: lax.fori_loop(1, count, drain, 0),
        )

    def rows_copy(p, slot):
        return remote(rows_ref.at[p], rrecv.at[slot], rs_s.at[p], rs_r.at[slot], {"seq": p})

    def gather_copy(p, slot):
        return remote(ragg.at[b], ragg.at[slot], ag_s.at[p], ag_r.at[slot], {"req": p})

    def part_copy(p, slot):
        cols = pl.ds(pl.multiple_of(lax.rem(p, 2) * 256, 256), 256)
        return remote(part.at[p // 2, :, cols], precv.at[slot], pt_s.at[p], pt_r.at[slot], {"seq": p})

    def h1_copy(p, slot):
        return remote(h1.at[b], h1.at[slot], h1_s.at[p], h1_r.at[slot], {"req": p})

    def h2_copy(p, slot):
        return remote(h1, h2.at[slot // 2, lax.rem(slot, 2)], h2_s.at[p], h2_r.at[slot], {"seq": p})

    def m1_copy(p, slot):
        return remote(mx1.at[b], mx1.at[slot], m1_s.at[p], m1_r.at[slot], {"req": p})

    def m2_copy(p, slot):
        return remote(mx2.at[s], mx2.at[slot], m2_s.at[p], m2_r.at[slot], {"seq": p})

    sy, sz = s // 4, lax.rem(s, 4)

    def even(c):
        return c + 1 - 2 * lax.rem(c, 2)

    def odd(c):
        return 3 - c

    orders = []
    for v in range(4):
        first_is_z = v % 2 == 0
        near, far = (even, odd) if v < 2 else (odd, even)
        c, e = (sz, sy) if first_is_z else (sy, sz)
        orders.append((first_is_z, near, far, c, e))

    def spot_of(v, c, e):
        return e * 4 + c if orders[v][0] else c * 4 + e

    def block(v, c, e):
        cols = pl.ds(pl.multiple_of(spot_of(v, c, e) * width, width), width)
        return (slice(None), pl.ds(32 * v, 32), cols)

    def stage1(v, i, q):
        _, near, far, c, _ = orders[v]
        p = near(c)
        src = tails_ref.at[block(v, p if i == 0 else far(p), q)]
        _, _, _, _, e = orders[v]
        return remote(src, p1.at[v, i, q], p1_s.at[v, i, q], p1_r.at[v, i, q], {"seq": spot_of(v, p, e)})

    def stage2(v, q):
        _, _, far, c, e = orders[v]
        return remote(
            p1.at[v, 1, q], p2.at[v, q], p2_s.at[v, q], p2_r.at[v, q], {"seq": spot_of(v, far(c), e)}
        )

    def stage3(v, i):
        _, near, far, c, e = orders[v]
        p = near(e)
        src = p2.at[v, p if i == 0 else far(p)]
        return remote(src, p3.at[v, i], p3_s.at[v, i], p3_r.at[v, i], {"seq": spot_of(v, c, p)})

    def stage4(v):
        _, _, far, c, e = orders[v]
        return remote(p3.at[v, 1], p4.at[v], p4_s.at[v], p4_r.at[v], {"seq": spot_of(v, c, far(e))})

    def each(act, one):
        for v in range(4):
            for i in range(2):
                if act == 1:

                    def step(q, _):
                        one(stage1(v, i, q))
                        return 0

                    lax.fori_loop(0, 4, step, 0)
                elif act == 2 and i == 0:

                    def step(q, _):
                        one(stage2(v, q))
                        return 0

                    lax.fori_loop(0, 4, step, 0)
                elif act == 3:
                    one(stage3(v, i))
                elif act == 4 and i == 0:
                    one(stage4(v))

    go = lambda copy: copy.start()
    got = lambda copy: copy.wait_recv()
    sent = lambda copy: copy.wait_send()

    def add1():
        for v in range(4):
            _, _, far, c, _ = orders[v]
            for i in range(2):

                def step(q, _):
                    p1[v, i, q] = p1[v, i, q] + tails_ref[block(v, c if i == 0 else far(c), q)]
                    return 0

                lax.fori_loop(0, 4, step, 0)

    def add2():
        for v in range(4):
            p2[v] = p2[v] + p1[v, 0]

    def add3():
        for v in range(4):
            _, _, far, _, e = orders[v]
            p3[v, 0] = p3[v, 0] + p2[v, e]
            p3[v, 1] = p3[v, 1] + p2[v, far(e)]

    rows_go, rows_in, rows_out = over(n, seq_peer, rows_copy, s)
    ag_go, ag_in, ag_out = over(m, req_peer, gather_copy, b)
    part_go, part_in, part_out = over(n, seq_peer, part_copy, s)
    h1_go, h1_in, h1_out = over(m, req_peer, h1_copy, b)
    h2_go, h2_in, h2_out = over(n, seq_peer, h2_copy, s)
    m1_go, m1_in, m1_out = over(m, req_peer, m1_copy, b)
    m2_go, m2_in, m2_out = over(n, seq_peer, m2_copy, s)

    rows_go()

    def w_copy(p):
        cols = pl.ds(pl.multiple_of(p * depth, depth), depth)
        return remote(
            w_ref.at[:, cols], wbuf.at[w_slot], w_s.at[p], w_r.at[w_slot], {"req": p, "seq": w_place}
        )

    def w_start(i, _):
        p = lax.rem(b + i, m)

        @pl.when(jnp.logical_not(to_self & (p == b)))
        def _():
            w_copy(p).start()

        return 0

    lax.fori_loop(0, m, w_start, 0)

    @pl.when(to_self)
    def _():
        wbuf[w_slot] = w_ref[:, pl.ds(pl.multiple_of(b * depth, depth), depth)]

    rrecv[s] = rows_ref[s]
    each(1, go)
    rows_in()
    ragg[b] = jnp.sum(rrecv[...], axis=0)
    ag_go()
    ag_in()

    def w_arrive(i, _):
        @pl.when(jnp.logical_not((from_b == b) & (from_s + i == s)))
        def _():
            remote(
                w_ref.at[:, pl.ds(0, depth)], wbuf.at[i], w_s.at[i], w_r.at[i], {"req": i, "seq": w_place}
            ).wait_recv()

        return 0

    lax.fori_loop(0, m, w_arrive, 0)

    lhs = ragg[...].reshape(8 * m, 128).astype(BF16)
    weights = wbuf[...].reshape(m * 32, depth)
    place = lax.broadcasted_iota(jnp.int32, (8 * m, depth), 0)
    both = jnp.where(place % 8 < 4, dot(lhs, weights[0:128]), dot(lhs, weights[128:256]))
    both = both + pltpu.roll(both, 4, 0)
    part[...] = both.reshape(m, 8, depth)
    part_go()
    precv[s] = part[s // 2, :, pl.ds(pl.multiple_of(lax.rem(s, 2) * 256, 256), 256)]
    each(1, got)
    add1()
    each(2, go)
    part_in()
    hidden = jnp.sum(precv[...], axis=0) + resid_ref[...].astype(F32)
    upper = pltpu.roll(hidden[:, 128:256], 4, 0)
    eight = lax.broadcasted_iota(jnp.int32, (8, 128), 0)
    h1[b] = jnp.where(eight < 4, upper, hidden[:, 0:128]).astype(BF16)
    h1_go()
    h1_in()
    h2_go()
    h2[s // 2, lax.rem(s, 2)] = h1[...]
    each(2, got)
    add2()
    each(3, go)
    h2_in()

    for k in range(m):
        for q in range(2):
            piece = h2[:, q, k].astype(F32).reshape(8 * m, 128)
            lo = k * depth + q * 256
            hf[:, lo : lo + 128] = piece
            hf[:, lo + 128 : lo + 256] = pltpu.roll(piece, 4, 0)
    h = hf[...]
    hid_ref[...] = hf[pl.ds(pl.multiple_of(b * 8, 8), 8), :].astype(BF16)
    scale = lax.rsqrt(jnp.mean(h * h, axis=1, keepdims=True) + TINY_FLOOR)
    normed = (h * scale * gain_ref[...]).astype(BF16)
    load.wait()
    top = jnp.full((1, 8 * m), -jnp.inf, F32)
    chunk = 256
    for k in range(vbuf.shape[0] // chunk):
        logits = dot_nt(vbuf[k * chunk : (k + 1) * chunk, :], normed)
        top = jnp.maximum(top, jnp.max(logits, axis=0, keepdims=True))
    top = jnp.concatenate([top, top], axis=1)
    mx1[b] = jnp.broadcast_to(top, (8, 128))
    m1_go()
    each(3, got)
    add3()
    each(4, go)
    m1_in()
    mx2[s] = jnp.max(mx1[...], axis=0)
    m2_go()

    each(4, got)
    for v in range(4):
        p4[v] = p4[v] + p3[v, 0]
    for r in range(SEQS - 1):
        share = jnp.concatenate([p4[v, r].astype(F32) for v in range(4)], axis=0)
        fin_ref[r] = (reach_ref[r] + share).T
    fin_ref[SEQS - 1] = reach_ref[SEQS - 1].T
    m2_in()
    max_ref[...] = jnp.max(mx2[...], axis=0)

    for drain in (rows_out, ag_out, part_out, h1_out, h2_out, m1_out, m2_out):
        drain()

    def w_drain(p, _):
        @pl.when(jnp.logical_not(to_self & (p == b)))
        def _():
            w_copy(p).wait_send()

        return 0

    lax.fori_loop(0, m, w_drain, 0)

    for act in range(1, 5):
        each(act, sent)


def tail(rows, out_weight, tails, reached, resid, gain, vocab, n, m):
    width = D // n
    vmem = pl.BlockSpec(memory_space=pltpu.VMEM)
    dma = pltpu.SemaphoreType.DMA
    return pl.pallas_call(
        functools.partial(tail_kernel, n, m),
        in_specs=[vmem] * 6 + [pl.BlockSpec(memory_space=pl.ANY)],
        out_specs=[vmem] * 3,
        out_shape=[
            jax.ShapeDtypeStruct((8, D), BF16),
            jax.ShapeDtypeStruct((8, 128), F32),
            jax.ShapeDtypeStruct((SEQS, width, STATE), F32),
        ],
        scratch_shapes=[
            pltpu.VMEM(vocab.shape, BF16),
            pltpu.VMEM((n, 8, 128), F32),
            pltpu.VMEM((m, 8, 128), F32),
            pltpu.VMEM((m, 32, D // m), BF16),
            pltpu.VMEM((m, 8, D // m), F32),
            pltpu.VMEM((n, 8, 256), F32),
            pltpu.VMEM((m, 8, 128), BF16),
            pltpu.VMEM((n // 2, 2, m, 8, 128), BF16),
            pltpu.VMEM((8 * m, D), F32),
            pltpu.VMEM((m, 8, 128), F32),
            pltpu.VMEM((n, 8, 128), F32),
            pltpu.VMEM((4, 2, 4, SEQS - 1, 32, width), BF16),
            pltpu.VMEM((4, 4, SEQS - 1, 32, width), BF16),
            pltpu.VMEM((4, 2, SEQS - 1, 32, width), BF16),
            pltpu.VMEM((4, SEQS - 1, 32, width), BF16),
            dma,
            dma((n,)),
            dma((n,)),
            dma((m,)),
            dma((m,)),
            dma((m,)),
            dma((m,)),
            dma((n,)),
            dma((n,)),
            dma((m,)),
            dma((m,)),
            dma((n,)),
            dma((n,)),
            dma((m,)),
            dma((m,)),
            dma((n,)),
            dma((n,)),
            dma((4, 2, 4)),
            dma((4, 2, 4)),
            dma((4, 4)),
            dma((4, 4)),
            dma((4, 2)),
            dma((4, 2)),
            dma((4,)),
            dma((4,)),
        ],
        compiler_params=pltpu.CompilerParams(
            collective_id=1, has_side_effects=True, vmem_limit_bytes=VMEM_LIMIT
        ),
        name="tail",
    )(rows, out_weight, tails, reached, resid, gain, vocab)


def body(
    conv_input,
    gate_projected,
    step_raw,
    step_bias,
    decay_log,
    head_direct_gain,
    conv_weight,
    convolution_bias,
    norm_weight,
    lengths,
    out_weight,
    residual_last,
    final_gain,
    vocab_weight,
):
    local_len = conv_input.shape[1]
    inner = HEADS * CHANNEL_WIDTH
    count = local_len // BLOCK
    seq_count = lax.axis_size("seq")
    seq_place = lax.axis_index("seq")
    req_place = lax.axis_index("req")
    first = seq_place * local_len
    conv = conv_input[0]
    route = [(i, i + 1) for i in range(seq_count - 1)]
    halo = lax.ppermute(conv[local_len - 8 :], "seq", route)
    bounds = jnp.cumsum(lengths[0]).astype(jnp.int32)
    meta = jnp.concatenate([first.astype(jnp.int32)[None], bounds])

    step = jax.nn.softplus(step_raw[0] + step_bias)
    step = step.reshape(count, BLOCK, GROUPS, PER_GROUP)
    dt = jnp.tile(step.transpose(2, 0, 1, 3), (1, 1, 1, 128 // PER_GROUP))
    dtt = step.transpose(2, 0, 3, 1)
    rate = (-jnp.exp(decay_log) * LOG2E).reshape(GROUPS, PER_GROUP)
    a = jnp.tile(rate, (1, 128 // PER_GROUP))[:, None, :]
    at = rate[:, :, None]
    dx = jnp.repeat(head_direct_gain, CHANNEL_WIDTH)[None]

    y, states, tails, aux, c, lead = local_pass(
        meta, conv, halo, conv_weight, convolution_bias[None], dt, dtt, a, at, dx
    )
    entering, reached = exchange(states, aux, seq_count)
    gated = finish(y, c, entering, lead, gate_projected[0], norm_weight[None])

    lasts = []
    for request in range(SEQS):
        local_end = bounds[request] - 1 - first
        owned = (local_end >= 0) & (local_end < local_len)
        spot = jnp.clip(local_end, 0, local_len - 1)
        lasts.append(jnp.where(owned, gated[spot].astype(jnp.float32), 0.0))
    last_local = jnp.stack(lasts)
    req_count = lax.axis_size("req")
    rows = last_local.reshape(SEQS, seq_count, 2, 128).transpose(1, 2, 0, 3).reshape(seq_count, 8, 128)
    resid = lax.dynamic_slice(
        residual_last,
        (seq_place // 2, 0, req_place * (D // req_count) + (seq_place % 2) * 256),
        (1, SEQS, 256),
    )[0]
    resid = jnp.concatenate([jnp.zeros_like(resid), resid], axis=0)
    hid, top, final = tail(
        rows, out_weight, tails, reached, resid, final_gain[None], vocab_weight, seq_count, req_count
    )
    own_hidden = hid[None, SEQS:]
    max_logit = lax.dynamic_slice(top, (0, req_place * 8 + SEQS), (1, SEQS))
    final_states = final.reshape(SEQS, HEADS // seq_count, CHANNEL_WIDTH, STATE)[None]
    return (gated[None], final_states, own_hidden, max_logit)


def solution(mesh):
    return jax.shard_map(
        body,
        mesh=mesh,
        in_specs=(
            P("req", "seq", None),
            P("req", "seq", None),
            P("req", "seq", None),
            P(),
            P(),
            P(),
            P(),
            P(),
            P(),
            P("req", None),
            P(("req", "seq"), None),
            P(),
            P(),
            P(("req", "seq"), None),
        ),
        out_specs=(
            P("req", "seq", None),
            P("req", None, "seq", None, None),
            P("req", None, None),
            P("req", None),
        ),
        check_vma=False,
    )
```

```python
import functools

import jax
import jax.numpy as jnp
from jax import lax
from jax.experimental import pallas as pl
from jax.experimental.pallas import tpu as pltpu
from jax.sharding import PartitionSpec as P

D = 4096
HEADS = 64
CHANNEL_WIDTH = 64
GROUPS = 4
STATE = 128
KERNEL = 4
BLOCK = 256
SEQS = 4
PER_GROUP = HEADS // GROUPS
GW = PER_GROUP * CHANNEL_WIDTH
TINY_FLOOR = 1e-05
LOG2E = 1.4426950408889634
MESH = pl.DeviceIdType.MESH
F32 = jnp.float32
BF16 = jnp.bfloat16
VMEM_LIMIT = 60 * 1024 * 1024


def dot(a, b):
    return lax.dot_general(a, b, (((1,), (0,)), ((), ())), preferred_element_type=F32)


def dot_nt(a, b):
    return lax.dot_general(a, b, (((1,), (1,)), ((), ())), preferred_element_type=F32)


def split2(x):
    hi = x.astype(BF16)
    return hi, (x - hi.astype(F32)).astype(BF16)


def split3(x):
    hi = x.astype(BF16)
    rest = x - hi.astype(F32)
    mid = rest.astype(BF16)
    return hi, mid, (rest - mid.astype(F32)).astype(BF16)


def seg_of(place, b1, b2, b3):
    one = lambda b: (place >= b).astype(jnp.int32)
    return one(b1) + one(b2) + one(b3)


def spread_matrix():
    lane = lax.broadcasted_iota(jnp.int32, (128, GW), 0)
    col = lax.broadcasted_iota(jnp.int32, (128, GW), 1)
    hit = (lane < 48) & (lane % PER_GROUP == col // CHANNEL_WIDTH)
    return jnp.where(hit, 1.0, 0.0).astype(BF16)


def spread(v, spread_ref):
    hi, mid, lo = split3(v)
    lane = lax.broadcasted_iota(jnp.int32, v.shape, 1)
    parts = jnp.where(
        lane < 16, hi.astype(F32), jnp.where(lane < 32, mid.astype(F32), lo.astype(F32))
    ).astype(BF16)
    return dot(parts, spread_ref[...])


def halves(h):
    return h + h * jnp.tanh(h)


def softplus(x):
    e = jnp.exp(-jnp.abs(x))
    w = 1.0 + e
    d = w - 1.0
    return jnp.maximum(x, 0.0) + jnp.where(d == 0.0, e, jnp.log(w) * (e / jnp.where(d == 0.0, 1.0, d)))


def bounds_of(len_ref):
    b1 = len_ref[0, 0]
    b2 = b1 + len_ref[0, 1]
    return b1, b2, b2 + len_ref[0, 2]


def local_kernel(
    len_ref,
    x_ref,
    b_ref,
    c_ref,
    xh_ref,
    bh_ref,
    ch_ref,
    wx_ref,
    wb_ref,
    wc_ref,
    vx_ref,
    vb_ref,
    vc_ref,
    raw_ref,
    bias_ref,
    log_ref,
    gain_ref,
    y_ref,
    st_ref,
    pt_ref,
    aux_ref,
    co_ref,
    ld_ref,
    xext,
    xf,
    s0,
    c0,
    cumr,
    sp,
    msk,
    alw,
    sgs,
    cums,
    lds,
    dxs,
    wst,
):
    g = pl.program_id(0)
    j = pl.program_id(1)
    span = pl.num_programs(1) * BLOCK
    first = lax.axis_index("seq") * span
    b1, b2, b3 = bounds_of(len_ref)
    bounds = (b1, b2, b3)
    start = first + j * BLOCK

    @pl.when((g == 0) & (j == 0))
    def _():
        sp[...] = spread_matrix()

    row = lax.broadcasted_iota(jnp.int32, (BLOCK, 128), 0) + start

    @pl.when(g == 0)
    def _():
        near = jnp.full((BLOCK, 128), 8, jnp.int32)
        for bound in bounds:
            gap = row - bound
            near = jnp.where(gap >= 0, jnp.minimum(near, gap), near)
        for k in range(3):
            msk[j, k] = (near >= 3 - k).astype(F32)
        sgs[j] = seg_of(row, b1, b2, b3)
        i0 = lax.broadcasted_iota(jnp.int32, (BLOCK, BLOCK), 0)
        i1 = lax.broadcasted_iota(jnp.int32, (BLOCK, BLOCK), 1)
        t_seg = seg_of(i0 + start, b1, b2, b3)
        s_seg = seg_of(i1 + start, b1, b2, b3)
        alw[j] = ((i0 >= i1) & (t_seg == s_seg)).astype(F32)
        tri = jnp.where(i0 >= i1, 1.0, 0.0).astype(BF16)
        dt = softplus(raw_ref[...] + bias_ref[...])
        dh, dm, dl = split3(dt * (jnp.exp(log_ref[...]) * -LOG2E))
        cums[j] = (dot(tri, dl) + dot(tri, dm)) + dot(tri, dh)
        lds[j] = jnp.log(dt) * LOG2E

    l0 = lax.broadcasted_iota(jnp.int32, (HEADS, 128), 0)
    l1 = lax.broadcasted_iota(jnp.int32, (HEADS, 128), 1)
    pick = jnp.where(l0 == g * PER_GROUP + l1 % PER_GROUP, 1.0, 0.0).astype(BF16)
    t0 = lax.broadcasted_iota(jnp.int32, (PER_GROUP, HEADS), 0)
    t1 = lax.broadcasted_iota(jnp.int32, (PER_GROUP, HEADS), 1)
    pickt = jnp.where(t1 == g * PER_GROUP + t0, 1.0, 0.0).astype(BF16)

    def group(v):
        hi, mid, lo = split3(v)
        return (dot(lo, pick) + dot(mid, pick)) + dot(hi, pick)

    @pl.when(j == 0)
    def _():
        xext[0:8, 0:GW] = xh_ref[...].astype(F32)
        xext[0:8, GW : GW + 128] = bh_ref[...].astype(F32)
        xext[0:8, GW + 128 : GW + 256] = ch_ref[...].astype(F32)
        for lo, hi, w_ref, v_ref in (
            (0, GW, wx_ref, vx_ref),
            (GW, GW + 128, wb_ref, vb_ref),
            (GW + 128, GW + 256, wc_ref, vc_ref),
        ):
            wst[0:KERNEL, lo:hi] = w_ref[...] * 0.5
            wst[KERNEL : KERNEL + 1, lo:hi] = v_ref[...] * 0.5
        pt_ref[...] = jnp.zeros_like(pt_ref)
        aux_ref[...] = jnp.zeros_like(aux_ref)
        c0[...] = jnp.zeros_like(c0)
        dxs[...] = spread(group(jnp.broadcast_to(gain_ref[...], (8, HEADS))), sp)

    @pl.when(j == 1)
    def _():
        xext[0:8, :] = xext[BLOCK : BLOCK + 8, :]

    xext[8 : BLOCK + 8, 0:GW] = x_ref[...].astype(F32)
    xext[8 : BLOCK + 8, GW : GW + 128] = b_ref[...].astype(F32)
    xext[8 : BLOCK + 8, GW + 128 : GW + 256] = c_ref[...].astype(F32)

    tile = 64

    def convolve(c, _):
        cols = pl.ds(pl.multiple_of(c * 128, 128), 128)
        w = [wst[k : k + 1, cols] for k in range(KERNEL)]
        bias = wst[KERNEL : KERNEL + 1, cols]
        for lo in range(0, BLOCK, tile):
            total = jnp.broadcast_to(bias, (tile, 128))
            for k in range(3):
                total = total + w[k] * xext[lo + 5 + k : lo + 5 + k + tile, cols] * msk[j, k, lo : lo + tile]
            total = total + w[3] * xext[lo + 8 : lo + 8 + tile, cols]
            xf[lo : lo + tile, cols] = halves(total)
        return 0

    lax.fori_loop(0, 10, convolve, 0)

    seg = sgs[j]
    bf = xf[:, GW : GW + 128]
    cb = xf[:, GW + 128 : GW + 256].astype(BF16)
    co_ref[...] = cb

    cum = group(cums[j])
    logdt = group(lds[j])
    rh, rm, rl = split3(lds[j] - cums[j])
    rt = (dot_nt(pickt, rl) + dot_nt(pickt, rm)) + dot_nt(pickt, rh)
    cumr[...] = cum
    last = cum[BLOCK - 1 : BLOCK, :]

    seg_before_span = seg_of(first - 1, b1, b2, b3)
    seg_before = seg_of(start - 1, b1, b2, b3)
    seg_end = seg_of(start + BLOCK - 1, b1, b2, b3)
    prior = c0[0:1, :]
    ld_ref[0, 0] = jnp.where(seg == seg_before_span, jnp.exp2(cum + prior), 0.0)

    bh, bl = split2(bf)
    sc = dot_nt(cb, bh) * alw[j]

    @pl.when(j == 0)
    def _():
        y_ref[...] = jnp.zeros_like(y_ref)

    @pl.when(j == 1)
    def _():
        lead = jnp.where(seg == seg_before, jnp.exp2(cum), 0.0)
        sh, sl = split2(s0[...])
        y_ref[...] = spread(lead, sp) * (dot(cb, sh) + dot(cb, sl))

    lane = lax.broadcasted_iota(jnp.int32, (BLOCK, 128), 1)
    half = BLOCK // 2
    sc_t = sc[:half, :half]
    sc_l = sc[half:, :half]
    sc_r = sc[half:, half:]
    for pair in range(PER_GROUP // 2):
        cols = slice(pair * 128, pair * 128 + 128)
        xb = xf[:, cols].astype(BF16)
        res = []
        for h in (2 * pair, 2 * pair + 1):
            col = cum[:, h : h + 1]
            r = rt[h : h + 1, :]
            top = jnp.exp2(jnp.minimum(col[:half] + r[:, :half], 100.0)) * sc_t
            left = jnp.exp2(col[half:] + r[:, :half]) * sc_l
            right = jnp.exp2(jnp.minimum(col[half:] + r[:, half:], 100.0)) * sc_r
            bottom = jnp.concatenate([left.astype(BF16), right.astype(BF16)], axis=1)
            res.append(
                jnp.concatenate([dot(top.astype(BF16), xb[:half]), dot(bottom, xb)], axis=0)
            )
        intra = jnp.where(lane < CHANNEL_WIDTH, res[0], res[1])
        y_ref[:, cols] = y_ref[:, cols] + (intra + dxs[0:1, cols] * xb.astype(F32))

    bht, blt = split2(bf.T)

    def state_of(weights):
        xs = xf[:, 0:GW] * spread(weights, sp)
        xs_h, xs_l = split2(xs)
        return dot(bht, xs_h) + (dot(blt, xs_h) + dot(bht, xs_l))

    def at_end(seg_e):
        return jnp.where(seg == seg_e, jnp.exp2(last - cum + logdt), 0.0)

    own = state_of(at_end(seg_end))

    for r in range(SEQS - 1):
        end = bounds[r] - 1
        local = end - start
        owned = (local >= 0) & (local < BLOCK)

        @pl.when(owned)
        def _():
            ce = cumr[pl.ds(jnp.clip(local, 0, BLOCK - 1), 1), :]
            inside = (row <= end) & (seg == r)
            w = jnp.exp2(jnp.where(inside, ce - cum + logdt, -1e30))
            reach = jnp.where(seg_before == r, jnp.exp2(ce), 0.0)
            tail = state_of(w)
            keep = jnp.where(j == 1, 1.0, 0.0)
            reach8 = spread(jnp.broadcast_to(reach * keep, (8, 128)), sp)
            tail = tail + jnp.where(j == 1, reach8[0:1] * s0[...], 0.0)
            pt_ref[r] = tail.astype(BF16)
            full = jnp.where(seg_before_span == r, jnp.exp2(ce + prior), 0.0)
            aux_ref[1 + r : 2 + r, :] = spread(jnp.broadcast_to(full, (8, 128)), sp)[0:1]

    @pl.when(j == 0)
    def _():
        s0[...] = own
        c0[...] = jnp.broadcast_to(last, c0.shape)

    @pl.when(j == 1)
    def _():
        carry = jnp.where(seg_end == seg_before, jnp.exp2(last), 0.0)
        whole = jnp.where(seg_end == seg_before_span, jnp.exp2(last + prior), 0.0)
        carry8 = spread(jnp.broadcast_to(carry, (8, 128)), sp)
        whole8 = spread(jnp.broadcast_to(whole, (8, 128)), sp)
        st_ref[...] = (carry8[0:1] * s0[...] + own).astype(BF16)
        aux_ref[0:1, :] = whole8[0:1]


def local_pass(lengths, conv, halo, conv_weight, conv_bias, raw, bias, log, gain):
    length = conv.shape[0]
    blocks = length // BLOCK
    maps = D // 128
    grid = (GROUPS, blocks)
    xs = lambda rows: [
        pl.BlockSpec((rows, GW), lambda g, j: (0, g)),
        pl.BlockSpec((rows, 128), lambda g, j: (0, maps + g)),
        pl.BlockSpec((rows, 128), lambda g, j: (0, maps + GROUPS + g)),
    ]
    in_specs = (
        [
            pl.BlockSpec(memory_space=pltpu.SMEM),
            pl.BlockSpec((BLOCK, GW), lambda g, j: (j, g)),
            pl.BlockSpec((BLOCK, 128), lambda g, j: (j, maps + g)),
            pl.BlockSpec((BLOCK, 128), lambda g, j: (j, maps + GROUPS + g)),
        ]
        + xs(8)
        + xs(KERNEL)
        + xs(1)
        + [
            pl.BlockSpec((BLOCK, HEADS), lambda g, j: (j, 0)),
            pl.BlockSpec((1, HEADS), lambda g, j: (0, 0)),
            pl.BlockSpec((1, HEADS), lambda g, j: (0, 0)),
            pl.BlockSpec((1, HEADS), lambda g, j: (0, 0)),
        ]
    )
    out_specs = [
        pl.BlockSpec((BLOCK, GW), lambda g, j: (j, g)),
        pl.BlockSpec((STATE, GW), lambda g, j: (0, g)),
        pl.BlockSpec((SEQS - 1, STATE, GW), lambda g, j: (0, 0, g)),
        pl.BlockSpec((8, GW), lambda g, j: (0, g)),
        pl.BlockSpec((BLOCK, 128), lambda g, j: (j, g)),
        pl.BlockSpec((1, 1, BLOCK, 128), lambda g, j: (g, j, 0, 0)),
    ]
    out_shape = [
        jax.ShapeDtypeStruct((length, D), F32),
        jax.ShapeDtypeStruct((STATE, D), BF16),
        jax.ShapeDtypeStruct((SEQS - 1, STATE, D), BF16),
        jax.ShapeDtypeStruct((8, D), F32),
        jax.ShapeDtypeStruct((length, GROUPS * STATE), BF16),
        jax.ShapeDtypeStruct((GROUPS, blocks, BLOCK, 128), F32),
    ]
    return pl.pallas_call(
        local_kernel,
        grid=grid,
        in_specs=in_specs,
        out_specs=out_specs,
        out_shape=out_shape,
        scratch_shapes=[
            pltpu.VMEM((BLOCK + 8, GW + 256), F32),
            pltpu.VMEM((BLOCK, GW + 256), F32),
            pltpu.VMEM((STATE, GW), F32),
            pltpu.VMEM((8, 128), F32),
            pltpu.VMEM((BLOCK, 128), F32),
            pltpu.VMEM((128, GW), BF16),
            pltpu.VMEM((blocks, 3, BLOCK, 128), F32),
            pltpu.VMEM((blocks, BLOCK, BLOCK), F32),
            pltpu.VMEM((blocks, BLOCK, 128), jnp.int32),
            pltpu.VMEM((blocks, BLOCK, HEADS), F32),
            pltpu.VMEM((blocks, BLOCK, HEADS), F32),
            pltpu.VMEM((8, GW), F32),
            pltpu.VMEM((8, GW + 256), F32),
        ],
        compiler_params=pltpu.CompilerParams(
            vmem_limit_bytes=VMEM_LIMIT, dimension_semantics=("arbitrary", "arbitrary")
        ),
        name="local_pass",
    )(
        lengths, conv, conv, conv, halo, halo, halo, conv_weight, conv_weight, conv_weight,
        conv_bias, conv_bias, conv_bias, raw, bias, log, gain,
    )


def exchange_kernel(
    n,
    st_ref,
    aux_ref,
    ent_ref,
    fin_ref,
    rs,
    ra,
    eb,
    send1,
    recv1,
    send2,
    recv2,
    send3,
    recv3,
):
    me = lax.axis_index("seq")
    width = D // n
    barrier = pltpu.get_barrier_semaphore()

    def peer(i):
        return lax.rem(me + i, n)

    def cols(p):
        return pl.ds(pl.multiple_of(p * width, width), width)

    def greet(i, _):
        pl.semaphore_signal(barrier, inc=1, device_id={"seq": peer(i)}, device_id_type=MESH)
        return 0

    lax.fori_loop(1, n, greet, 0)
    pl.semaphore_wait(barrier, n - 1)

    def out(p, slot):
        return (
            pltpu.make_async_remote_copy(
                src_ref=st_ref.at[:, cols(p)],
                dst_ref=rs.at[slot],
                send_sem=send1.at[p],
                recv_sem=recv1.at[slot],
                device_id={"seq": p},
                device_id_type=MESH,
            ),
            pltpu.make_async_remote_copy(
                src_ref=aux_ref.at[:, cols(p)],
                dst_ref=ra.at[slot],
                send_sem=send2.at[p],
                recv_sem=recv2.at[slot],
                device_id={"seq": p},
                device_id_type=MESH,
            ),
        )

    def back(p, slot):
        return pltpu.make_async_remote_copy(
            src_ref=eb.at[p],
            dst_ref=ent_ref.at[:, cols(slot)],
            send_sem=send3.at[p],
            recv_sem=recv3.at[slot],
            device_id={"seq": p},
            device_id_type=MESH,
        )

    def begin(i, _):
        for copy in out(peer(i), me):
            copy.start()
        return 0

    lax.fori_loop(1, n, begin, 0)
    rs[me] = st_ref[:, cols(me)]
    ra[me] = aux_ref[:, cols(me)]

    def arrive(i, _):
        for copy in out(peer(i), peer(i)):
            copy.wait_recv()
        return 0

    lax.fori_loop(1, n, arrive, 0)

    fin_ref[...] = jnp.zeros_like(fin_ref)

    def scan(d, _):
        now = fin_ref[SEQS - 1]
        eb[d] = now.astype(BF16)
        for r in range(SEQS - 1):
            fin_ref[r] = fin_ref[r] + ra[d, 1 + r : 2 + r, :] * now
        fin_ref[SEQS - 1] = ra[d, 0:1, :] * now + rs[d].astype(F32)
        return 0

    lax.fori_loop(0, n, scan, 0)

    def reply(i, _):
        back(peer(i), me).start()
        return 0

    lax.fori_loop(1, n, reply, 0)
    ent_ref[:, cols(me)] = eb[me]

    def done(i, _):
        back(peer(i), peer(i)).wait_recv()
        return 0

    lax.fori_loop(1, n, done, 0)

    def drain(i, _):
        for copy in out(peer(i), me):
            copy.wait_send()
        back(peer(i), me).wait_send()
        return 0

    lax.fori_loop(1, n, drain, 0)


def exchange(states, aux, n):
    width = D // n
    vmem = pl.BlockSpec(memory_space=pltpu.VMEM)
    return pl.pallas_call(
        functools.partial(exchange_kernel, n),
        in_specs=[vmem, vmem],
        out_specs=[vmem, vmem],
        out_shape=[
            jax.ShapeDtypeStruct((STATE, D), BF16),
            jax.ShapeDtypeStruct((SEQS, STATE, width), F32),
        ],
        scratch_shapes=[
            pltpu.VMEM((n, STATE, width), BF16),
            pltpu.VMEM((n, 8, width), F32),
            pltpu.VMEM((n, STATE, width), BF16),
        ]
        + [pltpu.SemaphoreType.DMA((n,)) for _ in range(6)],
        compiler_params=pltpu.CompilerParams(
            collective_id=0, has_side_effects=True, vmem_limit_bytes=VMEM_LIMIT
        ),
        name="exchange",
    )(states, aux)


def finish_kernel(len_ref, y_ref, c_ref, e_ref, ld_ref, gate_ref, nw_ref, out_ref, rows_ref, sp, of):
    g = pl.program_id(0)
    j = pl.program_id(1)

    @pl.when((g == 0) & (j == 0))
    def _():
        sp[...] = spread_matrix()

    @pl.when(j == 0)
    def _():
        rows_ref[...] = jnp.zeros_like(rows_ref)

    v = y_ref[...] + spread(ld_ref[0, 0], sp) * dot(c_ref[...], e_ref[...])
    v = v * halves(0.5 * gate_ref[...].astype(F32))
    scale = lax.rsqrt(jnp.mean(v * v, axis=1, keepdims=True) + TINY_FLOOR)
    out = (v * scale * nw_ref[...]).astype(BF16)
    out_ref[...] = out

    of[...] = out.astype(F32)
    start = lax.axis_index("seq") * (pl.num_programs(1) * BLOCK) + j * BLOCK
    bounds = bounds_of(len_ref)
    for r, bound in enumerate(bounds + (bounds[2] + len_ref[0, 3],)):
        local = bound - 1 - start

        @pl.when((local >= 0) & (local < BLOCK))
        def _():
            line = of[pl.ds(jnp.clip(local, 0, BLOCK - 1), 1), :]
            for c in range(GW // 128):
                place = c % 2 * SEQS + r
                rows_ref[c // 2, place : place + 1, :] = line[:, c * 128 : c * 128 + 128]


def finish(lengths, y, c, entering, lead, gate, norm_weight):
    length = y.shape[0]
    block = lambda width: pl.BlockSpec((BLOCK, width), lambda g, j: (j, g))
    return pl.pallas_call(
        finish_kernel,
        grid=(GROUPS, length // BLOCK),
        in_specs=[
            pl.BlockSpec(memory_space=pltpu.SMEM),
            block(GW),
            block(STATE),
            pl.BlockSpec((STATE, GW), lambda g, j: (0, g)),
            pl.BlockSpec((1, 1, BLOCK, 128), lambda g, j: (g, j, 0, 0)),
            block(GW),
            pl.BlockSpec((1, GW), lambda g, j: (0, g)),
        ],
        out_specs=[block(GW), pl.BlockSpec((GW // 256, 8, 128), lambda g, j: (g, 0, 0))],
        out_shape=[
            jax.ShapeDtypeStruct((length, D), BF16),
            jax.ShapeDtypeStruct((D // 256, 8, 128), F32),
        ],
        scratch_shapes=[pltpu.VMEM((128, GW), BF16), pltpu.VMEM((BLOCK, GW), F32)],
        compiler_params=pltpu.CompilerParams(
            vmem_limit_bytes=VMEM_LIMIT, dimension_semantics=("arbitrary", "arbitrary")
        ),
        name="finish",
    )(lengths, y, c, entering, lead, gate, norm_weight)


def tail_kernel(
    n,
    m,
    rows_ref,
    w_ref,
    tails_ref,
    reach_ref,
    resid_ref,
    gain_ref,
    vocab_ref,
    hid_ref,
    max_ref,
    fin_ref,
    vbuf,
    rrecv,
    ragg,
    wbuf,
    part,
    precv,
    h1,
    h2,
    hf,
    mx1,
    mx2,
    p1,
    p2,
    p3,
    p4,
    vsem,
    rs_s,
    rs_r,
    ag_s,
    ag_r,
    w_s,
    w_r,
    pt_s,
    pt_r,
    h1_s,
    h1_r,
    h2_s,
    h2_r,
    m1_s,
    m1_r,
    m2_s,
    m2_r,
    p1_s,
    p1_r,
    p2_s,
    p2_r,
    p3_s,
    p3_r,
    p4_s,
    p4_r,
):
    s = lax.axis_index("seq")
    b = lax.axis_index("req")
    width = D // n
    depth = D // m
    w_place = 2 * b + s // 8
    w_slot = lax.rem(s, 8)
    to_self = w_place == s
    from_b = s // 2
    from_s = 8 * lax.rem(s, 2)

    load = pltpu.make_async_copy(vocab_ref, vbuf, vsem)
    load.start()

    barrier = pltpu.get_barrier_semaphore()

    def signal(where):
        pl.semaphore_signal(barrier, inc=1, device_id=where, device_id_type=MESH)

    def seq_peer(i):
        return lax.rem(s + i, n)

    def req_peer(i):
        return lax.rem(b + i, m)

    def greet_seq(i, _):
        signal({"seq": seq_peer(i)})
        return 0

    def greet_req(i, _):
        signal({"req": req_peer(i)})
        return 0

    def greet_w(i, _):
        @pl.when(jnp.logical_not(to_self & (i == b)))
        def _():
            signal({"req": i, "seq": w_place})

        @pl.when(jnp.logical_not((from_b == b) & (from_s + i == s)))
        def _():
            signal({"req": from_b, "seq": from_s + i})

        return 0

    lax.fori_loop(1, n, greet_seq, 0)
    lax.fori_loop(1, m, greet_req, 0)
    lax.fori_loop(0, m, greet_w, 0)
    pl.semaphore_wait(barrier, (n - 1) + (m - 1) + 2 * m - 2 * to_self.astype(jnp.int32))

    def remote(src, dst, send, recv, where):
        return pltpu.make_async_remote_copy(
            src_ref=src, dst_ref=dst, send_sem=send, recv_sem=recv, device_id=where, device_id_type=MESH
        )

    def over(count, peer, copy, me):
        def start(i, _):
            copy(peer(i), me).start()
            return 0

        def arrive(i, _):
            copy(peer(i), peer(i)).wait_recv()
            return 0

        def drain(i, _):
            copy(peer(i), me).wait_send()
            return 0

        return (
            lambda: lax.fori_loop(1, count, start, 0),
            lambda: lax.fori_loop(1, count, arrive, 0),
            lambda: lax.fori_loop(1, count, drain, 0),
        )

    def rows_copy(p, slot):
        return remote(rows_ref.at[p], rrecv.at[slot], rs_s.at[p], rs_r.at[slot], {"seq": p})

    def gather_copy(p, slot):
        return remote(ragg.at[b], ragg.at[slot], ag_s.at[p], ag_r.at[slot], {"req": p})

    def part_copy(p, slot):
        cols = pl.ds(pl.multiple_of(lax.rem(p, 2) * 256, 256), 256)
        return remote(part.at[p // 2, :, cols], precv.at[slot], pt_s.at[p], pt_r.at[slot], {"seq": p})

    def h1_copy(p, slot):
        return remote(h1.at[b], h1.at[slot], h1_s.at[p], h1_r.at[slot], {"req": p})

    def h2_copy(p, slot):
        return remote(h1, h2.at[slot // 2, lax.rem(slot, 2)], h2_s.at[p], h2_r.at[slot], {"seq": p})

    def m1_copy(p, slot):
        return remote(mx1.at[b], mx1.at[slot], m1_s.at[p], m1_r.at[slot], {"req": p})

    def m2_copy(p, slot):
        return remote(mx2.at[s], mx2.at[slot], m2_s.at[p], m2_r.at[slot], {"seq": p})

    sy, sz = s // 4, lax.rem(s, 4)

    def even(c):
        return c + 1 - 2 * lax.rem(c, 2)

    def odd(c):
        return 3 - c

    orders = []
    for v in range(4):
        first_is_z = v % 2 == 0
        near, far = (even, odd) if v < 2 else (odd, even)
        c, e = (sz, sy) if first_is_z else (sy, sz)
        orders.append((first_is_z, near, far, c, e))

    def spot_of(v, c, e):
        return e * 4 + c if orders[v][0] else c * 4 + e

    def block(v, c, e):
        cols = pl.ds(pl.multiple_of(spot_of(v, c, e) * width, width), width)
        return (slice(None), pl.ds(32 * v, 32), cols)

    def stage1(v, i, q):
        _, near, far, c, _ = orders[v]
        p = near(c)
        src = tails_ref.at[block(v, p if i == 0 else far(p), q)]
        _, _, _, _, e = orders[v]
        return remote(src, p1.at[v, i, q], p1_s.at[v, i, q], p1_r.at[v, i, q], {"seq": spot_of(v, p, e)})

    def stage2(v, q):
        _, _, far, c, e = orders[v]
        return remote(
            p1.at[v, 1, q], p2.at[v, q], p2_s.at[v, q], p2_r.at[v, q], {"seq": spot_of(v, far(c), e)}
        )

    def stage3(v, i):
        _, near, far, c, e = orders[v]
        p = near(e)
        src = p2.at[v, p if i == 0 else far(p)]
        return remote(src, p3.at[v, i], p3_s.at[v, i], p3_r.at[v, i], {"seq": spot_of(v, c, p)})

    def stage4(v):
        _, _, far, c, e = orders[v]
        return remote(p3.at[v, 1], p4.at[v], p4_s.at[v], p4_r.at[v], {"seq": spot_of(v, c, far(e))})

    def each(act, one):
        for v in range(4):
            for i in range(2):
                if act == 1:

                    def step(q, _):
                        one(stage1(v, i, q))
                        return 0

                    lax.fori_loop(0, 4, step, 0)
                elif act == 2 and i == 0:

                    def step(q, _):
                        one(stage2(v, q))
                        return 0

                    lax.fori_loop(0, 4, step, 0)
                elif act == 3:
                    one(stage3(v, i))
                elif act == 4 and i == 0:
                    one(stage4(v))

    go = lambda copy: copy.start()
    got = lambda copy: copy.wait_recv()
    sent = lambda copy: copy.wait_send()

    def add1():
        for v in range(4):
            _, _, far, c, _ = orders[v]
            for i in range(2):

                def step(q, _):
                    p1[v, i, q] = p1[v, i, q] + tails_ref[block(v, c if i == 0 else far(c), q)]
                    return 0

                lax.fori_loop(0, 4, step, 0)

    def add2():
        for v in range(4):
            p2[v] = p2[v] + p1[v, 0]

    def add3():
        for v in range(4):
            _, _, far, _, e = orders[v]
            p3[v, 0] = p3[v, 0] + p2[v, e]
            p3[v, 1] = p3[v, 1] + p2[v, far(e)]

    rows_go, rows_in, rows_out = over(n, seq_peer, rows_copy, s)
    ag_go, ag_in, ag_out = over(m, req_peer, gather_copy, b)
    part_go, part_in, part_out = over(n, seq_peer, part_copy, s)
    h1_go, h1_in, h1_out = over(m, req_peer, h1_copy, b)
    h2_go, h2_in, h2_out = over(n, seq_peer, h2_copy, s)
    m1_go, m1_in, m1_out = over(m, req_peer, m1_copy, b)
    m2_go, m2_in, m2_out = over(n, seq_peer, m2_copy, s)

    rows_go()

    def w_copy(p):
        cols = pl.ds(pl.multiple_of(p * depth, depth), depth)
        return remote(
            w_ref.at[:, cols], wbuf.at[w_slot], w_s.at[p], w_r.at[w_slot], {"req": p, "seq": w_place}
        )

    def w_start(i, _):
        p = lax.rem(b + i, m)

        @pl.when(jnp.logical_not(to_self & (p == b)))
        def _():
            w_copy(p).start()

        return 0

    lax.fori_loop(0, m, w_start, 0)

    @pl.when(to_self)
    def _():
        wbuf[w_slot] = w_ref[:, pl.ds(pl.multiple_of(b * depth, depth), depth)]

    rrecv[s] = rows_ref[s]
    each(1, go)
    rows_in()
    ragg[b] = jnp.sum(rrecv[...], axis=0)
    ag_go()
    ag_in()

    def w_arrive(i, _):
        @pl.when(jnp.logical_not((from_b == b) & (from_s + i == s)))
        def _():
            remote(
                w_ref.at[:, pl.ds(0, depth)], wbuf.at[i], w_s.at[i], w_r.at[i], {"req": i, "seq": w_place}
            ).wait_recv()

        return 0

    lax.fori_loop(0, m, w_arrive, 0)

    lhs = ragg[...].reshape(8 * m, 128).astype(BF16)
    weights = wbuf[...].reshape(m * 32, depth)
    place = lax.broadcasted_iota(jnp.int32, (8 * m, depth), 0)
    both = jnp.where(place % 8 < 4, dot(lhs, weights[0:128]), dot(lhs, weights[128:256]))
    both = both + pltpu.roll(both, 4, 0)
    part[...] = both.reshape(m, 8, depth)
    part_go()
    precv[s] = part[s // 2, :, pl.ds(pl.multiple_of(lax.rem(s, 2) * 256, 256), 256)]
    each(1, got)
    add1()
    each(2, go)
    part_in()
    cols = pl.ds(pl.multiple_of(b * depth + lax.rem(s, 2) * 256, 256), 256)
    resid = resid_ref[s // 2, :, cols].astype(F32)
    hidden = jnp.sum(precv[...], axis=0) + jnp.concatenate([resid, resid], axis=0)
    upper = pltpu.roll(hidden[:, 128:256], 4, 0)
    eight = lax.broadcasted_iota(jnp.int32, (8, 128), 0)
    h1[b] = jnp.where(eight < 4, upper, hidden[:, 0:128]).astype(BF16)
    h1_go()
    h1_in()
    h2_go()
    h2[s // 2, lax.rem(s, 2)] = h1[...]
    each(2, got)
    add2()
    each(3, go)
    h2_in()

    for k in range(m):
        for q in range(2):
            piece = h2[:, q, k].astype(F32).reshape(8 * m, 128)
            lo = k * depth + q * 256
            hf[:, lo : lo + 128] = piece
            hf[:, lo + 128 : lo + 256] = pltpu.roll(piece, 4, 0)
    h = hf[...]
    hid_ref[0] = hf[pl.ds(pl.multiple_of(b * 8, 8), 8), :].astype(BF16)[SEQS:]
    scale = lax.rsqrt(jnp.mean(h * h, axis=1, keepdims=True) + TINY_FLOOR)
    normed = (h * scale * gain_ref[...]).astype(BF16)
    load.wait()
    top = jnp.full((1, 8 * m), -jnp.inf, F32)
    chunk = 256
    for k in range(vbuf.shape[0] // chunk):
        logits = dot_nt(vbuf[k * chunk : (k + 1) * chunk, :], normed)
        top = jnp.maximum(top, jnp.max(logits, axis=0, keepdims=True))
    top = jnp.concatenate([top, top], axis=1)
    mx1[b] = jnp.broadcast_to(top, (8, 128))
    m1_go()
    each(3, got)
    add3()
    each(4, go)
    m1_in()
    mx2[s] = jnp.max(mx1[...], axis=0)
    m2_go()

    each(4, got)
    for v in range(4):
        p4[v] = p4[v] + p3[v, 0]
    for r in range(SEQS - 1):
        share = jnp.concatenate([p4[v, r].astype(F32) for v in range(4)], axis=0)
        fin_ref[r] = (reach_ref[r] + share).T
    fin_ref[SEQS - 1] = reach_ref[SEQS - 1].T
    m2_in()
    best = jnp.max(mx2[...], axis=0)[0:1]
    lanes = lax.broadcasted_iota(jnp.int32, (1, 128), 1)
    four = lax.broadcasted_iota(jnp.int32, (1, SEQS), 1)
    top = jnp.zeros((1, SEQS), F32)
    for r in range(SEQS):
        one = jnp.max(jnp.where(lanes == b * 8 + SEQS + r, best, -jnp.inf), axis=1, keepdims=True)
        top = jnp.where(four == r, one, top)
    max_ref[...] = top

    for drain in (rows_out, ag_out, part_out, h1_out, h2_out, m1_out, m2_out):
        drain()

    def w_drain(p, _):
        @pl.when(jnp.logical_not(to_self & (p == b)))
        def _():
            w_copy(p).wait_send()

        return 0

    lax.fori_loop(0, m, w_drain, 0)

    for act in range(1, 5):
        each(act, sent)


def tail(rows, out_weight, tails, reached, resid, gain, vocab, n, m):
    width = D // n
    vmem = pl.BlockSpec(memory_space=pltpu.VMEM)
    dma = pltpu.SemaphoreType.DMA
    return pl.pallas_call(
        functools.partial(tail_kernel, n, m),
        in_specs=[vmem] * 6 + [pl.BlockSpec(memory_space=pl.ANY)],
        out_specs=[vmem] * 3,
        out_shape=[
            jax.ShapeDtypeStruct((1, SEQS, D), BF16),
            jax.ShapeDtypeStruct((1, SEQS), F32),
            jax.ShapeDtypeStruct((SEQS, width, STATE), F32),
        ],
        scratch_shapes=[
            pltpu.VMEM(vocab.shape, BF16),
            pltpu.VMEM((n, 8, 128), F32),
            pltpu.VMEM((m, 8, 128), F32),
            pltpu.VMEM((m, 32, D // m), BF16),
            pltpu.VMEM((m, 8, D // m), F32),
            pltpu.VMEM((n, 8, 256), F32),
            pltpu.VMEM((m, 8, 128), BF16),
            pltpu.VMEM((n // 2, 2, m, 8, 128), BF16),
            pltpu.VMEM((8 * m, D), F32),
            pltpu.VMEM((m, 8, 128), F32),
            pltpu.VMEM((n, 8, 128), F32),
            pltpu.VMEM((4, 2, 4, SEQS - 1, 32, width), BF16),
            pltpu.VMEM((4, 4, SEQS - 1, 32, width), BF16),
            pltpu.VMEM((4, 2, SEQS - 1, 32, width), BF16),
            pltpu.VMEM((4, SEQS - 1, 32, width), BF16),
            dma,
            dma((n,)),
            dma((n,)),
            dma((m,)),
            dma((m,)),
            dma((m,)),
            dma((m,)),
            dma((n,)),
            dma((n,)),
            dma((m,)),
            dma((m,)),
            dma((n,)),
            dma((n,)),
            dma((m,)),
            dma((m,)),
            dma((n,)),
            dma((n,)),
            dma((4, 2, 4)),
            dma((4, 2, 4)),
            dma((4, 4)),
            dma((4, 4)),
            dma((4, 2)),
            dma((4, 2)),
            dma((4,)),
            dma((4,)),
        ],
        compiler_params=pltpu.CompilerParams(
            collective_id=1, has_side_effects=True, vmem_limit_bytes=VMEM_LIMIT
        ),
        name="tail",
    )(rows, out_weight, tails, reached, resid, gain, vocab)


def body(
    conv_input,
    gate_projected,
    step_raw,
    step_bias,
    decay_log,
    head_direct_gain,
    conv_weight,
    convolution_bias,
    norm_weight,
    lengths,
    out_weight,
    residual_last,
    final_gain,
    vocab_weight,
):
    local_len = conv_input.shape[1]
    seq_count = lax.axis_size("seq")
    req_count = lax.axis_size("req")
    conv = conv_input[0]
    route = [(i, i + 1) for i in range(seq_count - 1)]
    halo = lax.ppermute(conv[local_len - 8 :], "seq", route)
    y, states, tails, aux, c, lead = local_pass(
        lengths,
        conv,
        halo,
        conv_weight,
        convolution_bias[None],
        step_raw[0],
        step_bias[None],
        decay_log[None],
        head_direct_gain[None],
    )
    entering, reached = exchange(states, aux, seq_count)
    gated, rows = finish(lengths, y, c, entering, lead, gate_projected[0], norm_weight[None])
    hid, top, final = tail(
        rows, out_weight, tails, reached, residual_last, final_gain[None], vocab_weight, seq_count, req_count
    )
    final_states = final.reshape(SEQS, HEADS // seq_count, CHANNEL_WIDTH, STATE)[None]
    return (gated[None], final_states, hid, top)


def solution(mesh):
    return jax.shard_map(
        body,
        mesh=mesh,
        in_specs=(
            P("req", "seq", None),
            P("req", "seq", None),
            P("req", "seq", None),
            P(),
            P(),
            P(),
            P(),
            P(),
            P(),
            P("req", None),
            P(("req", "seq"), None),
            P(),
            P(),
            P(("req", "seq"), None),
        ),
        out_specs=(
            P("req", "seq", None),
            P("req", None, "seq", None, None),
            P("req", None, None),
            P("req", None),
        ),
        check_vma=False,
    )
```

```python
import functools

import jax
import jax.numpy as jnp
from jax import lax
from jax.experimental import pallas as pl
from jax.experimental.pallas import tpu as pltpu
from jax.sharding import PartitionSpec as P

D = 4096
HEADS = 64
CHANNEL_WIDTH = 64
GROUPS = 4
STATE = 128
CHUNKS = [slice(c * 256, c * 256 + 256) for c in range(4)]
KERNEL = 4
BLOCK = 256
SEQS = 4
PER_GROUP = HEADS // GROUPS
GW = PER_GROUP * CHANNEL_WIDTH
TINY_FLOOR = 1e-05
LOG2E = 1.4426950408889634
MESH = pl.DeviceIdType.MESH
F32 = jnp.float32
BF16 = jnp.bfloat16
VMEM_LIMIT = 60 * 1024 * 1024


def dot(a, b):
    return lax.dot_general(a, b, (((1,), (0,)), ((), ())), preferred_element_type=F32)


def dot_nt(a, b):
    return lax.dot_general(a, b, (((1,), (1,)), ((), ())), preferred_element_type=F32)


def split2(x):
    hi = x.astype(BF16)
    return hi, (x - hi.astype(F32)).astype(BF16)


def split3(x):
    hi = x.astype(BF16)
    rest = x - hi.astype(F32)
    mid = rest.astype(BF16)
    return hi, mid, (rest - mid.astype(F32)).astype(BF16)


def seg_of(place, b1, b2, b3):
    one = lambda b: (place >= b).astype(jnp.int32)
    return one(b1) + one(b2) + one(b3)


def spread_matrix():
    lane = lax.broadcasted_iota(jnp.int32, (128, GW), 0)
    col = lax.broadcasted_iota(jnp.int32, (128, GW), 1)
    hit = (lane < 48) & (lane % PER_GROUP == col // CHANNEL_WIDTH)
    return jnp.where(hit, 1.0, 0.0).astype(BF16)


def spread_parts(v):
    hi, mid, lo = split3(v)
    lane = lax.broadcasted_iota(jnp.int32, v.shape, 1)
    parts = jnp.where(
        lane < 16, hi.astype(F32), jnp.where(lane < 32, mid.astype(F32), lo.astype(F32))
    ).astype(BF16)
    return parts


def spread(v, spread_ref):
    return dot(spread_parts(v), spread_ref[...])


def halves(h):
    return h + h * jnp.tanh(h)


def softplus(x):
    e = jnp.exp(-jnp.abs(x))
    w = 1.0 + e
    d = w - 1.0
    return jnp.maximum(x, 0.0) + jnp.where(d == 0.0, e, jnp.log(w) * (e / jnp.where(d == 0.0, 1.0, d)))


def bounds_of(len_ref):
    b1 = len_ref[0, 0]
    b2 = b1 + len_ref[0, 1]
    return b1, b2, b2 + len_ref[0, 2]


def local_kernel(
    len_ref,
    x_ref,
    b_ref,
    c_ref,
    xh_ref,
    bh_ref,
    ch_ref,
    wx_ref,
    wb_ref,
    wc_ref,
    vx_ref,
    vb_ref,
    vc_ref,
    raw_ref,
    bias_ref,
    log_ref,
    gain_ref,
    y_ref,
    st_ref,
    pt_ref,
    aux_ref,
    co_ref,
    ld_ref,
    xext,
    xf,
    s0,
    c0,
    cumr,
    sp,
    msk,
    alw,
    sgs,
    cums,
    lds,
    dxs,
    wst,
    ow,
):
    g = pl.program_id(0)
    j = pl.program_id(1)
    span = pl.num_programs(1) * BLOCK
    first = lax.axis_index("seq") * span
    b1, b2, b3 = bounds_of(len_ref)
    bounds = (b1, b2, b3)
    start = first + j * BLOCK

    @pl.when((g == 0) & (j == 0))
    def _():
        sp[...] = spread_matrix()

    row = lax.broadcasted_iota(jnp.int32, (BLOCK, 128), 0) + start

    @pl.when(g == 0)
    def _():
        near = jnp.full((BLOCK, 128), 8, jnp.int32)
        for bound in bounds:
            gap = row - bound
            near = jnp.where(gap >= 0, jnp.minimum(near, gap), near)
        for k in range(3):
            msk[j, k] = (near >= 3 - k).astype(F32)
        sgs[j] = seg_of(row, b1, b2, b3)
        i0 = lax.broadcasted_iota(jnp.int32, (BLOCK, BLOCK), 0)
        i1 = lax.broadcasted_iota(jnp.int32, (BLOCK, BLOCK), 1)
        t_seg = seg_of(i0 + start, b1, b2, b3)
        s_seg = seg_of(i1 + start, b1, b2, b3)
        alw[j] = ((i0 >= i1) & (t_seg == s_seg)).astype(F32)
        tri = jnp.where(i0 >= i1, 1.0, 0.0).astype(BF16)
        dt = softplus(raw_ref[...].T + bias_ref[...])
        dh, dm, dl = split3(dt * (jnp.exp(log_ref[...]) * -LOG2E))
        cums[j] = (dot(tri, dl) + dot(tri, dm)) + dot(tri, dh)
        lds[j] = jnp.log(dt) * LOG2E

    l0 = lax.broadcasted_iota(jnp.int32, (HEADS, 128), 0)
    l1 = lax.broadcasted_iota(jnp.int32, (HEADS, 128), 1)
    pick = jnp.where(l0 == g * PER_GROUP + l1 % PER_GROUP, 1.0, 0.0).astype(BF16)
    t0 = lax.broadcasted_iota(jnp.int32, (PER_GROUP, HEADS), 0)
    t1 = lax.broadcasted_iota(jnp.int32, (PER_GROUP, HEADS), 1)
    pickt = jnp.where(t1 == g * PER_GROUP + t0, 1.0, 0.0).astype(BF16)

    def group(v):
        hi, mid, lo = split3(v)
        return (dot(lo, pick) + dot(mid, pick)) + dot(hi, pick)

    @pl.when(j == 0)
    def _():
        xext[0:8, 0:GW] = xh_ref[...].astype(F32)
        xext[0:8, GW : GW + 128] = bh_ref[...].astype(F32)
        xext[0:8, GW + 128 : GW + 256] = ch_ref[...].astype(F32)
        for lo, hi, w_ref, v_ref in (
            (0, GW, wx_ref, vx_ref),
            (GW, GW + 128, wb_ref, vb_ref),
            (GW + 128, GW + 256, wc_ref, vc_ref),
        ):
            wst[0:KERNEL, lo:hi] = w_ref[...] * 0.5
            wst[KERNEL : KERNEL + 1, lo:hi] = v_ref[...] * 0.5
        pt_ref[...] = jnp.zeros_like(pt_ref)
        aux_ref[...] = jnp.zeros_like(aux_ref)
        c0[...] = jnp.zeros_like(c0)
        dxs[...] = spread(group(jnp.broadcast_to(gain_ref[...], (8, HEADS))), sp)

    @pl.when(j == 1)
    def _():
        xext[0:8, :] = xext[BLOCK : BLOCK + 8, :]

    xext[8 : BLOCK + 8, 0:GW] = x_ref[...].astype(F32)
    xext[8 : BLOCK + 8, GW : GW + 128] = b_ref[...].astype(F32)
    xext[8 : BLOCK + 8, GW + 128 : GW + 256] = c_ref[...].astype(F32)

    tile = 64

    def convolve(c, _):
        cols = pl.ds(pl.multiple_of(c * 128, 128), 128)
        w = [wst[k : k + 1, cols] for k in range(KERNEL)]
        bias = wst[KERNEL : KERNEL + 1, cols]
        for lo in range(0, BLOCK, tile):
            total = jnp.broadcast_to(bias, (tile, 128))
            for k in range(3):
                total = total + w[k] * xext[lo + 5 + k : lo + 5 + k + tile, cols] * msk[j, k, lo : lo + tile]
            total = total + w[3] * xext[lo + 8 : lo + 8 + tile, cols]
            xf[lo : lo + tile, cols] = halves(total)
        return 0

    lax.fori_loop(0, 10, convolve, 0)

    seg = sgs[j]
    bf = xf[:, GW : GW + 128]
    cb = xf[:, GW + 128 : GW + 256].astype(BF16)
    co_ref[...] = cb

    cum = group(cums[j])
    logdt = group(lds[j])
    rh, rm, rl = split3(lds[j] - cums[j])
    rt = (dot_nt(pickt, rl) + dot_nt(pickt, rm)) + dot_nt(pickt, rh)
    cumr[...] = cum
    last = cum[BLOCK - 1 : BLOCK, :]

    seg_before_span = seg_of(first - 1, b1, b2, b3)
    seg_before = seg_of(start - 1, b1, b2, b3)
    seg_end = seg_of(start + BLOCK - 1, b1, b2, b3)
    prior = c0[0:1, :]
    ld_ref[0, 0] = jnp.where(seg == seg_before_span, jnp.exp2(cum + prior), 0.0)

    bh, bl = split2(bf)
    sc = dot_nt(cb, bh) * alw[j]

    @pl.when(j == 0)
    def _():
        y_ref[...] = jnp.zeros_like(y_ref)

    @pl.when(j == 1)
    def _():
        lead = jnp.where(seg == seg_before, jnp.exp2(cum), 0.0)
        sh, sl = split2(s0[...])
        parts = spread_parts(lead)
        for cols in CHUNKS:
            y_ref[:, cols] = dot(parts, sp[:, cols]) * (dot(cb, sh[:, cols]) + dot(cb, sl[:, cols]))

    lane = lax.broadcasted_iota(jnp.int32, (BLOCK, 128), 1)
    half = BLOCK // 2
    sc_t = sc[:half, :half]
    sc_l = sc[half:, :half]
    sc_r = sc[half:, half:]
    for pair in range(PER_GROUP // 2):
        cols = slice(pair * 128, pair * 128 + 128)
        xb = xf[:, cols].astype(BF16)
        res = []
        for h in (2 * pair, 2 * pair + 1):
            col = cum[:, h : h + 1]
            r = rt[h : h + 1, :]
            top = jnp.exp2(jnp.minimum(col[:half] + r[:, :half], 100.0)) * sc_t
            left = jnp.exp2(col[half:] + r[:, :half]) * sc_l
            right = jnp.exp2(jnp.minimum(col[half:] + r[:, half:], 100.0)) * sc_r
            bottom = jnp.concatenate([left.astype(BF16), right.astype(BF16)], axis=1)
            res.append(
                jnp.concatenate([dot(top.astype(BF16), xb[:half]), dot(bottom, xb)], axis=0)
            )
        intra = jnp.where(lane < CHANNEL_WIDTH, res[0], res[1])
        y_ref[:, cols] = y_ref[:, cols] + (intra + dxs[0:1, cols] * xb.astype(F32))

    both = jnp.concatenate(split2(bf.T), axis=0)

    def state_of(weights, put):
        parts = spread_parts(weights)
        for cols in CHUNKS:
            xs = (xf[:, cols] * dot(parts, sp[:, cols])).astype(BF16)
            two = dot(both, xs)
            put(cols, two[:STATE] + two[STATE:])

    def at_end(seg_e):
        return jnp.where(seg == seg_e, jnp.exp2(last - cum + logdt), 0.0)

    def put_own(cols, value):
        ow[:, cols] = value

    state_of(at_end(seg_end), put_own)

    for r in range(SEQS - 1):
        end = bounds[r] - 1
        local = end - start
        owned = (local >= 0) & (local < BLOCK)

        @pl.when(owned)
        def _():
            ce = cumr[pl.ds(jnp.clip(local, 0, BLOCK - 1), 1), :]
            inside = (row <= end) & (seg == r)
            w = jnp.exp2(jnp.where(inside, ce - cum + logdt, -1e30))
            reach = jnp.where(seg_before == r, jnp.exp2(ce), 0.0)
            reach8 = spread(jnp.broadcast_to(reach, (8, 128)), sp)

            def put_tail(cols, value):
                before = jnp.where(j == 1, reach8[0:1, cols] * s0[:, cols], 0.0)
                pt_ref[r, :, cols] = (value + before).astype(BF16)

            state_of(w, put_tail)
            full = jnp.where(seg_before_span == r, jnp.exp2(ce + prior), 0.0)
            aux_ref[1 + r : 2 + r, :] = spread(jnp.broadcast_to(full, (8, 128)), sp)[0:1]

    @pl.when(j == 0)
    def _():
        s0[...] = ow[...]
        c0[...] = jnp.broadcast_to(last, c0.shape)

    @pl.when(j == 1)
    def _():
        carry = jnp.where(seg_end == seg_before, jnp.exp2(last), 0.0)
        whole = jnp.where(seg_end == seg_before_span, jnp.exp2(last + prior), 0.0)
        carry8 = spread(jnp.broadcast_to(carry, (8, 128)), sp)
        whole8 = spread(jnp.broadcast_to(whole, (8, 128)), sp)
        st_ref[...] = (carry8[0:1] * s0[...] + ow[...]).astype(BF16)
        aux_ref[0:1, :] = whole8[0:1]


def local_pass(lengths, conv, halo, conv_weight, conv_bias, raw, bias, log, gain):
    length = conv.shape[0]
    blocks = length // BLOCK
    maps = D // 128
    grid = (GROUPS, blocks)
    xs = lambda rows: [
        pl.BlockSpec((rows, GW), lambda g, j: (0, g)),
        pl.BlockSpec((rows, 128), lambda g, j: (0, maps + g)),
        pl.BlockSpec((rows, 128), lambda g, j: (0, maps + GROUPS + g)),
    ]
    in_specs = (
        [
            pl.BlockSpec(memory_space=pltpu.SMEM),
            pl.BlockSpec((BLOCK, GW), lambda g, j: (j, g)),
            pl.BlockSpec((BLOCK, 128), lambda g, j: (j, maps + g)),
            pl.BlockSpec((BLOCK, 128), lambda g, j: (j, maps + GROUPS + g)),
        ]
        + xs(8)
        + xs(KERNEL)
        + xs(1)
        + [
            pl.BlockSpec((HEADS, BLOCK), lambda g, j: (0, j)),
            pl.BlockSpec((1, HEADS), lambda g, j: (0, 0)),
            pl.BlockSpec((1, HEADS), lambda g, j: (0, 0)),
            pl.BlockSpec((1, HEADS), lambda g, j: (0, 0)),
        ]
    )
    out_specs = [
        pl.BlockSpec((BLOCK, GW), lambda g, j: (j, g)),
        pl.BlockSpec((STATE, GW), lambda g, j: (0, g)),
        pl.BlockSpec((SEQS - 1, STATE, GW), lambda g, j: (0, 0, g)),
        pl.BlockSpec((8, GW), lambda g, j: (0, g)),
        pl.BlockSpec((BLOCK, 128), lambda g, j: (j, g)),
        pl.BlockSpec((1, 1, BLOCK, 128), lambda g, j: (g, j, 0, 0)),
    ]
    out_shape = [
        jax.ShapeDtypeStruct((length, D), F32),
        jax.ShapeDtypeStruct((STATE, D), BF16),
        jax.ShapeDtypeStruct((SEQS - 1, STATE, D), BF16),
        jax.ShapeDtypeStruct((8, D), F32),
        jax.ShapeDtypeStruct((length, GROUPS * STATE), BF16),
        jax.ShapeDtypeStruct((GROUPS, blocks, BLOCK, 128), F32),
    ]
    return pl.pallas_call(
        local_kernel,
        grid=grid,
        in_specs=in_specs,
        out_specs=out_specs,
        out_shape=out_shape,
        scratch_shapes=[
            pltpu.VMEM((BLOCK + 8, GW + 256), F32),
            pltpu.VMEM((BLOCK, GW + 256), F32),
            pltpu.VMEM((STATE, GW), F32),
            pltpu.VMEM((8, 128), F32),
            pltpu.VMEM((BLOCK, 128), F32),
            pltpu.VMEM((128, GW), BF16),
            pltpu.VMEM((blocks, 3, BLOCK, 128), F32),
            pltpu.VMEM((blocks, BLOCK, BLOCK), F32),
            pltpu.VMEM((blocks, BLOCK, 128), jnp.int32),
            pltpu.VMEM((blocks, BLOCK, HEADS), F32),
            pltpu.VMEM((blocks, BLOCK, HEADS), F32),
            pltpu.VMEM((8, GW), F32),
            pltpu.VMEM((8, GW + 256), F32),
            pltpu.VMEM((STATE, GW), F32),
        ],
        compiler_params=pltpu.CompilerParams(
            vmem_limit_bytes=VMEM_LIMIT, dimension_semantics=("arbitrary", "arbitrary")
        ),
        name="local_pass",
    )(
        lengths, conv, conv, conv, halo, halo, halo, conv_weight, conv_weight, conv_weight,
        conv_bias, conv_bias, conv_bias, raw, bias, log, gain,
    )


def exchange_kernel(
    n,
    st_ref,
    aux_ref,
    ent_ref,
    fin_ref,
    rs,
    ra,
    eb,
    send1,
    recv1,
    send2,
    recv2,
    send3,
    recv3,
):
    me = lax.axis_index("seq")
    width = D // n
    barrier = pltpu.get_barrier_semaphore()

    def peer(i):
        return lax.rem(me + i, n)

    def cols(p):
        return pl.ds(pl.multiple_of(p * width, width), width)

    def greet(i, _):
        pl.semaphore_signal(barrier, inc=1, device_id={"seq": peer(i)}, device_id_type=MESH)
        return 0

    lax.fori_loop(1, n, greet, 0)
    pl.semaphore_wait(barrier, n - 1)

    def out(p, slot):
        return (
            pltpu.make_async_remote_copy(
                src_ref=st_ref.at[:, cols(p)],
                dst_ref=rs.at[slot],
                send_sem=send1.at[p],
                recv_sem=recv1.at[slot],
                device_id={"seq": p},
                device_id_type=MESH,
            ),
            pltpu.make_async_remote_copy(
                src_ref=aux_ref.at[:, cols(p)],
                dst_ref=ra.at[slot],
                send_sem=send2.at[p],
                recv_sem=recv2.at[slot],
                device_id={"seq": p},
                device_id_type=MESH,
            ),
        )

    def back(p, slot):
        return pltpu.make_async_remote_copy(
            src_ref=eb.at[p],
            dst_ref=ent_ref.at[:, cols(slot)],
            send_sem=send3.at[p],
            recv_sem=recv3.at[slot],
            device_id={"seq": p},
            device_id_type=MESH,
        )

    def begin(i, _):
        for copy in out(peer(i), me):
            copy.start()
        return 0

    lax.fori_loop(1, n, begin, 0)
    rs[me] = st_ref[:, cols(me)]
    ra[me] = aux_ref[:, cols(me)]

    fin_ref[...] = jnp.zeros_like(fin_ref)

    def scan(d, _):
        @pl.when(d != me)
        def _():
            for copy in out(d, d):
                copy.wait_recv()

        now = fin_ref[SEQS - 1]
        eb[d] = now.astype(BF16)

        @pl.when(d != me)
        def _():
            back(d, me).start()

        for r in range(SEQS - 1):
            fin_ref[r] = fin_ref[r] + ra[d, 1 + r : 2 + r, :] * now
        fin_ref[SEQS - 1] = ra[d, 0:1, :] * now + rs[d].astype(F32)
        return 0

    lax.fori_loop(0, n, scan, 0)
    ent_ref[:, cols(me)] = eb[me]

    def done(i, _):
        back(peer(i), peer(i)).wait_recv()
        return 0

    lax.fori_loop(1, n, done, 0)

    def drain(i, _):
        for copy in out(peer(i), me):
            copy.wait_send()
        back(peer(i), me).wait_send()
        return 0

    lax.fori_loop(1, n, drain, 0)


def exchange(states, aux, n):
    width = D // n
    vmem = pl.BlockSpec(memory_space=pltpu.VMEM)
    return pl.pallas_call(
        functools.partial(exchange_kernel, n),
        in_specs=[vmem, vmem],
        out_specs=[vmem, vmem],
        out_shape=[
            jax.ShapeDtypeStruct((STATE, D), BF16),
            jax.ShapeDtypeStruct((SEQS, STATE, width), F32),
        ],
        scratch_shapes=[
            pltpu.VMEM((n, STATE, width), BF16),
            pltpu.VMEM((n, 8, width), F32),
            pltpu.VMEM((n, STATE, width), BF16),
        ]
        + [pltpu.SemaphoreType.DMA((n,)) for _ in range(6)],
        compiler_params=pltpu.CompilerParams(
            collective_id=0, has_side_effects=True, vmem_limit_bytes=VMEM_LIMIT
        ),
        name="exchange",
    )(states, aux)


def finish_kernel(len_ref, y_ref, c_ref, e_ref, ld_ref, gate_ref, nw_ref, out_ref, rows_ref, sp, of, scales):
    g = pl.program_id(0)
    j = pl.program_id(1)

    @pl.when((g == 0) & (j == 0))
    def _():
        sp[...] = spread_matrix()

    @pl.when(j == 0)
    def _():
        rows_ref[...] = jnp.zeros_like(rows_ref)

    parts = spread_parts(ld_ref[0, 0])
    half = BLOCK // 2
    for lines in (slice(0, half), slice(half, BLOCK)):
        total = jnp.zeros((half, 128), F32)
        for cols in CHUNKS:
            v = y_ref[lines, cols] + dot(parts[lines], sp[:, cols]) * dot(c_ref[lines, :], e_ref[:, cols])
            v = v * halves(0.5 * gate_ref[lines, cols].astype(F32))
            of[lines, cols] = v
            total = total + v[:, :128] * v[:, :128] + v[:, 128:] * v[:, 128:]
        scale = lax.rsqrt(jnp.sum(total, axis=1, keepdims=True) * (1.0 / GW) + TINY_FLOOR)
        scales[lines, :] = jnp.broadcast_to(scale, (half, 128))
        for cols in CHUNKS:
            out_ref[lines, cols] = (of[lines, cols] * scale * nw_ref[:, cols]).astype(BF16)

    start = lax.axis_index("seq") * (pl.num_programs(1) * BLOCK) + j * BLOCK
    bounds = bounds_of(len_ref)
    for r, bound in enumerate(bounds + (bounds[2] + len_ref[0, 3],)):
        local = bound - 1 - start

        @pl.when((local >= 0) & (local < BLOCK))
        def _():
            spot = jnp.clip(local, 0, BLOCK - 1)
            line = of[pl.ds(spot, 1), :] * scales[pl.ds(spot, 1), :][:, 0:1] * nw_ref[...]
            line = line.astype(BF16).astype(F32)
            for c in range(GW // 128):
                place = c % 2 * SEQS + r
                rows_ref[c // 2, place : place + 1, :] = line[:, c * 128 : c * 128 + 128]


def finish(lengths, y, c, entering, lead, gate, norm_weight):
    length = y.shape[0]
    block = lambda width: pl.BlockSpec((BLOCK, width), lambda g, j: (j, g))
    return pl.pallas_call(
        finish_kernel,
        grid=(GROUPS, length // BLOCK),
        in_specs=[
            pl.BlockSpec(memory_space=pltpu.SMEM),
            block(GW),
            block(STATE),
            pl.BlockSpec((STATE, GW), lambda g, j: (0, g)),
            pl.BlockSpec((1, 1, BLOCK, 128), lambda g, j: (g, j, 0, 0)),
            block(GW),
            pl.BlockSpec((1, GW), lambda g, j: (0, g)),
        ],
        out_specs=[block(GW), pl.BlockSpec((GW // 256, 8, 128), lambda g, j: (g, 0, 0))],
        out_shape=[
            jax.ShapeDtypeStruct((length, D), BF16),
            jax.ShapeDtypeStruct((D // 256, 8, 128), F32),
        ],
        scratch_shapes=[
            pltpu.VMEM((128, GW), BF16),
            pltpu.VMEM((BLOCK, GW), F32),
            pltpu.VMEM((BLOCK, 128), F32),
        ],
        compiler_params=pltpu.CompilerParams(
            vmem_limit_bytes=VMEM_LIMIT, dimension_semantics=("arbitrary", "arbitrary")
        ),
        name="finish",
    )(lengths, y, c, entering, lead, gate, norm_weight)


def tail_kernel(
    n,
    m,
    rows_ref,
    w_ref,
    tails_ref,
    reach_ref,
    resid_ref,
    gain_ref,
    vocab_ref,
    hid_ref,
    max_ref,
    fin_ref,
    vbuf,
    rrecv,
    ragg,
    wbuf,
    part,
    precv,
    h1,
    h2,
    hf,
    mx1,
    mx2,
    p1,
    p2,
    p3,
    p4,
    vsem,
    rs_s,
    rs_r,
    ag_s,
    ag_r,
    w_s,
    w_r,
    pt_s,
    pt_r,
    h1_s,
    h1_r,
    h2_s,
    h2_r,
    m1_s,
    m1_r,
    m2_s,
    m2_r,
    p1_s,
    p1_r,
    p2_s,
    p2_r,
    p3_s,
    p3_r,
    p4_s,
    p4_r,
):
    s = lax.axis_index("seq")
    b = lax.axis_index("req")
    width = D // n
    depth = D // m
    w_place = 2 * b + s // 8
    w_slot = lax.rem(s, 8)
    to_self = w_place == s
    from_b = s // 2
    from_s = 8 * lax.rem(s, 2)

    load = pltpu.make_async_copy(vocab_ref, vbuf, vsem)
    load.start()

    barrier = pltpu.get_barrier_semaphore()

    def signal(where):
        pl.semaphore_signal(barrier, inc=1, device_id=where, device_id_type=MESH)

    def seq_peer(i):
        return lax.rem(s + i, n)

    def req_peer(i):
        return lax.rem(b + i, m)

    def greet_seq(i, _):
        signal({"seq": seq_peer(i)})
        return 0

    def greet_req(i, _):
        signal({"req": req_peer(i)})
        return 0

    def greet_w(i, _):
        @pl.when(jnp.logical_not(to_self & (i == b)))
        def _():
            signal({"req": i, "seq": w_place})

        @pl.when(jnp.logical_not((from_b == b) & (from_s + i == s)))
        def _():
            signal({"req": from_b, "seq": from_s + i})

        return 0

    lax.fori_loop(1, n, greet_seq, 0)
    lax.fori_loop(1, m, greet_req, 0)
    lax.fori_loop(0, m, greet_w, 0)
    pl.semaphore_wait(barrier, (n - 1) + (m - 1) + 2 * m - 2 * to_self.astype(jnp.int32))

    def remote(src, dst, send, recv, where):
        return pltpu.make_async_remote_copy(
            src_ref=src, dst_ref=dst, send_sem=send, recv_sem=recv, device_id=where, device_id_type=MESH
        )

    def over(count, peer, copy, me):
        def start(i, _):
            copy(peer(i), me).start()
            return 0

        def arrive(i, _):
            copy(peer(i), peer(i)).wait_recv()
            return 0

        def drain(i, _):
            copy(peer(i), me).wait_send()
            return 0

        return (
            lambda: lax.fori_loop(1, count, start, 0),
            lambda: lax.fori_loop(1, count, arrive, 0),
            lambda: lax.fori_loop(1, count, drain, 0),
        )

    def rows_copy(p, slot):
        return remote(rows_ref.at[p], rrecv.at[slot], rs_s.at[p], rs_r.at[slot], {"seq": p})

    def gather_copy(p, slot):
        return remote(ragg.at[b], ragg.at[slot], ag_s.at[p], ag_r.at[slot], {"req": p})

    def part_copy(p, slot):
        cols = pl.ds(pl.multiple_of(lax.rem(p, 2) * 256, 256), 256)
        return remote(part.at[p // 2, :, cols], precv.at[slot], pt_s.at[p], pt_r.at[slot], {"seq": p})

    def h1_copy(p, slot):
        return remote(h1.at[b], h1.at[slot], h1_s.at[p], h1_r.at[slot], {"req": p})

    def h2_copy(p, slot):
        return remote(h1, h2.at[slot // 2, lax.rem(slot, 2)], h2_s.at[p], h2_r.at[slot], {"seq": p})

    def m1_copy(p, slot):
        return remote(mx1.at[b], mx1.at[slot], m1_s.at[p], m1_r.at[slot], {"req": p})

    def m2_copy(p, slot):
        return remote(mx2.at[s], mx2.at[slot], m2_s.at[p], m2_r.at[slot], {"seq": p})

    sy, sz = s // 4, lax.rem(s, 4)

    def even(c):
        return c + 1 - 2 * lax.rem(c, 2)

    def odd(c):
        return 3 - c

    orders = []
    for v in range(4):
        first_is_z = v % 2 == 0
        near, far = (even, odd) if v < 2 else (odd, even)
        c, e = (sz, sy) if first_is_z else (sy, sz)
        orders.append((first_is_z, near, far, c, e))

    def spot_of(v, c, e):
        return e * 4 + c if orders[v][0] else c * 4 + e

    def block(v, c, e):
        cols = pl.ds(pl.multiple_of(spot_of(v, c, e) * width, width), width)
        return (slice(None), pl.ds(32 * v, 32), cols)

    def stage1(v, i, q):
        _, near, far, c, _ = orders[v]
        p = near(c)
        src = tails_ref.at[block(v, p if i == 0 else far(p), q)]
        _, _, _, _, e = orders[v]
        return remote(src, p1.at[v, i, q], p1_s.at[v, i, q], p1_r.at[v, i, q], {"seq": spot_of(v, p, e)})

    def stage2(v, q):
        _, _, far, c, e = orders[v]
        return remote(
            p1.at[v, 1, q], p2.at[v, q], p2_s.at[v, q], p2_r.at[v, q], {"seq": spot_of(v, far(c), e)}
        )

    def stage3(v, i):
        _, near, far, c, e = orders[v]
        p = near(e)
        src = p2.at[v, p if i == 0 else far(p)]
        return remote(src, p3.at[v, i], p3_s.at[v, i], p3_r.at[v, i], {"seq": spot_of(v, c, p)})

    def stage4(v):
        _, _, far, c, e = orders[v]
        return remote(p3.at[v, 1], p4.at[v], p4_s.at[v], p4_r.at[v], {"seq": spot_of(v, c, far(e))})

    def each(act, one):
        for v in range(4):
            for i in range(2):
                if act == 1:

                    def step(q, _):
                        one(stage1(v, i, q))
                        return 0

                    lax.fori_loop(0, 4, step, 0)
                elif act == 2 and i == 0:

                    def step(q, _):
                        one(stage2(v, q))
                        return 0

                    lax.fori_loop(0, 4, step, 0)
                elif act == 3:
                    one(stage3(v, i))
                elif act == 4 and i == 0:
                    one(stage4(v))

    go = lambda copy: copy.start()
    got = lambda copy: copy.wait_recv()
    sent = lambda copy: copy.wait_send()

    def add1():
        for v in range(4):
            _, _, far, c, _ = orders[v]
            for i in range(2):

                def step(q, _):
                    p1[v, i, q] = p1[v, i, q] + tails_ref[block(v, c if i == 0 else far(c), q)]
                    return 0

                lax.fori_loop(0, 4, step, 0)

    def add2():
        for v in range(4):
            p2[v] = p2[v] + p1[v, 0]

    def add3():
        for v in range(4):
            _, _, far, _, e = orders[v]
            p3[v, 0] = p3[v, 0] + p2[v, e]
            p3[v, 1] = p3[v, 1] + p2[v, far(e)]

    rows_go, rows_in, rows_out = over(n, seq_peer, rows_copy, s)
    ag_go, ag_in, ag_out = over(m, req_peer, gather_copy, b)
    part_go, part_in, part_out = over(n, seq_peer, part_copy, s)
    h1_go, h1_in, h1_out = over(m, req_peer, h1_copy, b)
    h2_go, h2_in, h2_out = over(n, seq_peer, h2_copy, s)
    m1_go, m1_in, m1_out = over(m, req_peer, m1_copy, b)
    m2_go, m2_in, m2_out = over(n, seq_peer, m2_copy, s)

    rows_go()

    def w_copy(p):
        cols = pl.ds(pl.multiple_of(p * depth, depth), depth)
        return remote(
            w_ref.at[:, cols], wbuf.at[w_slot], w_s.at[p], w_r.at[w_slot], {"req": p, "seq": w_place}
        )

    def w_start(i, _):
        p = lax.rem(b + i, m)

        @pl.when(jnp.logical_not(to_self & (p == b)))
        def _():
            w_copy(p).start()

        return 0

    lax.fori_loop(0, m, w_start, 0)

    @pl.when(to_self)
    def _():
        wbuf[w_slot] = w_ref[:, pl.ds(pl.multiple_of(b * depth, depth), depth)]

    rrecv[s] = rows_ref[s]
    each(1, go)
    rows_in()
    ragg[b] = jnp.sum(rrecv[...], axis=0)
    ag_go()
    ag_in()

    def w_arrive(i, _):
        @pl.when(jnp.logical_not((from_b == b) & (from_s + i == s)))
        def _():
            remote(
                w_ref.at[:, pl.ds(0, depth)], wbuf.at[i], w_s.at[i], w_r.at[i], {"req": i, "seq": w_place}
            ).wait_recv()

        return 0

    lax.fori_loop(0, m, w_arrive, 0)

    lhs = ragg[...].reshape(8 * m, 128).astype(BF16)
    weights = wbuf[...].reshape(m * 32, depth)
    place = lax.broadcasted_iota(jnp.int32, (8 * m, depth), 0)
    both = jnp.where(place % 8 < 4, dot(lhs, weights[0:128]), dot(lhs, weights[128:256]))
    both = both + pltpu.roll(both, 4, 0)
    part[...] = both.reshape(m, 8, depth)
    part_go()
    precv[s] = part[s // 2, :, pl.ds(pl.multiple_of(lax.rem(s, 2) * 256, 256), 256)]
    each(1, got)
    add1()
    each(2, go)
    part_in()
    cols = pl.ds(pl.multiple_of(b * depth + lax.rem(s, 2) * 256, 256), 256)
    resid = resid_ref[s // 2, :, cols].astype(F32)
    hidden = jnp.sum(precv[...], axis=0) + jnp.concatenate([resid, resid], axis=0)
    upper = pltpu.roll(hidden[:, 128:256], 4, 0)
    eight = lax.broadcasted_iota(jnp.int32, (8, 128), 0)
    h1[b] = jnp.where(eight < 4, upper, hidden[:, 0:128]).astype(BF16)
    h1_go()
    h1_in()
    h2_go()
    h2[s // 2, lax.rem(s, 2)] = h1[...]
    each(2, got)
    add2()
    each(3, go)
    h2_in()

    for k in range(m):
        for q in range(2):
            piece = h2[:, q, k].astype(F32).reshape(8 * m, 128)
            lo = k * depth + q * 256
            hf[:, lo : lo + 128] = piece
            hf[:, lo + 128 : lo + 256] = pltpu.roll(piece, 4, 0)
    h = hf[...]
    hid_ref[0] = hf[pl.ds(pl.multiple_of(b * 8, 8), 8), :].astype(BF16)[SEQS:]
    scale = lax.rsqrt(jnp.mean(h * h, axis=1, keepdims=True) + TINY_FLOOR)
    normed = (h * scale * gain_ref[...]).astype(BF16)
    load.wait()
    top = jnp.full((1, 8 * m), -jnp.inf, F32)
    chunk = 256
    for k in range(vbuf.shape[0] // chunk):
        logits = dot_nt(vbuf[k * chunk : (k + 1) * chunk, :], normed)
        top = jnp.maximum(top, jnp.max(logits, axis=0, keepdims=True))
    top = jnp.concatenate([top, top], axis=1)
    mx1[b] = jnp.broadcast_to(top, (8, 128))
    m1_go()
    each(3, got)
    add3()
    each(4, go)
    m1_in()
    mx2[s] = jnp.max(mx1[...], axis=0)
    m2_go()

    each(4, got)
    for v in range(4):
        p4[v] = p4[v] + p3[v, 0]
    for r in range(SEQS - 1):
        share = jnp.concatenate([p4[v, r].astype(F32) for v in range(4)], axis=0)
        fin_ref[r] = reach_ref[r] + share
    fin_ref[SEQS - 1] = reach_ref[SEQS - 1]
    m2_in()
    best = jnp.max(mx2[...], axis=0)[0:1]
    lanes = lax.broadcasted_iota(jnp.int32, (1, 128), 1)
    four = lax.broadcasted_iota(jnp.int32, (1, SEQS), 1)
    top = jnp.zeros((1, SEQS), F32)
    for r in range(SEQS):
        one = jnp.max(jnp.where(lanes == b * 8 + SEQS + r, best, -jnp.inf), axis=1, keepdims=True)
        top = jnp.where(four == r, one, top)
    max_ref[...] = top

    for drain in (rows_out, ag_out, part_out, h1_out, h2_out, m1_out, m2_out):
        drain()

    def w_drain(p, _):
        @pl.when(jnp.logical_not(to_self & (p == b)))
        def _():
            w_copy(p).wait_send()

        return 0

    lax.fori_loop(0, m, w_drain, 0)

    for act in range(1, 5):
        each(act, sent)


def tail(rows, out_weight, tails, reached, resid, gain, vocab, n, m):
    width = D // n
    vmem = pl.BlockSpec(memory_space=pltpu.VMEM)
    dma = pltpu.SemaphoreType.DMA
    return pl.pallas_call(
        functools.partial(tail_kernel, n, m),
        in_specs=[vmem] * 6 + [pl.BlockSpec(memory_space=pl.ANY)],
        out_specs=[vmem] * 3,
        out_shape=[
            jax.ShapeDtypeStruct((1, SEQS, D), BF16),
            jax.ShapeDtypeStruct((1, SEQS), F32),
            jax.ShapeDtypeStruct((SEQS, STATE, width), F32),
        ],
        scratch_shapes=[
            pltpu.VMEM(vocab.shape, BF16),
            pltpu.VMEM((n, 8, 128), F32),
            pltpu.VMEM((m, 8, 128), F32),
            pltpu.VMEM((m, 32, D // m), BF16),
            pltpu.VMEM((m, 8, D // m), F32),
            pltpu.VMEM((n, 8, 256), F32),
            pltpu.VMEM((m, 8, 128), BF16),
            pltpu.VMEM((n // 2, 2, m, 8, 128), BF16),
            pltpu.VMEM((8 * m, D), F32),
            pltpu.VMEM((m, 8, 128), F32),
            pltpu.VMEM((n, 8, 128), F32),
            pltpu.VMEM((4, 2, 4, SEQS - 1, 32, width), BF16),
            pltpu.VMEM((4, 4, SEQS - 1, 32, width), BF16),
            pltpu.VMEM((4, 2, SEQS - 1, 32, width), BF16),
            pltpu.VMEM((4, SEQS - 1, 32, width), BF16),
            dma,
            dma((n,)),
            dma((n,)),
            dma((m,)),
            dma((m,)),
            dma((m,)),
            dma((m,)),
            dma((n,)),
            dma((n,)),
            dma((m,)),
            dma((m,)),
            dma((n,)),
            dma((n,)),
            dma((m,)),
            dma((m,)),
            dma((n,)),
            dma((n,)),
            dma((4, 2, 4)),
            dma((4, 2, 4)),
            dma((4, 4)),
            dma((4, 4)),
            dma((4, 2)),
            dma((4, 2)),
            dma((4,)),
            dma((4,)),
        ],
        compiler_params=pltpu.CompilerParams(
            collective_id=1, has_side_effects=True, vmem_limit_bytes=VMEM_LIMIT
        ),
        name="tail",
    )(rows, out_weight, tails, reached, resid, gain, vocab)


def pack_kernel(fin_ref, hid_ref, top_ref, fin_out, hid_out, top_out):
    for r in range(SEQS):
        fin_out[r] = fin_ref[r].T
    hid_out[...] = hid_ref[...]
    top_out[...] = top_ref[...]


def pack(final, hid, top):
    vmem = pl.BlockSpec(memory_space=pltpu.VMEM)
    return pl.pallas_call(
        pack_kernel,
        in_specs=[vmem] * 3,
        out_specs=[vmem] * 3,
        out_shape=[
            jax.ShapeDtypeStruct((final.shape[0], final.shape[2], final.shape[1]), F32),
            jax.ShapeDtypeStruct(hid.shape, BF16),
            jax.ShapeDtypeStruct(top.shape, F32),
        ],
        name="pack",
    )(final, hid, top)


def body(
    conv_input,
    gate_projected,
    step_raw,
    step_bias,
    decay_log,
    head_direct_gain,
    conv_weight,
    convolution_bias,
    norm_weight,
    lengths,
    out_weight,
    residual_last,
    final_gain,
    vocab_weight,
):
    local_len = conv_input.shape[1]
    seq_count = lax.axis_size("seq")
    req_count = lax.axis_size("req")
    conv = conv_input[0]
    route = [(i, i + 1) for i in range(seq_count - 1)]
    halo = lax.ppermute(conv[local_len - 8 :], "seq", route)
    y, states, tails, aux, c, lead = local_pass(
        lengths,
        conv,
        halo,
        conv_weight,
        convolution_bias[None],
        step_raw[0].T,
        step_bias[None],
        decay_log[None],
        head_direct_gain[None],
    )
    entering, reached = exchange(states, aux, seq_count)
    gated, rows = finish(lengths, y, c, entering, lead, gate_projected[0], norm_weight[None])
    hid, top, final = tail(
        rows, out_weight, tails, reached, residual_last, final_gain[None], vocab_weight, seq_count, req_count
    )
    final, hid, top = pack(final, hid, top)
    final_states = final.reshape(SEQS, HEADS // seq_count, CHANNEL_WIDTH, STATE)[None]
    return (gated[None], final_states, hid, top)


def solution(mesh):
    return jax.shard_map(
        body,
        mesh=mesh,
        in_specs=(
            P("req", "seq", None),
            P("req", "seq", None),
            P("req", "seq", None),
            P(),
            P(),
            P(),
            P(),
            P(),
            P(),
            P("req", None),
            P(("req", "seq"), None),
            P(),
            P(),
            P(("req", "seq"), None),
        ),
        out_specs=(
            P("req", "seq", None),
            P("req", None, "seq", None, None),
            P("req", None, None),
            P("req", None),
        ),
        check_vma=False,
    )
```

```python
import functools

import jax
import jax.numpy as jnp
from jax import lax
from jax.experimental import pallas as pl
from jax.experimental.pallas import tpu as pltpu
from jax.sharding import PartitionSpec as P

D = 4096
HEADS = 64
CHANNEL_WIDTH = 64
GROUPS = 4
STATE = 128
CHUNKS = [slice(c * 256, c * 256 + 256) for c in range(4)]
KERNEL = 4
BLOCK = 256
SEQS = 4
PER_GROUP = HEADS // GROUPS
GW = PER_GROUP * CHANNEL_WIDTH
TINY_FLOOR = 1e-05
LOG2E = 1.4426950408889634
MESH = pl.DeviceIdType.MESH
F32 = jnp.float32
BF16 = jnp.bfloat16
VMEM_LIMIT = 60 * 1024 * 1024


def dot(a, b):
    return lax.dot_general(a, b, (((1,), (0,)), ((), ())), preferred_element_type=F32)


def dot_nt(a, b):
    return lax.dot_general(a, b, (((1,), (1,)), ((), ())), preferred_element_type=F32)


def split2(x):
    hi = x.astype(BF16)
    return hi, (x - hi.astype(F32)).astype(BF16)


def split3(x):
    hi = x.astype(BF16)
    rest = x - hi.astype(F32)
    mid = rest.astype(BF16)
    return hi, mid, (rest - mid.astype(F32)).astype(BF16)


def seg_of(place, b1, b2, b3):
    one = lambda b: (place >= b).astype(jnp.int32)
    return one(b1) + one(b2) + one(b3)


def spread_matrix():
    lane = lax.broadcasted_iota(jnp.int32, (128, GW), 0)
    col = lax.broadcasted_iota(jnp.int32, (128, GW), 1)
    hit = (lane < 48) & (lane % PER_GROUP == col // CHANNEL_WIDTH)
    return jnp.where(hit, 1.0, 0.0).astype(BF16)


def spread_parts(v):
    hi, mid, lo = split3(v)
    lane = lax.broadcasted_iota(jnp.int32, v.shape, 1)
    parts = jnp.where(
        lane < 16, hi.astype(F32), jnp.where(lane < 32, mid.astype(F32), lo.astype(F32))
    ).astype(BF16)
    return parts


def spread(v, spread_ref):
    return dot(spread_parts(v), spread_ref[...])


def halves(h):
    return h + h * jnp.tanh(h)


def softplus(x):
    e = jnp.exp(-jnp.abs(x))
    w = 1.0 + e
    d = w - 1.0
    return jnp.maximum(x, 0.0) + jnp.where(d == 0.0, e, jnp.log(w) * (e / jnp.where(d == 0.0, 1.0, d)))


def bounds_of(len_ref):
    b1 = len_ref[0, 0]
    b2 = b1 + len_ref[0, 1]
    return b1, b2, b2 + len_ref[0, 2]


def local_kernel(
    len_ref,
    x_ref,
    b_ref,
    c_ref,
    xh_ref,
    bh_ref,
    ch_ref,
    wx_ref,
    wb_ref,
    wc_ref,
    vx_ref,
    vb_ref,
    vc_ref,
    raw_ref,
    bias_ref,
    log_ref,
    gain_ref,
    y_ref,
    st_ref,
    pt_ref,
    aux_ref,
    co_ref,
    ld_ref,
    xext,
    xf,
    s0,
    c0,
    cumr,
    sp,
    msk,
    alw,
    sgs,
    cums,
    lds,
    dxs,
    wst,
    ow,
):
    g = pl.program_id(0)
    j = pl.program_id(1)
    span = pl.num_programs(1) * BLOCK
    first = lax.axis_index("seq") * span
    b1, b2, b3 = bounds_of(len_ref)
    bounds = (b1, b2, b3)
    start = first + j * BLOCK

    @pl.when((g == 0) & (j == 0))
    def _():
        sp[...] = spread_matrix()

    row = lax.broadcasted_iota(jnp.int32, (BLOCK, 128), 0) + start

    @pl.when(g == 0)
    def _():
        near = jnp.full((BLOCK, 128), 8, jnp.int32)
        for bound in bounds:
            gap = row - bound
            near = jnp.where(gap >= 0, jnp.minimum(near, gap), near)
        for k in range(3):
            msk[j, k] = (near >= 3 - k).astype(F32)
        sgs[j] = seg_of(row, b1, b2, b3)
        i0 = lax.broadcasted_iota(jnp.int32, (BLOCK, BLOCK), 0)
        i1 = lax.broadcasted_iota(jnp.int32, (BLOCK, BLOCK), 1)
        t_seg = seg_of(i0 + start, b1, b2, b3)
        s_seg = seg_of(i1 + start, b1, b2, b3)
        alw[j] = ((i0 >= i1) & (t_seg == s_seg)).astype(F32)
        tri = jnp.where(i0 >= i1, 1.0, 0.0).astype(BF16)
        dt = softplus(raw_ref[...].T + bias_ref[...])
        dh, dm, dl = split3(dt * (jnp.exp(log_ref[...]) * -LOG2E))
        cums[j] = (dot(tri, dl) + dot(tri, dm)) + dot(tri, dh)
        lds[j] = jnp.log(dt) * LOG2E

    l0 = lax.broadcasted_iota(jnp.int32, (HEADS, 128), 0)
    l1 = lax.broadcasted_iota(jnp.int32, (HEADS, 128), 1)
    pick = jnp.where(l0 == g * PER_GROUP + l1 % PER_GROUP, 1.0, 0.0).astype(BF16)
    t0 = lax.broadcasted_iota(jnp.int32, (PER_GROUP, HEADS), 0)
    t1 = lax.broadcasted_iota(jnp.int32, (PER_GROUP, HEADS), 1)
    pickt = jnp.where(t1 == g * PER_GROUP + t0, 1.0, 0.0).astype(BF16)

    def group(v):
        hi, mid, lo = split3(v)
        return (dot(lo, pick) + dot(mid, pick)) + dot(hi, pick)

    @pl.when(j == 0)
    def _():
        xext[0:8, 0:GW] = xh_ref[...].astype(F32)
        xext[0:8, GW : GW + 128] = bh_ref[...].astype(F32)
        xext[0:8, GW + 128 : GW + 256] = ch_ref[...].astype(F32)
        for lo, hi, w_ref, v_ref in (
            (0, GW, wx_ref, vx_ref),
            (GW, GW + 128, wb_ref, vb_ref),
            (GW + 128, GW + 256, wc_ref, vc_ref),
        ):
            wst[0:KERNEL, lo:hi] = w_ref[...] * 0.5
            wst[KERNEL : KERNEL + 1, lo:hi] = v_ref[...] * 0.5
        pt_ref[...] = jnp.zeros_like(pt_ref)
        aux_ref[...] = jnp.zeros_like(aux_ref)
        c0[...] = jnp.zeros_like(c0)
        dxs[...] = spread(group(jnp.broadcast_to(gain_ref[...], (8, HEADS))), sp)

    @pl.when(j == 1)
    def _():
        xext[0:8, :] = xext[BLOCK : BLOCK + 8, :]

    xext[8 : BLOCK + 8, 0:GW] = x_ref[...].astype(F32)
    xext[8 : BLOCK + 8, GW : GW + 128] = b_ref[...].astype(F32)
    xext[8 : BLOCK + 8, GW + 128 : GW + 256] = c_ref[...].astype(F32)

    tile = 64

    def convolve(c, _):
        cols = pl.ds(pl.multiple_of(c * 128, 128), 128)
        w = [wst[k : k + 1, cols] for k in range(KERNEL)]
        bias = wst[KERNEL : KERNEL + 1, cols]
        for lo in range(0, BLOCK, tile):
            total = jnp.broadcast_to(bias, (tile, 128))
            for k in range(3):
                total = total + w[k] * xext[lo + 5 + k : lo + 5 + k + tile, cols] * msk[j, k, lo : lo + tile]
            total = total + w[3] * xext[lo + 8 : lo + 8 + tile, cols]
            xf[lo : lo + tile, cols] = halves(total)
        return 0

    lax.fori_loop(0, 10, convolve, 0)

    seg = sgs[j]
    bf = xf[:, GW : GW + 128]
    cb = xf[:, GW + 128 : GW + 256].astype(BF16)
    co_ref[...] = cb

    cum = group(cums[j])
    logdt = group(lds[j])
    rh, rm, rl = split3(lds[j] - cums[j])
    rt = (dot_nt(pickt, rl) + dot_nt(pickt, rm)) + dot_nt(pickt, rh)
    cumr[...] = cum
    last = cum[BLOCK - 1 : BLOCK, :]

    seg_before_span = seg_of(first - 1, b1, b2, b3)
    seg_before = seg_of(start - 1, b1, b2, b3)
    seg_end = seg_of(start + BLOCK - 1, b1, b2, b3)
    prior = c0[0:1, :]
    ld_ref[0, 0] = jnp.where(seg == seg_before_span, jnp.exp2(cum + prior), 0.0)

    bh, bl = split2(bf)
    sc = dot_nt(cb, bh) * alw[j]

    @pl.when(j == 0)
    def _():
        y_ref[...] = jnp.zeros_like(y_ref)

    @pl.when(j == 1)
    def _():
        lead = jnp.where(seg == seg_before, jnp.exp2(cum), 0.0)
        sh, sl = split2(s0[...])
        parts = spread_parts(lead)
        for cols in CHUNKS:
            y_ref[:, cols] = dot(parts, sp[:, cols]) * (dot(cb, sh[:, cols]) + dot(cb, sl[:, cols]))

    lane = lax.broadcasted_iota(jnp.int32, (BLOCK, 128), 1)
    half = BLOCK // 2
    sc_t = sc[:half, :half]
    sc_l = sc[half:, :half]
    sc_r = sc[half:, half:]
    for pair in range(PER_GROUP // 2):
        cols = slice(pair * 128, pair * 128 + 128)
        xb = xf[:, cols].astype(BF16)
        res = []
        for h in (2 * pair, 2 * pair + 1):
            col = cum[:, h : h + 1]
            r = rt[h : h + 1, :]
            top = jnp.exp2(jnp.minimum(col[:half] + r[:, :half], 100.0)) * sc_t
            left = jnp.exp2(col[half:] + r[:, :half]) * sc_l
            right = jnp.exp2(jnp.minimum(col[half:] + r[:, half:], 100.0)) * sc_r
            bottom = jnp.concatenate([left.astype(BF16), right.astype(BF16)], axis=1)
            res.append(
                jnp.concatenate([dot(top.astype(BF16), xb[:half]), dot(bottom, xb)], axis=0)
            )
        intra = jnp.where(lane < CHANNEL_WIDTH, res[0], res[1])
        y_ref[:, cols] = y_ref[:, cols] + (intra + dxs[0:1, cols] * xb.astype(F32))

    both = jnp.concatenate(split2(bf.T), axis=0)

    def state_of(weights, put):
        parts = spread_parts(weights)
        for cols in CHUNKS:
            xs = (xf[:, cols] * dot(parts, sp[:, cols])).astype(BF16)
            two = dot(both, xs)
            put(cols, two[:STATE] + two[STATE:])

    def at_end(seg_e):
        return jnp.where(seg == seg_e, jnp.exp2(last - cum + logdt), 0.0)

    def put_own(cols, value):
        ow[:, cols] = value

    state_of(at_end(seg_end), put_own)

    for r in range(SEQS - 1):
        end = bounds[r] - 1
        local = end - start
        owned = (local >= 0) & (local < BLOCK)

        @pl.when(owned)
        def _():
            ce = cumr[pl.ds(jnp.clip(local, 0, BLOCK - 1), 1), :]
            inside = (row <= end) & (seg == r)
            w = jnp.exp2(jnp.where(inside, ce - cum + logdt, -1e30))
            reach = jnp.where(seg_before == r, jnp.exp2(ce), 0.0)
            reach8 = spread(jnp.broadcast_to(reach, (8, 128)), sp)

            def put_tail(cols, value):
                before = jnp.where(j == 1, reach8[0:1, cols] * s0[:, cols], 0.0)
                pt_ref[r, :, cols] = (value + before).astype(BF16)

            state_of(w, put_tail)
            full = jnp.where(seg_before_span == r, jnp.exp2(ce + prior), 0.0)
            aux_ref[1 + r : 2 + r, :] = spread(jnp.broadcast_to(full, (8, 128)), sp)[0:1]

    @pl.when(j == 0)
    def _():
        s0[...] = ow[...]
        c0[...] = jnp.broadcast_to(last, c0.shape)

    @pl.when(j == 1)
    def _():
        carry = jnp.where(seg_end == seg_before, jnp.exp2(last), 0.0)
        whole = jnp.where(seg_end == seg_before_span, jnp.exp2(last + prior), 0.0)
        carry8 = spread(jnp.broadcast_to(carry, (8, 128)), sp)
        whole8 = spread(jnp.broadcast_to(whole, (8, 128)), sp)
        st_ref[...] = (carry8[0:1] * s0[...] + ow[...]).astype(BF16)
        aux_ref[0:1, :] = whole8[0:1]


def local_pass(lengths, conv, halo, conv_weight, conv_bias, raw, bias, log, gain):
    length = conv.shape[0]
    blocks = length // BLOCK
    maps = D // 128
    grid = (GROUPS, blocks)
    xs = lambda rows: [
        pl.BlockSpec((rows, GW), lambda g, j: (0, g)),
        pl.BlockSpec((rows, 128), lambda g, j: (0, maps + g)),
        pl.BlockSpec((rows, 128), lambda g, j: (0, maps + GROUPS + g)),
    ]
    in_specs = (
        [
            pl.BlockSpec(memory_space=pltpu.SMEM),
            pl.BlockSpec((BLOCK, GW), lambda g, j: (j, g)),
            pl.BlockSpec((BLOCK, 128), lambda g, j: (j, maps + g)),
            pl.BlockSpec((BLOCK, 128), lambda g, j: (j, maps + GROUPS + g)),
        ]
        + xs(8)
        + xs(KERNEL)
        + xs(1)
        + [
            pl.BlockSpec((HEADS, BLOCK), lambda g, j: (0, j)),
            pl.BlockSpec((1, HEADS), lambda g, j: (0, 0)),
            pl.BlockSpec((1, HEADS), lambda g, j: (0, 0)),
            pl.BlockSpec((1, HEADS), lambda g, j: (0, 0)),
        ]
    )
    out_specs = [
        pl.BlockSpec((BLOCK, GW), lambda g, j: (j, g)),
        pl.BlockSpec((STATE, GW), lambda g, j: (0, g)),
        pl.BlockSpec((SEQS - 1, STATE, GW), lambda g, j: (0, 0, g)),
        pl.BlockSpec((8, GW), lambda g, j: (0, g)),
        pl.BlockSpec((BLOCK, 128), lambda g, j: (j, g)),
        pl.BlockSpec((1, 1, BLOCK, 128), lambda g, j: (g, j, 0, 0)),
    ]
    out_shape = [
        jax.ShapeDtypeStruct((length, D), F32),
        jax.ShapeDtypeStruct((STATE, D), BF16),
        jax.ShapeDtypeStruct((SEQS - 1, STATE, D), BF16),
        jax.ShapeDtypeStruct((8, D), F32),
        jax.ShapeDtypeStruct((length, GROUPS * STATE), BF16),
        jax.ShapeDtypeStruct((GROUPS, blocks, BLOCK, 128), F32),
    ]
    return pl.pallas_call(
        local_kernel,
        grid=grid,
        in_specs=in_specs,
        out_specs=out_specs,
        out_shape=out_shape,
        scratch_shapes=[
            pltpu.VMEM((BLOCK + 8, GW + 256), F32),
            pltpu.VMEM((BLOCK, GW + 256), F32),
            pltpu.VMEM((STATE, GW), F32),
            pltpu.VMEM((8, 128), F32),
            pltpu.VMEM((BLOCK, 128), F32),
            pltpu.VMEM((128, GW), BF16),
            pltpu.VMEM((blocks, 3, BLOCK, 128), F32),
            pltpu.VMEM((blocks, BLOCK, BLOCK), F32),
            pltpu.VMEM((blocks, BLOCK, 128), jnp.int32),
            pltpu.VMEM((blocks, BLOCK, HEADS), F32),
            pltpu.VMEM((blocks, BLOCK, HEADS), F32),
            pltpu.VMEM((8, GW), F32),
            pltpu.VMEM((8, GW + 256), F32),
            pltpu.VMEM((STATE, GW), F32),
        ],
        compiler_params=pltpu.CompilerParams(
            vmem_limit_bytes=VMEM_LIMIT, dimension_semantics=("arbitrary", "arbitrary")
        ),
        name="local_pass",
    )(
        lengths, conv, conv, conv, halo, halo, halo, conv_weight, conv_weight, conv_weight,
        conv_bias, conv_bias, conv_bias, raw, bias, log, gain,
    )


def halo_kernel(n, conv_ref, out_ref, got, send, recv):
    me = lax.axis_index("seq")
    right = lax.rem(me + 1, n)
    left = lax.rem(me + n - 1, n)
    barrier = pltpu.get_barrier_semaphore()
    for p in (left, right):
        pl.semaphore_signal(barrier, inc=1, device_id={"seq": p}, device_id_type=MESH)
    pl.semaphore_wait(barrier, 2)
    copy = pltpu.make_async_remote_copy(
        src_ref=conv_ref.at[pl.ds(conv_ref.shape[0] - 8, 8), :],
        dst_ref=got,
        send_sem=send,
        recv_sem=recv,
        device_id={"seq": right},
        device_id_type=MESH,
    )
    copy.start()
    copy.wait()
    keep = jnp.where(me == 0, 0.0, 1.0)
    out_ref[...] = (got[...].astype(F32) * keep).astype(BF16)


def halo_rows(conv, n):
    shape = (8, conv.shape[1])
    return pl.pallas_call(
        functools.partial(halo_kernel, n),
        in_specs=[pl.BlockSpec(memory_space=pl.ANY)],
        out_specs=pl.BlockSpec(memory_space=pltpu.VMEM),
        out_shape=jax.ShapeDtypeStruct(shape, BF16),
        scratch_shapes=[
            pltpu.VMEM(shape, BF16),
            pltpu.SemaphoreType.DMA,
            pltpu.SemaphoreType.DMA,
        ],
        compiler_params=pltpu.CompilerParams(collective_id=2, has_side_effects=True),
        name="halo",
    )(conv)


def exchange_kernel(
    n,
    st_ref,
    aux_ref,
    ent_ref,
    fin_ref,
    rs,
    ra,
    eb,
    send1,
    recv1,
    send2,
    recv2,
    send3,
    recv3,
):
    me = lax.axis_index("seq")
    width = D // n
    barrier = pltpu.get_barrier_semaphore()

    def peer(i):
        return lax.rem(me + i, n)

    def cols(p):
        return pl.ds(pl.multiple_of(p * width, width), width)

    def greet(i, _):
        pl.semaphore_signal(barrier, inc=1, device_id={"seq": peer(i)}, device_id_type=MESH)
        return 0

    lax.fori_loop(1, n, greet, 0)
    pl.semaphore_wait(barrier, n - 1)

    def out(p, slot):
        return (
            pltpu.make_async_remote_copy(
                src_ref=st_ref.at[:, cols(p)],
                dst_ref=rs.at[slot],
                send_sem=send1.at[p],
                recv_sem=recv1.at[slot],
                device_id={"seq": p},
                device_id_type=MESH,
            ),
            pltpu.make_async_remote_copy(
                src_ref=aux_ref.at[:, cols(p)],
                dst_ref=ra.at[slot],
                send_sem=send2.at[p],
                recv_sem=recv2.at[slot],
                device_id={"seq": p},
                device_id_type=MESH,
            ),
        )

    def back(p, slot):
        return pltpu.make_async_remote_copy(
            src_ref=eb.at[p],
            dst_ref=ent_ref.at[:, cols(slot)],
            send_sem=send3.at[p],
            recv_sem=recv3.at[slot],
            device_id={"seq": p},
            device_id_type=MESH,
        )

    def begin(i, _):
        for copy in out(peer(i), me):
            copy.start()
        return 0

    lax.fori_loop(1, n, begin, 0)
    rs[me] = st_ref[:, cols(me)]
    ra[me] = aux_ref[:, cols(me)]

    fin_ref[...] = jnp.zeros_like(fin_ref)

    def scan(d, _):
        @pl.when(d != me)
        def _():
            for copy in out(d, d):
                copy.wait_recv()

        now = fin_ref[SEQS - 1]
        eb[d] = now.astype(BF16)

        @pl.when(d != me)
        def _():
            back(d, me).start()

        for r in range(SEQS - 1):
            fin_ref[r] = fin_ref[r] + ra[d, 1 + r : 2 + r, :] * now
        fin_ref[SEQS - 1] = ra[d, 0:1, :] * now + rs[d].astype(F32)
        return 0

    lax.fori_loop(0, n, scan, 0)
    ent_ref[:, cols(me)] = eb[me]

    def done(i, _):
        back(peer(i), peer(i)).wait_recv()
        return 0

    lax.fori_loop(1, n, done, 0)

    def drain(i, _):
        for copy in out(peer(i), me):
            copy.wait_send()
        back(peer(i), me).wait_send()
        return 0

    lax.fori_loop(1, n, drain, 0)


def exchange(states, aux, n):
    width = D // n
    vmem = pl.BlockSpec(memory_space=pltpu.VMEM)
    return pl.pallas_call(
        functools.partial(exchange_kernel, n),
        in_specs=[vmem, vmem],
        out_specs=[vmem, vmem],
        out_shape=[
            jax.ShapeDtypeStruct((STATE, D), BF16),
            jax.ShapeDtypeStruct((SEQS, STATE, width), F32),
        ],
        scratch_shapes=[
            pltpu.VMEM((n, STATE, width), BF16),
            pltpu.VMEM((n, 8, width), F32),
            pltpu.VMEM((n, STATE, width), BF16),
        ]
        + [pltpu.SemaphoreType.DMA((n,)) for _ in range(6)],
        compiler_params=pltpu.CompilerParams(
            collective_id=0, has_side_effects=True, vmem_limit_bytes=VMEM_LIMIT
        ),
        name="exchange",
    )(states, aux)


def finish_kernel(len_ref, y_ref, c_ref, e_ref, ld_ref, gate_ref, nw_ref, out_ref, rows_ref, sp, of, scales):
    g = pl.program_id(0)
    j = pl.program_id(1)

    @pl.when((g == 0) & (j == 0))
    def _():
        sp[...] = spread_matrix()

    @pl.when(j == 0)
    def _():
        rows_ref[...] = jnp.zeros_like(rows_ref)

    parts = spread_parts(ld_ref[0, 0])
    half = BLOCK // 2
    for lines in (slice(0, half), slice(half, BLOCK)):
        total = jnp.zeros((half, 128), F32)
        for cols in CHUNKS:
            v = y_ref[lines, cols] + dot(parts[lines], sp[:, cols]) * dot(c_ref[lines, :], e_ref[:, cols])
            v = v * halves(0.5 * gate_ref[lines, cols].astype(F32))
            of[lines, cols] = v
            total = total + v[:, :128] * v[:, :128] + v[:, 128:] * v[:, 128:]
        scale = lax.rsqrt(jnp.sum(total, axis=1, keepdims=True) * (1.0 / GW) + TINY_FLOOR)
        scales[lines, :] = jnp.broadcast_to(scale, (half, 128))
        for cols in CHUNKS:
            out_ref[lines, cols] = (of[lines, cols] * scale * nw_ref[:, cols]).astype(BF16)

    start = lax.axis_index("seq") * (pl.num_programs(1) * BLOCK) + j * BLOCK
    bounds = bounds_of(len_ref)
    for r, bound in enumerate(bounds + (bounds[2] + len_ref[0, 3],)):
        local = bound - 1 - start

        @pl.when((local >= 0) & (local < BLOCK))
        def _():
            spot = jnp.clip(local, 0, BLOCK - 1)
            line = of[pl.ds(spot, 1), :] * scales[pl.ds(spot, 1), :][:, 0:1] * nw_ref[...]
            line = line.astype(BF16).astype(F32)
            for c in range(GW // 128):
                place = c % 2 * SEQS + r
                rows_ref[c // 2, place : place + 1, :] = line[:, c * 128 : c * 128 + 128]


def finish(lengths, y, c, entering, lead, gate, norm_weight):
    length = y.shape[0]
    block = lambda width: pl.BlockSpec((BLOCK, width), lambda g, j: (j, g))
    return pl.pallas_call(
        finish_kernel,
        grid=(GROUPS, length // BLOCK),
        in_specs=[
            pl.BlockSpec(memory_space=pltpu.SMEM),
            block(GW),
            block(STATE),
            pl.BlockSpec((STATE, GW), lambda g, j: (0, g)),
            pl.BlockSpec((1, 1, BLOCK, 128), lambda g, j: (g, j, 0, 0)),
            block(GW),
            pl.BlockSpec((1, GW), lambda g, j: (0, g)),
        ],
        out_specs=[block(GW), pl.BlockSpec((GW // 256, 8, 128), lambda g, j: (g, 0, 0))],
        out_shape=[
            jax.ShapeDtypeStruct((length, D), BF16),
            jax.ShapeDtypeStruct((D // 256, 8, 128), F32),
        ],
        scratch_shapes=[
            pltpu.VMEM((128, GW), BF16),
            pltpu.VMEM((BLOCK, GW), F32),
            pltpu.VMEM((BLOCK, 128), F32),
        ],
        compiler_params=pltpu.CompilerParams(
            vmem_limit_bytes=VMEM_LIMIT, dimension_semantics=("arbitrary", "arbitrary")
        ),
        name="finish",
    )(lengths, y, c, entering, lead, gate, norm_weight)


def tail_kernel(
    n,
    m,
    rows_ref,
    w_ref,
    tails_ref,
    reach_ref,
    resid_ref,
    gain_ref,
    vocab_ref,
    hid_ref,
    max_ref,
    fin_ref,
    vbuf,
    rrecv,
    ragg,
    wbuf,
    part,
    precv,
    h1,
    h2,
    hf,
    mx1,
    mx2,
    p1,
    p2,
    p3,
    p4,
    vsem,
    rs_s,
    rs_r,
    ag_s,
    ag_r,
    w_s,
    w_r,
    pt_s,
    pt_r,
    h1_s,
    h1_r,
    h2_s,
    h2_r,
    m1_s,
    m1_r,
    m2_s,
    m2_r,
    p1_s,
    p1_r,
    p2_s,
    p2_r,
    p3_s,
    p3_r,
    p4_s,
    p4_r,
):
    s = lax.axis_index("seq")
    b = lax.axis_index("req")
    width = D // n
    depth = D // m
    w_place = 2 * b + s // 8
    w_slot = lax.rem(s, 8)
    to_self = w_place == s
    from_b = s // 2
    from_s = 8 * lax.rem(s, 2)

    load = pltpu.make_async_copy(vocab_ref, vbuf, vsem)
    load.start()

    barrier = pltpu.get_barrier_semaphore()

    def signal(where):
        pl.semaphore_signal(barrier, inc=1, device_id=where, device_id_type=MESH)

    def seq_peer(i):
        return lax.rem(s + i, n)

    def req_peer(i):
        return lax.rem(b + i, m)

    def greet_seq(i, _):
        signal({"seq": seq_peer(i)})
        return 0

    def greet_req(i, _):
        signal({"req": req_peer(i)})
        return 0

    def greet_w(i, _):
        @pl.when(jnp.logical_not(to_self & (i == b)))
        def _():
            signal({"req": i, "seq": w_place})

        @pl.when(jnp.logical_not((from_b == b) & (from_s + i == s)))
        def _():
            signal({"req": from_b, "seq": from_s + i})

        return 0

    lax.fori_loop(1, n, greet_seq, 0)
    lax.fori_loop(1, m, greet_req, 0)
    lax.fori_loop(0, m, greet_w, 0)
    pl.semaphore_wait(barrier, (n - 1) + (m - 1) + 2 * m - 2 * to_self.astype(jnp.int32))

    def remote(src, dst, send, recv, where):
        return pltpu.make_async_remote_copy(
            src_ref=src, dst_ref=dst, send_sem=send, recv_sem=recv, device_id=where, device_id_type=MESH
        )

    def over(count, peer, copy, me):
        def start(i, _):
            copy(peer(i), me).start()
            return 0

        def arrive(i, _):
            copy(peer(i), peer(i)).wait_recv()
            return 0

        def drain(i, _):
            copy(peer(i), me).wait_send()
            return 0

        return (
            lambda: lax.fori_loop(1, count, start, 0),
            lambda: lax.fori_loop(1, count, arrive, 0),
            lambda: lax.fori_loop(1, count, drain, 0),
        )

    def rows_copy(p, slot):
        return remote(rows_ref.at[p], rrecv.at[slot], rs_s.at[p], rs_r.at[slot], {"seq": p})

    def gather_copy(p, slot):
        return remote(ragg.at[b], ragg.at[slot], ag_s.at[p], ag_r.at[slot], {"req": p})

    def part_copy(p, slot):
        cols = pl.ds(pl.multiple_of(lax.rem(p, 2) * 256, 256), 256)
        return remote(part.at[p // 2, :, cols], precv.at[slot], pt_s.at[p], pt_r.at[slot], {"seq": p})

    def h1_copy(p, slot):
        return remote(h1.at[b], h1.at[slot], h1_s.at[p], h1_r.at[slot], {"req": p})

    def h2_copy(p, slot):
        return remote(h1, h2.at[slot // 2, lax.rem(slot, 2)], h2_s.at[p], h2_r.at[slot], {"seq": p})

    def m1_copy(p, slot):
        return remote(mx1.at[b], mx1.at[slot], m1_s.at[p], m1_r.at[slot], {"req": p})

    def m2_copy(p, slot):
        return remote(mx2.at[s], mx2.at[slot], m2_s.at[p], m2_r.at[slot], {"seq": p})

    sy, sz = s // 4, lax.rem(s, 4)

    def even(c):
        return c + 1 - 2 * lax.rem(c, 2)

    def odd(c):
        return 3 - c

    orders = []
    for v in range(4):
        first_is_z = v % 2 == 0
        near, far = (even, odd) if v < 2 else (odd, even)
        c, e = (sz, sy) if first_is_z else (sy, sz)
        orders.append((first_is_z, near, far, c, e))

    def spot_of(v, c, e):
        return e * 4 + c if orders[v][0] else c * 4 + e

    def block(v, c, e):
        cols = pl.ds(pl.multiple_of(spot_of(v, c, e) * width, width), width)
        return (slice(None), pl.ds(32 * v, 32), cols)

    def stage1(v, i, q):
        _, near, far, c, _ = orders[v]
        p = near(c)
        src = tails_ref.at[block(v, p if i == 0 else far(p), q)]
        _, _, _, _, e = orders[v]
        return remote(src, p1.at[v, i, q], p1_s.at[v, i, q], p1_r.at[v, i, q], {"seq": spot_of(v, p, e)})

    def stage2(v, q):
        _, _, far, c, e = orders[v]
        return remote(
            p1.at[v, 1, q], p2.at[v, q], p2_s.at[v, q], p2_r.at[v, q], {"seq": spot_of(v, far(c), e)}
        )

    def stage3(v, i):
        _, near, far, c, e = orders[v]
        p = near(e)
        src = p2.at[v, p if i == 0 else far(p)]
        return remote(src, p3.at[v, i], p3_s.at[v, i], p3_r.at[v, i], {"seq": spot_of(v, c, p)})

    def stage4(v):
        _, _, far, c, e = orders[v]
        return remote(p3.at[v, 1], p4.at[v], p4_s.at[v], p4_r.at[v], {"seq": spot_of(v, c, far(e))})

    def each(act, one):
        for v in range(4):
            for i in range(2):
                if act == 1:

                    def step(q, _):
                        one(stage1(v, i, q))
                        return 0

                    lax.fori_loop(0, 4, step, 0)
                elif act == 2 and i == 0:

                    def step(q, _):
                        one(stage2(v, q))
                        return 0

                    lax.fori_loop(0, 4, step, 0)
                elif act == 3:
                    one(stage3(v, i))
                elif act == 4 and i == 0:
                    one(stage4(v))

    go = lambda copy: copy.start()
    got = lambda copy: copy.wait_recv()
    sent = lambda copy: copy.wait_send()

    def add1():
        for v in range(4):
            _, _, far, c, _ = orders[v]
            for i in range(2):

                def step(q, _):
                    p1[v, i, q] = p1[v, i, q] + tails_ref[block(v, c if i == 0 else far(c), q)]
                    return 0

                lax.fori_loop(0, 4, step, 0)

    def add2():
        for v in range(4):
            p2[v] = p2[v] + p1[v, 0]

    def add3():
        for v in range(4):
            _, _, far, _, e = orders[v]
            p3[v, 0] = p3[v, 0] + p2[v, e]
            p3[v, 1] = p3[v, 1] + p2[v, far(e)]

    rows_go, rows_in, rows_out = over(n, seq_peer, rows_copy, s)
    ag_go, ag_in, ag_out = over(m, req_peer, gather_copy, b)
    part_go, part_in, part_out = over(n, seq_peer, part_copy, s)
    h1_go, h1_in, h1_out = over(m, req_peer, h1_copy, b)
    h2_go, h2_in, h2_out = over(n, seq_peer, h2_copy, s)
    m1_go, m1_in, m1_out = over(m, req_peer, m1_copy, b)
    m2_go, m2_in, m2_out = over(n, seq_peer, m2_copy, s)

    rows_go()

    def w_copy(p):
        cols = pl.ds(pl.multiple_of(p * depth, depth), depth)
        return remote(
            w_ref.at[:, cols], wbuf.at[w_slot], w_s.at[p], w_r.at[w_slot], {"req": p, "seq": w_place}
        )

    def w_start(i, _):
        p = lax.rem(b + i, m)

        @pl.when(jnp.logical_not(to_self & (p == b)))
        def _():
            w_copy(p).start()

        return 0

    lax.fori_loop(0, m, w_start, 0)

    @pl.when(to_self)
    def _():
        wbuf[w_slot] = w_ref[:, pl.ds(pl.multiple_of(b * depth, depth), depth)]

    rrecv[s] = rows_ref[s]
    each(1, go)
    rows_in()
    ragg[b] = jnp.sum(rrecv[...], axis=0)
    ag_go()
    ag_in()

    def w_arrive(i, _):
        @pl.when(jnp.logical_not((from_b == b) & (from_s + i == s)))
        def _():
            remote(
                w_ref.at[:, pl.ds(0, depth)], wbuf.at[i], w_s.at[i], w_r.at[i], {"req": i, "seq": w_place}
            ).wait_recv()

        return 0

    lax.fori_loop(0, m, w_arrive, 0)

    lhs = ragg[...].reshape(8 * m, 128).astype(BF16)
    weights = wbuf[...].reshape(m * 32, depth)
    place = lax.broadcasted_iota(jnp.int32, (8 * m, depth), 0)
    both = jnp.where(place % 8 < 4, dot(lhs, weights[0:128]), dot(lhs, weights[128:256]))
    both = both + pltpu.roll(both, 4, 0)
    part[...] = both.reshape(m, 8, depth)
    part_go()
    precv[s] = part[s // 2, :, pl.ds(pl.multiple_of(lax.rem(s, 2) * 256, 256), 256)]
    each(1, got)
    add1()
    each(2, go)
    part_in()
    cols = pl.ds(pl.multiple_of(b * depth + lax.rem(s, 2) * 256, 256), 256)
    resid = resid_ref[s // 2, :, cols].astype(F32)
    hidden = jnp.sum(precv[...], axis=0) + jnp.concatenate([resid, resid], axis=0)
    upper = pltpu.roll(hidden[:, 128:256], 4, 0)
    eight = lax.broadcasted_iota(jnp.int32, (8, 128), 0)
    h1[b] = jnp.where(eight < 4, upper, hidden[:, 0:128]).astype(BF16)
    h1_go()
    h1_in()
    h2_go()
    h2[s // 2, lax.rem(s, 2)] = h1[...]
    each(2, got)
    add2()
    each(3, go)
    h2_in()

    for k in range(m):
        for q in range(2):
            piece = h2[:, q, k].astype(F32).reshape(8 * m, 128)
            lo = k * depth + q * 256
            hf[:, lo : lo + 128] = piece
            hf[:, lo + 128 : lo + 256] = pltpu.roll(piece, 4, 0)
    h = hf[...]
    hid_ref[0] = hf[pl.ds(pl.multiple_of(b * 8, 8), 8), :].astype(BF16)[SEQS:]
    scale = lax.rsqrt(jnp.mean(h * h, axis=1, keepdims=True) + TINY_FLOOR)
    normed = (h * scale * gain_ref[...]).astype(BF16)
    load.wait()
    top = jnp.full((1, 8 * m), -jnp.inf, F32)
    chunk = 256
    for k in range(vbuf.shape[0] // chunk):
        logits = dot_nt(vbuf[k * chunk : (k + 1) * chunk, :], normed)
        top = jnp.maximum(top, jnp.max(logits, axis=0, keepdims=True))
    top = jnp.concatenate([top, top], axis=1)
    mx1[b] = jnp.broadcast_to(top, (8, 128))
    m1_go()
    each(3, got)
    add3()
    each(4, go)
    m1_in()
    mx2[s] = jnp.max(mx1[...], axis=0)
    m2_go()

    each(4, got)
    for v in range(4):
        p4[v] = p4[v] + p3[v, 0]
    for r in range(SEQS - 1):
        share = jnp.concatenate([p4[v, r].astype(F32) for v in range(4)], axis=0)
        fin_ref[r] = reach_ref[r] + share
    fin_ref[SEQS - 1] = reach_ref[SEQS - 1]
    m2_in()
    best = jnp.max(mx2[...], axis=0)[0:1]
    lanes = lax.broadcasted_iota(jnp.int32, (1, 128), 1)
    four = lax.broadcasted_iota(jnp.int32, (1, SEQS), 1)
    top = jnp.zeros((1, SEQS), F32)
    for r in range(SEQS):
        one = jnp.max(jnp.where(lanes == b * 8 + SEQS + r, best, -jnp.inf), axis=1, keepdims=True)
        top = jnp.where(four == r, one, top)
    max_ref[...] = top

    for drain in (rows_out, ag_out, part_out, h1_out, h2_out, m1_out, m2_out):
        drain()

    def w_drain(p, _):
        @pl.when(jnp.logical_not(to_self & (p == b)))
        def _():
            w_copy(p).wait_send()

        return 0

    lax.fori_loop(0, m, w_drain, 0)

    for act in range(1, 5):
        each(act, sent)


def tail(rows, out_weight, tails, reached, resid, gain, vocab, n, m):
    width = D // n
    vmem = pl.BlockSpec(memory_space=pltpu.VMEM)
    dma = pltpu.SemaphoreType.DMA
    return pl.pallas_call(
        functools.partial(tail_kernel, n, m),
        in_specs=[vmem] * 6 + [pl.BlockSpec(memory_space=pl.ANY)],
        out_specs=[vmem] * 3,
        out_shape=[
            jax.ShapeDtypeStruct((1, SEQS, D), BF16),
            jax.ShapeDtypeStruct((1, SEQS), F32),
            jax.ShapeDtypeStruct((SEQS, STATE, width), F32),
        ],
        scratch_shapes=[
            pltpu.VMEM(vocab.shape, BF16),
            pltpu.VMEM((n, 8, 128), F32),
            pltpu.VMEM((m, 8, 128), F32),
            pltpu.VMEM((m, 32, D // m), BF16),
            pltpu.VMEM((m, 8, D // m), F32),
            pltpu.VMEM((n, 8, 256), F32),
            pltpu.VMEM((m, 8, 128), BF16),
            pltpu.VMEM((n // 2, 2, m, 8, 128), BF16),
            pltpu.VMEM((8 * m, D), F32),
            pltpu.VMEM((m, 8, 128), F32),
            pltpu.VMEM((n, 8, 128), F32),
            pltpu.VMEM((4, 2, 4, SEQS - 1, 32, width), BF16),
            pltpu.VMEM((4, 4, SEQS - 1, 32, width), BF16),
            pltpu.VMEM((4, 2, SEQS - 1, 32, width), BF16),
            pltpu.VMEM((4, SEQS - 1, 32, width), BF16),
            dma,
            dma((n,)),
            dma((n,)),
            dma((m,)),
            dma((m,)),
            dma((m,)),
            dma((m,)),
            dma((n,)),
            dma((n,)),
            dma((m,)),
            dma((m,)),
            dma((n,)),
            dma((n,)),
            dma((m,)),
            dma((m,)),
            dma((n,)),
            dma((n,)),
            dma((4, 2, 4)),
            dma((4, 2, 4)),
            dma((4, 4)),
            dma((4, 4)),
            dma((4, 2)),
            dma((4, 2)),
            dma((4,)),
            dma((4,)),
        ],
        compiler_params=pltpu.CompilerParams(
            collective_id=1, has_side_effects=True, vmem_limit_bytes=VMEM_LIMIT
        ),
        name="tail",
    )(rows, out_weight, tails, reached, resid, gain, vocab)


def pack_kernel(fin_ref, hid_ref, top_ref, fin_out, hid_out, top_out):
    for r in range(SEQS):
        fin_out[r] = fin_ref[r].T
    hid_out[...] = hid_ref[...]
    top_out[...] = top_ref[...]


def pack(final, hid, top):
    vmem = pl.BlockSpec(memory_space=pltpu.VMEM)
    return pl.pallas_call(
        pack_kernel,
        in_specs=[vmem] * 3,
        out_specs=[vmem] * 3,
        out_shape=[
            jax.ShapeDtypeStruct((final.shape[0], final.shape[2], final.shape[1]), F32),
            jax.ShapeDtypeStruct(hid.shape, BF16),
            jax.ShapeDtypeStruct(top.shape, F32),
        ],
        name="pack",
    )(final, hid, top)


def body(
    conv_input,
    gate_projected,
    step_raw,
    step_bias,
    decay_log,
    head_direct_gain,
    conv_weight,
    convolution_bias,
    norm_weight,
    lengths,
    out_weight,
    residual_last,
    final_gain,
    vocab_weight,
):
    seq_count = lax.axis_size("seq")
    req_count = lax.axis_size("req")
    conv = conv_input[0]
    halo = halo_rows(conv, seq_count)
    y, states, tails, aux, c, lead = local_pass(
        lengths,
        conv,
        halo,
        conv_weight,
        convolution_bias[None],
        step_raw[0].T,
        step_bias[None],
        decay_log[None],
        head_direct_gain[None],
    )
    entering, reached = exchange(states, aux, seq_count)
    gated, rows = finish(lengths, y, c, entering, lead, gate_projected[0], norm_weight[None])
    hid, top, final = tail(
        rows, out_weight, tails, reached, residual_last, final_gain[None], vocab_weight, seq_count, req_count
    )
    final, hid, top = pack(final, hid, top)
    final_states = final.reshape(SEQS, HEADS // seq_count, CHANNEL_WIDTH, STATE)[None]
    return (gated[None], final_states, hid, top)


def solution(mesh):
    return jax.shard_map(
        body,
        mesh=mesh,
        in_specs=(
            P("req", "seq", None),
            P("req", "seq", None),
            P("req", "seq", None),
            P(),
            P(),
            P(),
            P(),
            P(),
            P(),
            P("req", None),
            P(("req", "seq"), None),
            P(),
            P(),
            P(("req", "seq"), None),
        ),
        out_specs=(
            P("req", "seq", None),
            P("req", None, "seq", None, None),
            P("req", None, None),
            P("req", None),
        ),
        check_vma=False,
    )
```

```python
import functools

import jax
import jax.numpy as jnp
from jax import lax
from jax.experimental import pallas as pl
from jax.experimental.pallas import tpu as pltpu
from jax.sharding import PartitionSpec as P

D = 4096
HEADS = 64
CHANNEL_WIDTH = 64
GROUPS = 4
STATE = 128
CHUNKS = [slice(c * 256, c * 256 + 256) for c in range(4)]
KERNEL = 4
BLOCK = 256
SEQS = 4
PER_GROUP = HEADS // GROUPS
GW = PER_GROUP * CHANNEL_WIDTH
TINY_FLOOR = 1e-05
LOG2E = 1.4426950408889634
MESH = pl.DeviceIdType.MESH
F32 = jnp.float32
BF16 = jnp.bfloat16
VMEM_LIMIT = 60 * 1024 * 1024


def dot(a, b):
    return lax.dot_general(a, b, (((1,), (0,)), ((), ())), preferred_element_type=F32)


def dot_nt(a, b):
    return lax.dot_general(a, b, (((1,), (1,)), ((), ())), preferred_element_type=F32)


def split2(x):
    hi = x.astype(BF16)
    return hi, (x - hi.astype(F32)).astype(BF16)


def split3(x):
    hi = x.astype(BF16)
    rest = x - hi.astype(F32)
    mid = rest.astype(BF16)
    return hi, mid, (rest - mid.astype(F32)).astype(BF16)


def seg_of(place, b1, b2, b3):
    one = lambda b: (place >= b).astype(jnp.int32)
    return one(b1) + one(b2) + one(b3)


def spread_matrix():
    lane = lax.broadcasted_iota(jnp.int32, (128, GW), 0)
    col = lax.broadcasted_iota(jnp.int32, (128, GW), 1)
    hit = (lane < 48) & (lane % PER_GROUP == col // CHANNEL_WIDTH)
    return jnp.where(hit, 1.0, 0.0).astype(BF16)


def spread_parts(v):
    hi, mid, lo = split3(v)
    lane = lax.broadcasted_iota(jnp.int32, v.shape, 1)
    parts = jnp.where(
        lane < 16, hi.astype(F32), jnp.where(lane < 32, mid.astype(F32), lo.astype(F32))
    ).astype(BF16)
    return parts


def spread(v, spread_ref):
    return dot(spread_parts(v), spread_ref[...])


def halves(h):
    return h + h * jnp.tanh(h)


def softplus(x):
    e = jnp.exp(-jnp.abs(x))
    w = 1.0 + e
    d = w - 1.0
    return jnp.maximum(x, 0.0) + jnp.where(d == 0.0, e, jnp.log(w) * (e / jnp.where(d == 0.0, 1.0, d)))


def bounds_of(len_ref):
    b1 = len_ref[0, 0]
    b2 = b1 + len_ref[0, 1]
    return b1, b2, b2 + len_ref[0, 2]


def local_kernel(
    len_ref,
    x_ref,
    b_ref,
    c_ref,
    xh_ref,
    bh_ref,
    ch_ref,
    wx_ref,
    wb_ref,
    wc_ref,
    vx_ref,
    vb_ref,
    vc_ref,
    raw_ref,
    bias_ref,
    log_ref,
    gain_ref,
    y_ref,
    st_ref,
    pt_ref,
    aux_ref,
    co_ref,
    ld_ref,
    xb_ref,
    sc_ref,
    cum_ref,
    rt_ref,
    dx_ref,
    xext,
    xf,
    s0,
    c0,
    cumr,
    sp,
    msk,
    alw,
    sgs,
    cums,
    lds,
    wst,
    ow,
):
    g = pl.program_id(0)
    j = pl.program_id(1)
    span = pl.num_programs(1) * BLOCK
    first = lax.axis_index("seq") * span
    b1, b2, b3 = bounds_of(len_ref)
    bounds = (b1, b2, b3)
    start = first + j * BLOCK

    @pl.when((g == 0) & (j == 0))
    def _():
        sp[...] = spread_matrix()

    row = lax.broadcasted_iota(jnp.int32, (BLOCK, 128), 0) + start

    @pl.when(g == 0)
    def _():
        near = jnp.full((BLOCK, 128), 8, jnp.int32)
        for bound in bounds:
            gap = row - bound
            near = jnp.where(gap >= 0, jnp.minimum(near, gap), near)
        for k in range(3):
            msk[j, k] = (near >= 3 - k).astype(F32)
        sgs[j] = seg_of(row, b1, b2, b3)
        i0 = lax.broadcasted_iota(jnp.int32, (BLOCK, BLOCK), 0)
        i1 = lax.broadcasted_iota(jnp.int32, (BLOCK, BLOCK), 1)
        t_seg = seg_of(i0 + start, b1, b2, b3)
        s_seg = seg_of(i1 + start, b1, b2, b3)
        alw[j] = ((i0 >= i1) & (t_seg == s_seg)).astype(F32)
        tri = jnp.where(i0 >= i1, 1.0, 0.0).astype(BF16)
        dt = softplus(raw_ref[...].T + bias_ref[...])
        dh, dm, dl = split3(dt * (jnp.exp(log_ref[...]) * -LOG2E))
        cums[j] = (dot(tri, dl) + dot(tri, dm)) + dot(tri, dh)
        lds[j] = jnp.log(dt) * LOG2E

    l0 = lax.broadcasted_iota(jnp.int32, (HEADS, 128), 0)
    l1 = lax.broadcasted_iota(jnp.int32, (HEADS, 128), 1)
    pick = jnp.where(l0 == g * PER_GROUP + l1 % PER_GROUP, 1.0, 0.0).astype(BF16)
    t0 = lax.broadcasted_iota(jnp.int32, (PER_GROUP, HEADS), 0)
    t1 = lax.broadcasted_iota(jnp.int32, (PER_GROUP, HEADS), 1)
    pickt = jnp.where(t1 == g * PER_GROUP + t0, 1.0, 0.0).astype(BF16)

    def group(v):
        hi, mid, lo = split3(v)
        return (dot(lo, pick) + dot(mid, pick)) + dot(hi, pick)

    @pl.when(j == 0)
    def _():
        xext[0:8, 0:GW] = xh_ref[...].astype(F32)
        xext[0:8, GW : GW + 128] = bh_ref[...].astype(F32)
        xext[0:8, GW + 128 : GW + 256] = ch_ref[...].astype(F32)
        for lo, hi, w_ref, v_ref in (
            (0, GW, wx_ref, vx_ref),
            (GW, GW + 128, wb_ref, vb_ref),
            (GW + 128, GW + 256, wc_ref, vc_ref),
        ):
            wst[0:KERNEL, lo:hi] = w_ref[...] * 0.5
            wst[KERNEL : KERNEL + 1, lo:hi] = v_ref[...] * 0.5
        pt_ref[...] = jnp.zeros_like(pt_ref)
        aux_ref[...] = jnp.zeros_like(aux_ref)
        c0[...] = jnp.zeros_like(c0)
        dx_ref[...] = spread(group(jnp.broadcast_to(gain_ref[...], (8, HEADS))), sp)

    @pl.when(j == 1)
    def _():
        xext[0:8, :] = xext[BLOCK : BLOCK + 8, :]

    xext[8 : BLOCK + 8, 0:GW] = x_ref[...].astype(F32)
    xext[8 : BLOCK + 8, GW : GW + 128] = b_ref[...].astype(F32)
    xext[8 : BLOCK + 8, GW + 128 : GW + 256] = c_ref[...].astype(F32)

    tile = 64

    def convolve(c, _):
        cols = pl.ds(pl.multiple_of(c * 128, 128), 128)
        w = [wst[k : k + 1, cols] for k in range(KERNEL)]
        bias = wst[KERNEL : KERNEL + 1, cols]
        for lo in range(0, BLOCK, tile):
            total = jnp.broadcast_to(bias, (tile, 128))
            for k in range(3):
                total = total + w[k] * xext[lo + 5 + k : lo + 5 + k + tile, cols] * msk[j, k, lo : lo + tile]
            total = total + w[3] * xext[lo + 8 : lo + 8 + tile, cols]
            xf[lo : lo + tile, cols] = halves(total)
        return 0

    lax.fori_loop(0, 10, convolve, 0)

    seg = sgs[j]
    bf = xf[:, GW : GW + 128]
    cb = xf[:, GW + 128 : GW + 256].astype(BF16)
    co_ref[...] = cb

    cum = group(cums[j])
    logdt = group(lds[j])
    rh, rm, rl = split3(lds[j] - cums[j])
    rt = (dot_nt(pickt, rl) + dot_nt(pickt, rm)) + dot_nt(pickt, rh)
    cumr[...] = cum
    last = cum[BLOCK - 1 : BLOCK, :]

    seg_before_span = seg_of(first - 1, b1, b2, b3)
    seg_before = seg_of(start - 1, b1, b2, b3)
    seg_end = seg_of(start + BLOCK - 1, b1, b2, b3)
    prior = c0[0:1, :]
    ld_ref[0, 0] = jnp.where(seg == seg_before_span, jnp.exp2(cum + prior), 0.0)

    bh, bl = split2(bf)
    sc = dot_nt(cb, bh) * alw[j]

    xb_ref[0] = xf[:, 0:GW].astype(BF16)
    sc_ref[0] = sc
    cum_ref[0] = cum
    rt_ref[0] = rt

    @pl.when(j == 1)
    def _():
        lead = jnp.where(seg == seg_before, jnp.exp2(cum), 0.0)
        sh, sl = split2(s0[...])
        parts = spread_parts(lead)
        for cols in CHUNKS:
            y_ref[:, cols] = dot(parts, sp[:, cols]) * (dot(cb, sh[:, cols]) + dot(cb, sl[:, cols]))

    both = jnp.concatenate(split2(bf.T), axis=0)

    def state_of(weights, put):
        parts = spread_parts(weights)
        for cols in CHUNKS:
            xs = (xf[:, cols] * dot(parts, sp[:, cols])).astype(BF16)
            two = dot(both, xs)
            put(cols, two[:STATE] + two[STATE:])

    def at_end(seg_e):
        return jnp.where(seg == seg_e, jnp.exp2(last - cum + logdt), 0.0)

    def put_own(cols, value):
        ow[:, cols] = value

    state_of(at_end(seg_end), put_own)

    for r in range(SEQS - 1):
        end = bounds[r] - 1
        local = end - start
        owned = (local >= 0) & (local < BLOCK)

        @pl.when(owned)
        def _():
            ce = cumr[pl.ds(jnp.clip(local, 0, BLOCK - 1), 1), :]
            inside = (row <= end) & (seg == r)
            w = jnp.exp2(jnp.where(inside, ce - cum + logdt, -1e30))
            reach = jnp.where(seg_before == r, jnp.exp2(ce), 0.0)
            reach8 = spread(jnp.broadcast_to(reach, (8, 128)), sp)

            def put_tail(cols, value):
                before = jnp.where(j == 1, reach8[0:1, cols] * s0[:, cols], 0.0)
                pt_ref[r, :, cols] = (value + before).astype(BF16)

            state_of(w, put_tail)
            full = jnp.where(seg_before_span == r, jnp.exp2(ce + prior), 0.0)
            aux_ref[1 + r : 2 + r, :] = spread(jnp.broadcast_to(full, (8, 128)), sp)[0:1]

    @pl.when(j == 0)
    def _():
        s0[...] = ow[...]
        c0[...] = jnp.broadcast_to(last, c0.shape)

    @pl.when(j == 1)
    def _():
        carry = jnp.where(seg_end == seg_before, jnp.exp2(last), 0.0)
        whole = jnp.where(seg_end == seg_before_span, jnp.exp2(last + prior), 0.0)
        carry8 = spread(jnp.broadcast_to(carry, (8, 128)), sp)
        whole8 = spread(jnp.broadcast_to(whole, (8, 128)), sp)
        st_ref[...] = (carry8[0:1] * s0[...] + ow[...]).astype(BF16)
        aux_ref[0:1, :] = whole8[0:1]


def local_pass(lengths, conv, halo, conv_weight, conv_bias, raw, bias, log, gain):
    length = conv.shape[0]
    blocks = length // BLOCK
    maps = D // 128
    grid = (GROUPS, blocks)
    xs = lambda rows: [
        pl.BlockSpec((rows, GW), lambda g, j: (0, g)),
        pl.BlockSpec((rows, 128), lambda g, j: (0, maps + g)),
        pl.BlockSpec((rows, 128), lambda g, j: (0, maps + GROUPS + g)),
    ]
    in_specs = (
        [
            pl.BlockSpec(memory_space=pltpu.SMEM),
            pl.BlockSpec((BLOCK, GW), lambda g, j: (j, g)),
            pl.BlockSpec((BLOCK, 128), lambda g, j: (j, maps + g)),
            pl.BlockSpec((BLOCK, 128), lambda g, j: (j, maps + GROUPS + g)),
        ]
        + xs(8)
        + xs(KERNEL)
        + xs(1)
        + [
            pl.BlockSpec((HEADS, BLOCK), lambda g, j: (0, j)),
            pl.BlockSpec((1, HEADS), lambda g, j: (0, 0)),
            pl.BlockSpec((1, HEADS), lambda g, j: (0, 0)),
            pl.BlockSpec((1, HEADS), lambda g, j: (0, 0)),
        ]
    )
    each = lambda *shape: pl.BlockSpec((1,) + shape, lambda g, j: (g * blocks + j, 0, 0))
    out_specs = [
        pl.BlockSpec((BLOCK, GW), lambda g, j: (0, g)),
        pl.BlockSpec((STATE, GW), lambda g, j: (0, g)),
        pl.BlockSpec((SEQS - 1, STATE, GW), lambda g, j: (0, 0, g)),
        pl.BlockSpec((8, GW), lambda g, j: (0, g)),
        pl.BlockSpec((BLOCK, 128), lambda g, j: (j, g)),
        pl.BlockSpec((1, 1, BLOCK, 128), lambda g, j: (g, j, 0, 0)),
        each(BLOCK, GW),
        each(BLOCK, BLOCK),
        each(BLOCK, 128),
        each(PER_GROUP, BLOCK),
        pl.BlockSpec((8, GW), lambda g, j: (0, g)),
    ]
    steps = GROUPS * blocks
    out_shape = [
        jax.ShapeDtypeStruct((BLOCK, D), F32),
        jax.ShapeDtypeStruct((STATE, D), BF16),
        jax.ShapeDtypeStruct((SEQS - 1, STATE, D), BF16),
        jax.ShapeDtypeStruct((8, D), F32),
        jax.ShapeDtypeStruct((length, GROUPS * STATE), BF16),
        jax.ShapeDtypeStruct((GROUPS, blocks, BLOCK, 128), F32),
        jax.ShapeDtypeStruct((steps, BLOCK, GW), BF16),
        jax.ShapeDtypeStruct((steps, BLOCK, BLOCK), F32),
        jax.ShapeDtypeStruct((steps, BLOCK, 128), F32),
        jax.ShapeDtypeStruct((steps, PER_GROUP, BLOCK), F32),
        jax.ShapeDtypeStruct((8, D), F32),
    ]
    return pl.pallas_call(
        local_kernel,
        grid=grid,
        in_specs=in_specs,
        out_specs=out_specs,
        out_shape=out_shape,
        scratch_shapes=[
            pltpu.VMEM((BLOCK + 8, GW + 256), F32),
            pltpu.VMEM((BLOCK, GW + 256), F32),
            pltpu.VMEM((STATE, GW), F32),
            pltpu.VMEM((8, 128), F32),
            pltpu.VMEM((BLOCK, 128), F32),
            pltpu.VMEM((128, GW), BF16),
            pltpu.VMEM((blocks, 3, BLOCK, 128), F32),
            pltpu.VMEM((blocks, BLOCK, BLOCK), F32),
            pltpu.VMEM((blocks, BLOCK, 128), jnp.int32),
            pltpu.VMEM((blocks, BLOCK, HEADS), F32),
            pltpu.VMEM((blocks, BLOCK, HEADS), F32),
            pltpu.VMEM((8, GW + 256), F32),
            pltpu.VMEM((STATE, GW), F32),
        ],
        compiler_params=pltpu.CompilerParams(
            vmem_limit_bytes=VMEM_LIMIT, dimension_semantics=("arbitrary", "arbitrary")
        ),
        name="local_pass",
    )(
        lengths, conv, conv, conv, halo, halo, halo, conv_weight, conv_weight, conv_weight,
        conv_bias, conv_bias, conv_bias, raw, bias, log, gain,
    )


def halo_kernel(n, conv_ref, out_ref, got, send, recv):
    me = lax.axis_index("seq")
    right = lax.rem(me + 1, n)
    left = lax.rem(me + n - 1, n)
    barrier = pltpu.get_barrier_semaphore()
    for p in (left, right):
        pl.semaphore_signal(barrier, inc=1, device_id={"seq": p}, device_id_type=MESH)
    pl.semaphore_wait(barrier, 2)
    copy = pltpu.make_async_remote_copy(
        src_ref=conv_ref.at[pl.ds(conv_ref.shape[0] - 8, 8), :],
        dst_ref=got,
        send_sem=send,
        recv_sem=recv,
        device_id={"seq": right},
        device_id_type=MESH,
    )
    copy.start()
    copy.wait()
    keep = jnp.where(me == 0, 0.0, 1.0)
    out_ref[...] = (got[...].astype(F32) * keep).astype(BF16)


def halo_rows(conv, n):
    shape = (8, conv.shape[1])
    return pl.pallas_call(
        functools.partial(halo_kernel, n),
        in_specs=[pl.BlockSpec(memory_space=pl.ANY)],
        out_specs=pl.BlockSpec(memory_space=pltpu.VMEM),
        out_shape=jax.ShapeDtypeStruct(shape, BF16),
        scratch_shapes=[
            pltpu.VMEM(shape, BF16),
            pltpu.SemaphoreType.DMA,
            pltpu.SemaphoreType.DMA,
        ],
        compiler_params=pltpu.CompilerParams(collective_id=2, has_side_effects=True),
        name="halo",
    )(conv)


def exchange_kernel(
    n,
    st_ref,
    aux_ref,
    dx_ref,
    xb_ref,
    sc_ref,
    cum_ref,
    rt_ref,
    ent_ref,
    fin_ref,
    y_ref,
    rs,
    ra,
    eb,
    xbv,
    scv,
    cumv,
    rtv,
    yv,
    send1,
    recv1,
    send2,
    recv2,
    send3,
    recv3,
    lsem,
    ysem,
):
    me = lax.axis_index("seq")
    steps = xb_ref.shape[0]

    def loads(k):
        pairs = ((xb_ref, xbv), (sc_ref, scv), (cum_ref, cumv), (rt_ref, rtv))
        return [pltpu.make_async_copy(a.at[k], v.at[k], lsem.at[k, i]) for i, (a, v) in enumerate(pairs)]

    def store(k):
        return pltpu.make_async_copy(yv.at[k], y_ref.at[k], ysem.at[k])

    def fetch(k, _):
        for copy in loads(k):
            copy.start()
        return 0

    lax.fori_loop(0, steps, fetch, 0)
    width = D // n
    barrier = pltpu.get_barrier_semaphore()

    def peer(i):
        return lax.rem(me + i, n)

    def cols(p):
        return pl.ds(pl.multiple_of(p * width, width), width)

    def greet(i, _):
        pl.semaphore_signal(barrier, inc=1, device_id={"seq": peer(i)}, device_id_type=MESH)
        return 0

    lax.fori_loop(1, n, greet, 0)
    pl.semaphore_wait(barrier, n - 1)

    def out(p, slot):
        return (
            pltpu.make_async_remote_copy(
                src_ref=st_ref.at[:, cols(p)],
                dst_ref=rs.at[slot],
                send_sem=send1.at[p],
                recv_sem=recv1.at[slot],
                device_id={"seq": p},
                device_id_type=MESH,
            ),
            pltpu.make_async_remote_copy(
                src_ref=aux_ref.at[:, cols(p)],
                dst_ref=ra.at[slot],
                send_sem=send2.at[p],
                recv_sem=recv2.at[slot],
                device_id={"seq": p},
                device_id_type=MESH,
            ),
        )

    def back(p, slot):
        return pltpu.make_async_remote_copy(
            src_ref=eb.at[p],
            dst_ref=ent_ref.at[:, cols(slot)],
            send_sem=send3.at[p],
            recv_sem=recv3.at[slot],
            device_id={"seq": p},
            device_id_type=MESH,
        )

    def begin(i, _):
        for copy in out(peer(i), me):
            copy.start()
        return 0

    lax.fori_loop(1, n, begin, 0)
    rs[me] = st_ref[:, cols(me)]
    ra[me] = aux_ref[:, cols(me)]

    lane = lax.broadcasted_iota(jnp.int32, (BLOCK, 128), 1)
    half = BLOCK // 2

    def mix(k, _):
        for copy in loads(k):
            copy.wait()
        sc_t = scv[k, :half, :half]
        sc_l = scv[k, half:, :half]
        sc_r = scv[k, half:, half:]
        for pair in range(PER_GROUP // 2):
            span = slice(pair * 128, pair * 128 + 128)
            xb = xbv[k, :, span]
            res = []
            for h in (2 * pair, 2 * pair + 1):
                col = cumv[k, :, h : h + 1]
                r = rtv[k, h : h + 1, :]
                top = jnp.exp2(jnp.minimum(col[:half] + r[:, :half], 100.0)) * sc_t
                left = jnp.exp2(col[half:] + r[:, :half]) * sc_l
                right = jnp.exp2(jnp.minimum(col[half:] + r[:, half:], 100.0)) * sc_r
                bottom = jnp.concatenate([left.astype(BF16), right.astype(BF16)], axis=1)
                res.append(jnp.concatenate([dot(top.astype(BF16), xb[:half]), dot(bottom, xb)], axis=0))
            intra = jnp.where(lane < CHANNEL_WIDTH, res[0], res[1])
            direct = dx_ref[0:1, pl.ds(pl.multiple_of(k // 2 * GW + pair * 128, 128), 128)]
            yv[k, :, span] = intra + direct * xb.astype(F32)
        store(k).start()
        return 0

    lax.fori_loop(0, steps, mix, 0)
    fin_ref[...] = jnp.zeros_like(fin_ref)

    def scan(d, _):
        @pl.when(d != me)
        def _():
            for copy in out(d, d):
                copy.wait_recv()

        now = fin_ref[SEQS - 1]
        eb[d] = now.astype(BF16)

        @pl.when(d != me)
        def _():
            back(d, me).start()

        for r in range(SEQS - 1):
            fin_ref[r] = fin_ref[r] + ra[d, 1 + r : 2 + r, :] * now
        fin_ref[SEQS - 1] = ra[d, 0:1, :] * now + rs[d].astype(F32)
        return 0

    lax.fori_loop(0, n, scan, 0)
    ent_ref[:, cols(me)] = eb[me]

    def done(i, _):
        back(peer(i), peer(i)).wait_recv()
        return 0

    lax.fori_loop(1, n, done, 0)

    def drain(i, _):
        for copy in out(peer(i), me):
            copy.wait_send()
        back(peer(i), me).wait_send()
        return 0

    lax.fori_loop(1, n, drain, 0)

    def stored(k, _):
        store(k).wait()
        return 0

    lax.fori_loop(0, steps, stored, 0)


def exchange(states, aux, dx, xb, sc, cum, rt, n):
    width = D // n
    steps = xb.shape[0]
    far = pl.BlockSpec(memory_space=pl.ANY)
    vmem = pl.BlockSpec(memory_space=pltpu.VMEM)
    return pl.pallas_call(
        functools.partial(exchange_kernel, n),
        in_specs=[vmem] * 3 + [far] * 4,
        out_specs=[vmem, vmem, far],
        out_shape=[
            jax.ShapeDtypeStruct((STATE, D), BF16),
            jax.ShapeDtypeStruct((SEQS, STATE, width), F32),
            jax.ShapeDtypeStruct((steps, BLOCK, GW), F32),
        ],
        scratch_shapes=[
            pltpu.VMEM((n, STATE, width), BF16),
            pltpu.VMEM((n, 8, width), F32),
            pltpu.VMEM((n, STATE, width), BF16),
            pltpu.VMEM(xb.shape, BF16),
            pltpu.VMEM(sc.shape, F32),
            pltpu.VMEM(cum.shape, F32),
            pltpu.VMEM(rt.shape, F32),
            pltpu.VMEM((steps, BLOCK, GW), F32),
        ]
        + [pltpu.SemaphoreType.DMA((n,)) for _ in range(6)]
        + [pltpu.SemaphoreType.DMA((steps, 4)), pltpu.SemaphoreType.DMA((steps,))],
        compiler_params=pltpu.CompilerParams(
            collective_id=0, has_side_effects=True, vmem_limit_bytes=VMEM_LIMIT
        ),
        name="exchange",
    )(states, aux, dx, xb, sc, cum, rt)


def finish_kernel(len_ref, y_ref, yb_ref, c_ref, e_ref, ld_ref, gate_ref, nw_ref, out_ref, rows_ref, sp, of, scales):
    g = pl.program_id(0)
    j = pl.program_id(1)

    @pl.when((g == 0) & (j == 0))
    def _():
        sp[...] = spread_matrix()

    @pl.when(j == 0)
    def _():
        rows_ref[...] = jnp.zeros_like(rows_ref)

    parts = spread_parts(ld_ref[0, 0])
    later = (j > 0).astype(F32)
    half = BLOCK // 2
    for lines in (slice(0, half), slice(half, BLOCK)):
        total = jnp.zeros((half, 128), F32)
        for cols in CHUNKS:
            v = y_ref[0, lines, cols] + later * yb_ref[lines, cols]
            v = v + dot(parts[lines], sp[:, cols]) * dot(c_ref[lines, :], e_ref[:, cols])
            v = v * halves(0.5 * gate_ref[lines, cols].astype(F32))
            of[lines, cols] = v
            total = total + v[:, :128] * v[:, :128] + v[:, 128:] * v[:, 128:]
        scale = lax.rsqrt(jnp.sum(total, axis=1, keepdims=True) * (1.0 / GW) + TINY_FLOOR)
        scales[lines, :] = jnp.broadcast_to(scale, (half, 128))
        for cols in CHUNKS:
            out_ref[lines, cols] = (of[lines, cols] * scale * nw_ref[:, cols]).astype(BF16)

    start = lax.axis_index("seq") * (pl.num_programs(1) * BLOCK) + j * BLOCK
    bounds = bounds_of(len_ref)
    for r, bound in enumerate(bounds + (bounds[2] + len_ref[0, 3],)):
        local = bound - 1 - start

        @pl.when((local >= 0) & (local < BLOCK))
        def _():
            spot = jnp.clip(local, 0, BLOCK - 1)
            line = of[pl.ds(spot, 1), :] * scales[pl.ds(spot, 1), :][:, 0:1] * nw_ref[...]
            line = line.astype(BF16).astype(F32)
            for c in range(GW // 128):
                place = c % 2 * SEQS + r
                rows_ref[c // 2, place : place + 1, :] = line[:, c * 128 : c * 128 + 128]


def finish(lengths, y, yb, c, entering, lead, gate, norm_weight):
    length = gate.shape[0]
    blocks = length // BLOCK
    block = lambda width: pl.BlockSpec((BLOCK, width), lambda g, j: (j, g))
    return pl.pallas_call(
        finish_kernel,
        grid=(GROUPS, length // BLOCK),
        in_specs=[
            pl.BlockSpec(memory_space=pltpu.SMEM),
            pl.BlockSpec((1, BLOCK, GW), lambda g, j: (g * blocks + j, 0, 0)),
            pl.BlockSpec((BLOCK, GW), lambda g, j: (0, g)),
            block(STATE),
            pl.BlockSpec((STATE, GW), lambda g, j: (0, g)),
            pl.BlockSpec((1, 1, BLOCK, 128), lambda g, j: (g, j, 0, 0)),
            block(GW),
            pl.BlockSpec((1, GW), lambda g, j: (0, g)),
        ],
        out_specs=[block(GW), pl.BlockSpec((GW // 256, 8, 128), lambda g, j: (g, 0, 0))],
        out_shape=[
            jax.ShapeDtypeStruct((length, D), BF16),
            jax.ShapeDtypeStruct((D // 256, 8, 128), F32),
        ],
        scratch_shapes=[
            pltpu.VMEM((128, GW), BF16),
            pltpu.VMEM((BLOCK, GW), F32),
            pltpu.VMEM((BLOCK, 128), F32),
        ],
        compiler_params=pltpu.CompilerParams(
            vmem_limit_bytes=VMEM_LIMIT, dimension_semantics=("arbitrary", "arbitrary")
        ),
        name="finish",
    )(lengths, y, yb, c, entering, lead, gate, norm_weight)


def tail_kernel(
    n,
    m,
    rows_ref,
    w_ref,
    tails_ref,
    reach_ref,
    resid_ref,
    gain_ref,
    vocab_ref,
    hid_ref,
    max_ref,
    fin_ref,
    vbuf,
    rrecv,
    ragg,
    wbuf,
    part,
    precv,
    h1,
    h2,
    hf,
    mx1,
    mx2,
    p1,
    p2,
    p3,
    p4,
    vsem,
    rs_s,
    rs_r,
    ag_s,
    ag_r,
    w_s,
    w_r,
    pt_s,
    pt_r,
    h1_s,
    h1_r,
    h2_s,
    h2_r,
    m1_s,
    m1_r,
    m2_s,
    m2_r,
    p1_s,
    p1_r,
    p2_s,
    p2_r,
    p3_s,
    p3_r,
    p4_s,
    p4_r,
):
    s = lax.axis_index("seq")
    b = lax.axis_index("req")
    width = D // n
    depth = D // m
    w_place = 2 * b + s // 8
    w_slot = lax.rem(s, 8)
    to_self = w_place == s
    from_b = s // 2
    from_s = 8 * lax.rem(s, 2)

    load = pltpu.make_async_copy(vocab_ref, vbuf, vsem)
    load.start()

    barrier = pltpu.get_barrier_semaphore()

    def signal(where):
        pl.semaphore_signal(barrier, inc=1, device_id=where, device_id_type=MESH)

    def seq_peer(i):
        return lax.rem(s + i, n)

    def req_peer(i):
        return lax.rem(b + i, m)

    def greet_seq(i, _):
        signal({"seq": seq_peer(i)})
        return 0

    def greet_req(i, _):
        signal({"req": req_peer(i)})
        return 0

    def greet_w(i, _):
        @pl.when(jnp.logical_not(to_self & (i == b)))
        def _():
            signal({"req": i, "seq": w_place})

        @pl.when(jnp.logical_not((from_b == b) & (from_s + i == s)))
        def _():
            signal({"req": from_b, "seq": from_s + i})

        return 0

    lax.fori_loop(1, n, greet_seq, 0)
    lax.fori_loop(1, m, greet_req, 0)
    lax.fori_loop(0, m, greet_w, 0)
    pl.semaphore_wait(barrier, (n - 1) + (m - 1) + 2 * m - 2 * to_self.astype(jnp.int32))

    def remote(src, dst, send, recv, where):
        return pltpu.make_async_remote_copy(
            src_ref=src, dst_ref=dst, send_sem=send, recv_sem=recv, device_id=where, device_id_type=MESH
        )

    def over(count, peer, copy, me):
        def start(i, _):
            copy(peer(i), me).start()
            return 0

        def arrive(i, _):
            copy(peer(i), peer(i)).wait_recv()
            return 0

        def drain(i, _):
            copy(peer(i), me).wait_send()
            return 0

        return (
            lambda: lax.fori_loop(1, count, start, 0),
            lambda: lax.fori_loop(1, count, arrive, 0),
            lambda: lax.fori_loop(1, count, drain, 0),
        )

    def rows_copy(p, slot):
        return remote(rows_ref.at[p], rrecv.at[slot], rs_s.at[p], rs_r.at[slot], {"seq": p})

    def gather_copy(p, slot):
        return remote(ragg.at[b], ragg.at[slot], ag_s.at[p], ag_r.at[slot], {"req": p})

    def part_copy(p, slot):
        cols = pl.ds(pl.multiple_of(lax.rem(p, 2) * 256, 256), 256)
        return remote(part.at[p // 2, :, cols], precv.at[slot], pt_s.at[p], pt_r.at[slot], {"seq": p})

    def h1_copy(p, slot):
        return remote(h1.at[b], h1.at[slot], h1_s.at[p], h1_r.at[slot], {"req": p})

    def h2_copy(p, slot):
        return remote(h1, h2.at[slot // 2, lax.rem(slot, 2)], h2_s.at[p], h2_r.at[slot], {"seq": p})

    def m1_copy(p, slot):
        return remote(mx1.at[b], mx1.at[slot], m1_s.at[p], m1_r.at[slot], {"req": p})

    def m2_copy(p, slot):
        return remote(mx2.at[s], mx2.at[slot], m2_s.at[p], m2_r.at[slot], {"seq": p})

    sy, sz = s // 4, lax.rem(s, 4)

    def even(c):
        return c + 1 - 2 * lax.rem(c, 2)

    def odd(c):
        return 3 - c

    orders = []
    for v in range(4):
        first_is_z = v % 2 == 0
        near, far = (even, odd) if v < 2 else (odd, even)
        c, e = (sz, sy) if first_is_z else (sy, sz)
        orders.append((first_is_z, near, far, c, e))

    def spot_of(v, c, e):
        return e * 4 + c if orders[v][0] else c * 4 + e

    def block(v, c, e):
        cols = pl.ds(pl.multiple_of(spot_of(v, c, e) * width, width), width)
        return (slice(None), pl.ds(32 * v, 32), cols)

    def stage1(v, i, q):
        _, near, far, c, _ = orders[v]
        p = near(c)
        src = tails_ref.at[block(v, p if i == 0 else far(p), q)]
        _, _, _, _, e = orders[v]
        return remote(src, p1.at[v, i, q], p1_s.at[v, i, q], p1_r.at[v, i, q], {"seq": spot_of(v, p, e)})

    def stage2(v, q):
        _, _, far, c, e = orders[v]
        return remote(
            p1.at[v, 1, q], p2.at[v, q], p2_s.at[v, q], p2_r.at[v, q], {"seq": spot_of(v, far(c), e)}
        )

    def stage3(v, i):
        _, near, far, c, e = orders[v]
        p = near(e)
        src = p2.at[v, p if i == 0 else far(p)]
        return remote(src, p3.at[v, i], p3_s.at[v, i], p3_r.at[v, i], {"seq": spot_of(v, c, p)})

    def stage4(v):
        _, _, far, c, e = orders[v]
        return remote(p3.at[v, 1], p4.at[v], p4_s.at[v], p4_r.at[v], {"seq": spot_of(v, c, far(e))})

    def each(act, one):
        for v in range(4):
            for i in range(2):
                if act == 1:

                    def step(q, _):
                        one(stage1(v, i, q))
                        return 0

                    lax.fori_loop(0, 4, step, 0)
                elif act == 2 and i == 0:

                    def step(q, _):
                        one(stage2(v, q))
                        return 0

                    lax.fori_loop(0, 4, step, 0)
                elif act == 3:
                    one(stage3(v, i))
                elif act == 4 and i == 0:
                    one(stage4(v))

    go = lambda copy: copy.start()
    got = lambda copy: copy.wait_recv()
    sent = lambda copy: copy.wait_send()

    def add1():
        for v in range(4):
            _, _, far, c, _ = orders[v]
            for i in range(2):

                def step(q, _):
                    p1[v, i, q] = p1[v, i, q] + tails_ref[block(v, c if i == 0 else far(c), q)]
                    return 0

                lax.fori_loop(0, 4, step, 0)

    def add2():
        for v in range(4):
            p2[v] = p2[v] + p1[v, 0]

    def add3():
        for v in range(4):
            _, _, far, _, e = orders[v]
            p3[v, 0] = p3[v, 0] + p2[v, e]
            p3[v, 1] = p3[v, 1] + p2[v, far(e)]

    rows_go, rows_in, rows_out = over(n, seq_peer, rows_copy, s)
    ag_go, ag_in, ag_out = over(m, req_peer, gather_copy, b)
    part_go, part_in, part_out = over(n, seq_peer, part_copy, s)
    h1_go, h1_in, h1_out = over(m, req_peer, h1_copy, b)
    h2_go, h2_in, h2_out = over(n, seq_peer, h2_copy, s)
    m1_go, m1_in, m1_out = over(m, req_peer, m1_copy, b)
    m2_go, m2_in, m2_out = over(n, seq_peer, m2_copy, s)

    rows_go()

    def w_copy(p):
        cols = pl.ds(pl.multiple_of(p * depth, depth), depth)
        return remote(
            w_ref.at[:, cols], wbuf.at[w_slot], w_s.at[p], w_r.at[w_slot], {"req": p, "seq": w_place}
        )

    def w_start(i, _):
        p = lax.rem(b + i, m)

        @pl.when(jnp.logical_not(to_self & (p == b)))
        def _():
            w_copy(p).start()

        return 0

    lax.fori_loop(0, m, w_start, 0)

    @pl.when(to_self)
    def _():
        wbuf[w_slot] = w_ref[:, pl.ds(pl.multiple_of(b * depth, depth), depth)]

    rrecv[s] = rows_ref[s]
    each(1, go)
    rows_in()
    ragg[b] = jnp.sum(rrecv[...], axis=0)
    ag_go()
    ag_in()

    def w_arrive(i, _):
        @pl.when(jnp.logical_not((from_b == b) & (from_s + i == s)))
        def _():
            remote(
                w_ref.at[:, pl.ds(0, depth)], wbuf.at[i], w_s.at[i], w_r.at[i], {"req": i, "seq": w_place}
            ).wait_recv()

        return 0

    lax.fori_loop(0, m, w_arrive, 0)

    lhs = ragg[...].reshape(8 * m, 128).astype(BF16)
    weights = wbuf[...].reshape(m * 32, depth)
    place = lax.broadcasted_iota(jnp.int32, (8 * m, depth), 0)
    both = jnp.where(place % 8 < 4, dot(lhs, weights[0:128]), dot(lhs, weights[128:256]))
    both = both + pltpu.roll(both, 4, 0)
    part[...] = both.reshape(m, 8, depth)
    part_go()
    precv[s] = part[s // 2, :, pl.ds(pl.multiple_of(lax.rem(s, 2) * 256, 256), 256)]
    each(1, got)
    add1()
    each(2, go)
    part_in()
    cols = pl.ds(pl.multiple_of(b * depth + lax.rem(s, 2) * 256, 256), 256)
    resid = resid_ref[s // 2, :, cols].astype(F32)
    hidden = jnp.sum(precv[...], axis=0) + jnp.concatenate([resid, resid], axis=0)
    upper = pltpu.roll(hidden[:, 128:256], 4, 0)
    eight = lax.broadcasted_iota(jnp.int32, (8, 128), 0)
    h1[b] = jnp.where(eight < 4, upper, hidden[:, 0:128]).astype(BF16)
    h1_go()
    h1_in()
    h2_go()
    h2[s // 2, lax.rem(s, 2)] = h1[...]
    each(2, got)
    add2()
    each(3, go)
    h2_in()

    for k in range(m):
        for q in range(2):
            piece = h2[:, q, k].astype(F32).reshape(8 * m, 128)
            lo = k * depth + q * 256
            hf[:, lo : lo + 128] = piece
            hf[:, lo + 128 : lo + 256] = pltpu.roll(piece, 4, 0)
    h = hf[...]
    hid_ref[0] = hf[pl.ds(pl.multiple_of(b * 8, 8), 8), :].astype(BF16)[SEQS:]
    scale = lax.rsqrt(jnp.mean(h * h, axis=1, keepdims=True) + TINY_FLOOR)
    normed = (h * scale * gain_ref[...]).astype(BF16)
    load.wait()
    top = jnp.full((1, 8 * m), -jnp.inf, F32)
    chunk = 256
    for k in range(vbuf.shape[0] // chunk):
        logits = dot_nt(vbuf[k * chunk : (k + 1) * chunk, :], normed)
        top = jnp.maximum(top, jnp.max(logits, axis=0, keepdims=True))
    top = jnp.concatenate([top, top], axis=1)
    mx1[b] = jnp.broadcast_to(top, (8, 128))
    m1_go()
    each(3, got)
    add3()
    each(4, go)
    m1_in()
    mx2[s] = jnp.max(mx1[...], axis=0)
    m2_go()

    each(4, got)
    for v in range(4):
        p4[v] = p4[v] + p3[v, 0]
    for r in range(SEQS - 1):
        share = jnp.concatenate([p4[v, r].astype(F32) for v in range(4)], axis=0)
        fin_ref[r] = reach_ref[r] + share
    fin_ref[SEQS - 1] = reach_ref[SEQS - 1]
    m2_in()
    best = jnp.max(mx2[...], axis=0)[0:1]
    lanes = lax.broadcasted_iota(jnp.int32, (1, 128), 1)
    four = lax.broadcasted_iota(jnp.int32, (1, SEQS), 1)
    top = jnp.zeros((1, SEQS), F32)
    for r in range(SEQS):
        one = jnp.max(jnp.where(lanes == b * 8 + SEQS + r, best, -jnp.inf), axis=1, keepdims=True)
        top = jnp.where(four == r, one, top)
    max_ref[...] = top

    for drain in (rows_out, ag_out, part_out, h1_out, h2_out, m1_out, m2_out):
        drain()

    def w_drain(p, _):
        @pl.when(jnp.logical_not(to_self & (p == b)))
        def _():
            w_copy(p).wait_send()

        return 0

    lax.fori_loop(0, m, w_drain, 0)

    for act in range(1, 5):
        each(act, sent)


def tail(rows, out_weight, tails, reached, resid, gain, vocab, n, m):
    width = D // n
    vmem = pl.BlockSpec(memory_space=pltpu.VMEM)
    dma = pltpu.SemaphoreType.DMA
    return pl.pallas_call(
        functools.partial(tail_kernel, n, m),
        in_specs=[vmem] * 6 + [pl.BlockSpec(memory_space=pl.ANY)],
        out_specs=[vmem] * 3,
        out_shape=[
            jax.ShapeDtypeStruct((1, SEQS, D), BF16),
            jax.ShapeDtypeStruct((1, SEQS), F32),
            jax.ShapeDtypeStruct((SEQS, STATE, width), F32),
        ],
        scratch_shapes=[
            pltpu.VMEM(vocab.shape, BF16),
            pltpu.VMEM((n, 8, 128), F32),
            pltpu.VMEM((m, 8, 128), F32),
            pltpu.VMEM((m, 32, D // m), BF16),
            pltpu.VMEM((m, 8, D // m), F32),
            pltpu.VMEM((n, 8, 256), F32),
            pltpu.VMEM((m, 8, 128), BF16),
            pltpu.VMEM((n // 2, 2, m, 8, 128), BF16),
            pltpu.VMEM((8 * m, D), F32),
            pltpu.VMEM((m, 8, 128), F32),
            pltpu.VMEM((n, 8, 128), F32),
            pltpu.VMEM((4, 2, 4, SEQS - 1, 32, width), BF16),
            pltpu.VMEM((4, 4, SEQS - 1, 32, width), BF16),
            pltpu.VMEM((4, 2, SEQS - 1, 32, width), BF16),
            pltpu.VMEM((4, SEQS - 1, 32, width), BF16),
            dma,
            dma((n,)),
            dma((n,)),
            dma((m,)),
            dma((m,)),
            dma((m,)),
            dma((m,)),
            dma((n,)),
            dma((n,)),
            dma((m,)),
            dma((m,)),
            dma((n,)),
            dma((n,)),
            dma((m,)),
            dma((m,)),
            dma((n,)),
            dma((n,)),
            dma((4, 2, 4)),
            dma((4, 2, 4)),
            dma((4, 4)),
            dma((4, 4)),
            dma((4, 2)),
            dma((4, 2)),
            dma((4,)),
            dma((4,)),
        ],
        compiler_params=pltpu.CompilerParams(
            collective_id=1, has_side_effects=True, vmem_limit_bytes=VMEM_LIMIT
        ),
        name="tail",
    )(rows, out_weight, tails, reached, resid, gain, vocab)


def pack_kernel(fin_ref, hid_ref, top_ref, fin_out, hid_out, top_out):
    for r in range(SEQS):
        fin_out[r] = fin_ref[r].T
    hid_out[...] = hid_ref[...]
    top_out[...] = top_ref[...]


def pack(final, hid, top):
    vmem = pl.BlockSpec(memory_space=pltpu.VMEM)
    return pl.pallas_call(
        pack_kernel,
        in_specs=[vmem] * 3,
        out_specs=[vmem] * 3,
        out_shape=[
            jax.ShapeDtypeStruct((final.shape[0], final.shape[2], final.shape[1]), F32),
            jax.ShapeDtypeStruct(hid.shape, BF16),
            jax.ShapeDtypeStruct(top.shape, F32),
        ],
        name="pack",
    )(final, hid, top)


def body(
    conv_input,
    gate_projected,
    step_raw,
    step_bias,
    decay_log,
    head_direct_gain,
    conv_weight,
    convolution_bias,
    norm_weight,
    lengths,
    out_weight,
    residual_last,
    final_gain,
    vocab_weight,
):
    seq_count = lax.axis_size("seq")
    req_count = lax.axis_size("req")
    conv = conv_input[0]
    halo = halo_rows(conv, seq_count)
    yb, states, tails, aux, c, lead, xb, sc, cum, rt, dx = local_pass(
        lengths,
        conv,
        halo,
        conv_weight,
        convolution_bias[None],
        step_raw[0].T,
        step_bias[None],
        decay_log[None],
        head_direct_gain[None],
    )
    entering, reached, y = exchange(states, aux, dx, xb, sc, cum, rt, seq_count)
    gated, rows = finish(lengths, y, yb, c, entering, lead, gate_projected[0], norm_weight[None])
    hid, top, final = tail(
        rows, out_weight, tails, reached, residual_last, final_gain[None], vocab_weight, seq_count, req_count
    )
    final, hid, top = pack(final, hid, top)
    final_states = final.reshape(SEQS, HEADS // seq_count, CHANNEL_WIDTH, STATE)[None]
    return (gated[None], final_states, hid, top)


def solution(mesh):
    return jax.shard_map(
        body,
        mesh=mesh,
        in_specs=(
            P("req", "seq", None),
            P("req", "seq", None),
            P("req", "seq", None),
            P(),
            P(),
            P(),
            P(),
            P(),
            P(),
            P("req", None),
            P(("req", "seq"), None),
            P(),
            P(),
            P(("req", "seq"), None),
        ),
        out_specs=(
            P("req", "seq", None),
            P("req", None, "seq", None, None),
            P("req", None, None),
            P("req", None),
        ),
        check_vma=False,
    )
```

```python
import functools

import jax
import jax.numpy as jnp
from jax import lax
from jax.experimental import pallas as pl
from jax.experimental.pallas import tpu as pltpu
from jax.sharding import PartitionSpec as P

D = 4096
HEADS = 64
CHANNEL_WIDTH = 64
GROUPS = 4
STATE = 128
CHUNKS = [slice(c * 256, c * 256 + 256) for c in range(4)]
KERNEL = 4
BLOCK = 256
SEQS = 4
PER_GROUP = HEADS // GROUPS
GW = PER_GROUP * CHANNEL_WIDTH
TINY_FLOOR = 1e-05
LOG2E = 1.4426950408889634
MESH = pl.DeviceIdType.MESH
F32 = jnp.float32
BF16 = jnp.bfloat16
VMEM_LIMIT = 60 * 1024 * 1024


def dot(a, b):
    return lax.dot_general(a, b, (((1,), (0,)), ((), ())), preferred_element_type=F32)


def dot_nt(a, b):
    return lax.dot_general(a, b, (((1,), (1,)), ((), ())), preferred_element_type=F32)


def split2(x):
    hi = x.astype(BF16)
    return hi, (x - hi.astype(F32)).astype(BF16)


def split3(x):
    hi = x.astype(BF16)
    rest = x - hi.astype(F32)
    mid = rest.astype(BF16)
    return hi, mid, (rest - mid.astype(F32)).astype(BF16)


def seg_of(place, b1, b2, b3):
    one = lambda b: (place >= b).astype(jnp.int32)
    return one(b1) + one(b2) + one(b3)


def spread_matrix():
    lane = lax.broadcasted_iota(jnp.int32, (128, GW), 0)
    col = lax.broadcasted_iota(jnp.int32, (128, GW), 1)
    hit = (lane < 48) & (lane % PER_GROUP == col // CHANNEL_WIDTH)
    return jnp.where(hit, 1.0, 0.0).astype(BF16)


def spread_parts(v):
    hi, mid, lo = split3(v)
    lane = lax.broadcasted_iota(jnp.int32, v.shape, 1)
    parts = jnp.where(
        lane < 16, hi.astype(F32), jnp.where(lane < 32, mid.astype(F32), lo.astype(F32))
    ).astype(BF16)
    return parts


def spread(v, spread_ref):
    return dot(spread_parts(v), spread_ref[...])


def halves(h):
    return h + h * jnp.tanh(h)


def softplus(x):
    e = jnp.exp(-jnp.abs(x))
    w = 1.0 + e
    d = w - 1.0
    return jnp.maximum(x, 0.0) + jnp.where(d == 0.0, e, jnp.log(w) * (e / jnp.where(d == 0.0, 1.0, d)))


def bounds_of(len_ref):
    b1 = len_ref[0, 0]
    b2 = b1 + len_ref[0, 1]
    return b1, b2, b2 + len_ref[0, 2]


def local_kernel(
    len_ref,
    x_ref,
    b_ref,
    c_ref,
    xh_ref,
    bh_ref,
    ch_ref,
    wx_ref,
    wb_ref,
    wc_ref,
    vx_ref,
    vb_ref,
    vc_ref,
    raw_ref,
    bias_ref,
    log_ref,
    gain_ref,
    lp_ref,
    sh_ref,
    st_ref,
    pt_ref,
    aux_ref,
    co_ref,
    ld_ref,
    xb_ref,
    sc_ref,
    cum_ref,
    rt_ref,
    dx_ref,
    xext,
    xf,
    s0,
    c0,
    cumr,
    sp,
    msk,
    alw,
    sgs,
    cums,
    lds,
    wst,
    ow,
):
    g = pl.program_id(0)
    j = pl.program_id(1)
    span = pl.num_programs(1) * BLOCK
    first = lax.axis_index("seq") * span
    b1, b2, b3 = bounds_of(len_ref)
    bounds = (b1, b2, b3)
    start = first + j * BLOCK

    @pl.when((g == 0) & (j == 0))
    def _():
        sp[...] = spread_matrix()

    row = lax.broadcasted_iota(jnp.int32, (BLOCK, 128), 0) + start

    @pl.when(g == 0)
    def _():
        near = jnp.full((BLOCK, 128), 8, jnp.int32)
        for bound in bounds:
            gap = row - bound
            near = jnp.where(gap >= 0, jnp.minimum(near, gap), near)
        for k in range(3):
            msk[j, k] = (near >= 3 - k).astype(F32)
        sgs[j] = seg_of(row, b1, b2, b3)
        i0 = lax.broadcasted_iota(jnp.int32, (BLOCK, BLOCK), 0)
        i1 = lax.broadcasted_iota(jnp.int32, (BLOCK, BLOCK), 1)
        t_seg = seg_of(i0 + start, b1, b2, b3)
        s_seg = seg_of(i1 + start, b1, b2, b3)
        alw[j] = ((i0 >= i1) & (t_seg == s_seg)).astype(F32)
        tri = jnp.where(i0 >= i1, 1.0, 0.0).astype(BF16)
        dt = softplus(raw_ref[...].T + bias_ref[...])
        dh, dm, dl = split3(dt * (jnp.exp(log_ref[...]) * -LOG2E))
        run = (dot(tri, dl) + dot(tri, dm)) + dot(tri, dh)
        logs = jnp.log(dt) * LOG2E
        cums[j] = jnp.concatenate([run, logs], axis=1)
        lds[j] = logs - run

    l0 = lax.broadcasted_iota(jnp.int32, (2 * HEADS, 256), 0)
    l1 = lax.broadcasted_iota(jnp.int32, (2 * HEADS, 256), 1)
    pick = jnp.where(
        l0 == l1 // 128 * HEADS + g * PER_GROUP + l1 % PER_GROUP, 1.0, 0.0
    ).astype(BF16)
    t0 = lax.broadcasted_iota(jnp.int32, (PER_GROUP, HEADS), 0)
    t1 = lax.broadcasted_iota(jnp.int32, (PER_GROUP, HEADS), 1)
    pickt = jnp.where(t1 == g * PER_GROUP + t0, 1.0, 0.0).astype(BF16)

    def group(v):
        hi, mid, lo = split3(v)
        return (dot(lo, pick) + dot(mid, pick)) + dot(hi, pick)

    @pl.when(j == 0)
    def _():
        xext[0:8, 0:GW] = xh_ref[...].astype(F32)
        xext[0:8, GW : GW + 128] = bh_ref[...].astype(F32)
        xext[0:8, GW + 128 : GW + 256] = ch_ref[...].astype(F32)
        for lo, hi, w_ref, v_ref in (
            (0, GW, wx_ref, vx_ref),
            (GW, GW + 128, wb_ref, vb_ref),
            (GW + 128, GW + 256, wc_ref, vc_ref),
        ):
            wst[0:KERNEL, lo:hi] = w_ref[...] * 0.5
            wst[KERNEL : KERNEL + 1, lo:hi] = v_ref[...] * 0.5
        pt_ref[...] = jnp.zeros_like(pt_ref)
        aux_ref[...] = jnp.zeros_like(aux_ref)
        c0[...] = jnp.zeros_like(c0)
        gains = jnp.broadcast_to(gain_ref[...], (8, HEADS))
        dx_ref[...] = spread(group(jnp.concatenate([gains, gains], axis=1))[:, 0:128], sp)

    @pl.when(j == 1)
    def _():
        xext[0:8, :] = xext[BLOCK : BLOCK + 8, :]

    xext[8 : BLOCK + 8, 0:GW] = x_ref[...].astype(F32)
    xext[8 : BLOCK + 8, GW : GW + 128] = b_ref[...].astype(F32)
    xext[8 : BLOCK + 8, GW + 128 : GW + 256] = c_ref[...].astype(F32)

    tile = 64

    def convolve(c, _):
        cols = pl.ds(pl.multiple_of(c * 128, 128), 128)
        w = [wst[k : k + 1, cols] for k in range(KERNEL)]
        bias = wst[KERNEL : KERNEL + 1, cols]
        for lo in range(0, BLOCK, tile):
            total = jnp.broadcast_to(bias, (tile, 128))
            for k in range(3):
                total = total + w[k] * xext[lo + 5 + k : lo + 5 + k + tile, cols] * msk[j, k, lo : lo + tile]
            total = total + w[3] * xext[lo + 8 : lo + 8 + tile, cols]
            xf[lo : lo + tile, cols] = halves(total)
        return 0

    lax.fori_loop(0, 10, convolve, 0)

    seg = sgs[j]
    bf = xf[:, GW : GW + 128]
    cb = xf[:, GW + 128 : GW + 256].astype(BF16)
    co_ref[...] = cb

    grouped = group(cums[j])
    cum = grouped[:, 0:128]
    logdt = grouped[:, 128:256]
    rh, rm, rl = split3(lds[j])
    rt = (dot_nt(pickt, rl) + dot_nt(pickt, rm)) + dot_nt(pickt, rh)
    cumr[...] = cum
    last = cum[BLOCK - 1 : BLOCK, :]

    seg_before_span = seg_of(first - 1, b1, b2, b3)
    seg_before = seg_of(start - 1, b1, b2, b3)
    seg_end = seg_of(start + BLOCK - 1, b1, b2, b3)
    prior = c0[0:1, :]
    ld_ref[0, 0] = jnp.where(seg == seg_before_span, jnp.exp2(cum + prior), 0.0)

    bh, bl = split2(bf)
    sc = dot_nt(cb, bh) * alw[j]

    xb_ref[0] = xf[:, 0:GW].astype(BF16)
    sc_ref[0] = sc
    cum_ref[0] = cum
    rt_ref[0] = rt

    @pl.when(j == 1)
    def _():
        lead = jnp.where(seg == seg_before, jnp.exp2(cum), 0.0)
        lp_ref[0] = spread_parts(lead)
        sh, sl = split2(s0[...])
        sh_ref[0] = sh
        sh_ref[1] = sl

    both = jnp.concatenate(split2(bf.T), axis=0)

    def state_of(weights, put):
        parts = spread_parts(weights)
        for cols in CHUNKS:
            xs = (xf[:, cols] * dot(parts, sp[:, cols])).astype(BF16)
            two = dot(both, xs)
            put(cols, two[:STATE] + two[STATE:])

    def at_end(seg_e):
        return jnp.where(seg == seg_e, jnp.exp2(last - cum + logdt), 0.0)

    def put_own(cols, value):
        ow[:, cols] = value

    state_of(at_end(seg_end), put_own)

    for r in range(SEQS - 1):
        end = bounds[r] - 1
        local = end - start
        owned = (local >= 0) & (local < BLOCK)

        @pl.when(owned)
        def _():
            ce = cumr[pl.ds(jnp.clip(local, 0, BLOCK - 1), 1), :]
            inside = (row <= end) & (seg == r)
            w = jnp.exp2(jnp.where(inside, ce - cum + logdt, -1e30))
            reach = jnp.where(seg_before == r, jnp.exp2(ce), 0.0)
            reach8 = spread(jnp.broadcast_to(reach, (8, 128)), sp)

            def put_tail(cols, value):
                before = jnp.where(j == 1, reach8[0:1, cols] * s0[:, cols], 0.0)
                pt_ref[r, :, cols] = (value + before).astype(BF16)

            state_of(w, put_tail)
            full = jnp.where(seg_before_span == r, jnp.exp2(ce + prior), 0.0)
            aux_ref[1 + r : 2 + r, :] = spread(jnp.broadcast_to(full, (8, 128)), sp)[0:1]

    @pl.when(j == 0)
    def _():
        s0[...] = ow[...]
        c0[...] = jnp.broadcast_to(last, c0.shape)

    @pl.when(j == 1)
    def _():
        carry = jnp.where(seg_end == seg_before, jnp.exp2(last), 0.0)
        whole = jnp.where(seg_end == seg_before_span, jnp.exp2(last + prior), 0.0)
        carry8 = spread(jnp.broadcast_to(carry, (8, 128)), sp)
        whole8 = spread(jnp.broadcast_to(whole, (8, 128)), sp)
        st_ref[...] = (carry8[0:1] * s0[...] + ow[...]).astype(BF16)
        aux_ref[0:1, :] = whole8[0:1]


def local_pass(lengths, conv, halo, conv_weight, conv_bias, raw, bias, log, gain):
    length = conv.shape[0]
    blocks = length // BLOCK
    maps = D // 128
    grid = (GROUPS, blocks)
    xs = lambda rows: [
        pl.BlockSpec((rows, GW), lambda g, j: (0, g)),
        pl.BlockSpec((rows, 128), lambda g, j: (0, maps + g)),
        pl.BlockSpec((rows, 128), lambda g, j: (0, maps + GROUPS + g)),
    ]
    in_specs = (
        [
            pl.BlockSpec(memory_space=pltpu.SMEM),
            pl.BlockSpec((BLOCK, GW), lambda g, j: (j, g)),
            pl.BlockSpec((BLOCK, 128), lambda g, j: (j, maps + g)),
            pl.BlockSpec((BLOCK, 128), lambda g, j: (j, maps + GROUPS + g)),
        ]
        + xs(8)
        + xs(KERNEL)
        + xs(1)
        + [
            pl.BlockSpec((HEADS, BLOCK), lambda g, j: (0, j)),
            pl.BlockSpec((1, HEADS), lambda g, j: (0, 0)),
            pl.BlockSpec((1, HEADS), lambda g, j: (0, 0)),
            pl.BlockSpec((1, HEADS), lambda g, j: (0, 0)),
        ]
    )
    each = lambda *shape: pl.BlockSpec((1,) + shape, lambda g, j: (g * blocks + j, 0, 0))
    out_specs = [
        pl.BlockSpec((1, BLOCK, 128), lambda g, j: (g, 0, 0)),
        pl.BlockSpec((2, STATE, GW), lambda g, j: (0, 0, g)),
        pl.BlockSpec((STATE, GW), lambda g, j: (0, g)),
        pl.BlockSpec((SEQS - 1, STATE, GW), lambda g, j: (0, 0, g)),
        pl.BlockSpec((8, GW), lambda g, j: (0, g)),
        pl.BlockSpec((BLOCK, 128), lambda g, j: (j, g)),
        pl.BlockSpec((1, 1, BLOCK, 128), lambda g, j: (g, j, 0, 0)),
        each(BLOCK, GW),
        each(BLOCK, BLOCK),
        each(BLOCK, 128),
        each(PER_GROUP, BLOCK),
        pl.BlockSpec((8, GW), lambda g, j: (0, g)),
    ]
    steps = GROUPS * blocks
    out_shape = [
        jax.ShapeDtypeStruct((GROUPS, BLOCK, 128), BF16),
        jax.ShapeDtypeStruct((2, STATE, D), BF16),
        jax.ShapeDtypeStruct((STATE, D), BF16),
        jax.ShapeDtypeStruct((SEQS - 1, STATE, D), BF16),
        jax.ShapeDtypeStruct((8, D), F32),
        jax.ShapeDtypeStruct((length, GROUPS * STATE), BF16),
        jax.ShapeDtypeStruct((GROUPS, blocks, BLOCK, 128), F32),
        jax.ShapeDtypeStruct((steps, BLOCK, GW), BF16),
        jax.ShapeDtypeStruct((steps, BLOCK, BLOCK), F32),
        jax.ShapeDtypeStruct((steps, BLOCK, 128), F32),
        jax.ShapeDtypeStruct((steps, PER_GROUP, BLOCK), F32),
        jax.ShapeDtypeStruct((8, D), F32),
    ]
    return pl.pallas_call(
        local_kernel,
        grid=grid,
        in_specs=in_specs,
        out_specs=out_specs,
        out_shape=out_shape,
        scratch_shapes=[
            pltpu.VMEM((BLOCK + 8, GW + 256), F32),
            pltpu.VMEM((BLOCK, GW + 256), F32),
            pltpu.VMEM((STATE, GW), F32),
            pltpu.VMEM((8, 128), F32),
            pltpu.VMEM((BLOCK, 128), F32),
            pltpu.VMEM((128, GW), BF16),
            pltpu.VMEM((blocks, 3, BLOCK, 128), F32),
            pltpu.VMEM((blocks, BLOCK, BLOCK), F32),
            pltpu.VMEM((blocks, BLOCK, 128), jnp.int32),
            pltpu.VMEM((blocks, BLOCK, 2 * HEADS), F32),
            pltpu.VMEM((blocks, BLOCK, HEADS), F32),
            pltpu.VMEM((8, GW + 256), F32),
            pltpu.VMEM((STATE, GW), F32),
        ],
        compiler_params=pltpu.CompilerParams(
            vmem_limit_bytes=VMEM_LIMIT, dimension_semantics=("arbitrary", "arbitrary")
        ),
        name="local_pass",
    )(
        lengths, conv, conv, conv, halo, halo, halo, conv_weight, conv_weight, conv_weight,
        conv_bias, conv_bias, conv_bias, raw, bias, log, gain,
    )


def halo_kernel(n, conv_ref, out_ref, got, send, recv):
    me = lax.axis_index("seq")
    right = lax.rem(me + 1, n)
    left = lax.rem(me + n - 1, n)
    barrier = pltpu.get_barrier_semaphore()
    for p in (left, right):
        pl.semaphore_signal(barrier, inc=1, device_id={"seq": p}, device_id_type=MESH)
    pl.semaphore_wait(barrier, 2)
    copy = pltpu.make_async_remote_copy(
        src_ref=conv_ref.at[pl.ds(conv_ref.shape[0] - 8, 8), :],
        dst_ref=got,
        send_sem=send,
        recv_sem=recv,
        device_id={"seq": right},
        device_id_type=MESH,
    )
    copy.start()
    copy.wait()
    keep = jnp.where(me == 0, 0.0, 1.0)
    out_ref[...] = (got[...].astype(F32) * keep).astype(BF16)


def halo_rows(conv, n):
    shape = (8, conv.shape[1])
    return pl.pallas_call(
        functools.partial(halo_kernel, n),
        in_specs=[pl.BlockSpec(memory_space=pl.ANY)],
        out_specs=pl.BlockSpec(memory_space=pltpu.VMEM),
        out_shape=jax.ShapeDtypeStruct(shape, BF16),
        scratch_shapes=[
            pltpu.VMEM(shape, BF16),
            pltpu.SemaphoreType.DMA,
            pltpu.SemaphoreType.DMA,
        ],
        compiler_params=pltpu.CompilerParams(collective_id=2, has_side_effects=True),
        name="halo",
    )(conv)


def exchange_kernel(
    n,
    st_ref,
    aux_ref,
    dx_ref,
    xb_ref,
    sc_ref,
    cum_ref,
    rt_ref,
    lp_ref,
    sh_ref,
    c_ref,
    ent_ref,
    fin_ref,
    y_ref,
    rs,
    ra,
    eb,
    xbv,
    scv,
    cumv,
    rtv,
    lpv,
    shv,
    cv,
    sp,
    yv,
    send1,
    recv1,
    send2,
    recv2,
    send3,
    recv3,
    lsem,
    wsem,
    ysem,
):
    me = lax.axis_index("seq")
    steps = xb_ref.shape[0]

    def loads(k):
        pairs = ((xb_ref, xbv), (sc_ref, scv), (cum_ref, cumv), (rt_ref, rtv))
        return [pltpu.make_async_copy(a.at[k], v.at[k], lsem.at[k, i]) for i, (a, v) in enumerate(pairs)]

    def store(k):
        return pltpu.make_async_copy(yv.at[k], y_ref.at[k], ysem.at[k])

    def fetch(k, _):
        for copy in loads(k):
            copy.start()
        return 0

    wholes = [
        pltpu.make_async_copy(a, v, wsem.at[i])
        for i, (a, v) in enumerate(((lp_ref, lpv), (sh_ref, shv), (c_ref, cv)))
    ]
    for copy in wholes:
        copy.start()
    lax.fori_loop(0, steps, fetch, 0)
    width = D // n
    barrier = pltpu.get_barrier_semaphore()

    def peer(i):
        return lax.rem(me + i, n)

    def cols(p):
        return pl.ds(pl.multiple_of(p * width, width), width)

    def greet(i, _):
        pl.semaphore_signal(barrier, inc=1, device_id={"seq": peer(i)}, device_id_type=MESH)
        return 0

    lax.fori_loop(1, n, greet, 0)
    pl.semaphore_wait(barrier, n - 1)

    def out(p, slot):
        return (
            pltpu.make_async_remote_copy(
                src_ref=st_ref.at[:, cols(p)],
                dst_ref=rs.at[slot],
                send_sem=send1.at[p],
                recv_sem=recv1.at[slot],
                device_id={"seq": p},
                device_id_type=MESH,
            ),
            pltpu.make_async_remote_copy(
                src_ref=aux_ref.at[:, cols(p)],
                dst_ref=ra.at[slot],
                send_sem=send2.at[p],
                recv_sem=recv2.at[slot],
                device_id={"seq": p},
                device_id_type=MESH,
            ),
        )

    def back(p, slot):
        return pltpu.make_async_remote_copy(
            src_ref=eb.at[p],
            dst_ref=ent_ref.at[:, cols(slot)],
            send_sem=send3.at[p],
            recv_sem=recv3.at[slot],
            device_id={"seq": p},
            device_id_type=MESH,
        )

    def begin(i, _):
        for copy in out(peer(i), me):
            copy.start()
        return 0

    lax.fori_loop(1, n, begin, 0)
    rs[me] = st_ref[:, cols(me)]
    ra[me] = aux_ref[:, cols(me)]

    lane = lax.broadcasted_iota(jnp.int32, (BLOCK, 128), 1)
    half = BLOCK // 2
    sp[...] = spread_matrix()
    for copy in wholes:
        copy.wait()

    def mix(k, _):
        for copy in loads(k):
            copy.wait()
        sc_t = scv[k, :half, :half]
        sc_l = scv[k, half:, :half]
        sc_r = scv[k, half:, half:]
        for pair in range(PER_GROUP // 2):
            span = slice(pair * 128, pair * 128 + 128)
            xb = xbv[k, :, span]
            res = []
            for h in (2 * pair, 2 * pair + 1):
                col = cumv[k, :, h : h + 1]
                r = rtv[k, h : h + 1, :]
                top = jnp.exp2(jnp.minimum(col[:half] + r[:, :half], 100.0)) * sc_t
                left = jnp.exp2(col[half:] + r[:, :half]) * sc_l
                right = jnp.exp2(jnp.minimum(col[half:] + r[:, half:], 100.0)) * sc_r
                bottom = jnp.concatenate([left.astype(BF16), right.astype(BF16)], axis=1)
                res.append(jnp.concatenate([dot(top.astype(BF16), xb[:half]), dot(bottom, xb)], axis=0))
            intra = jnp.where(lane < CHANNEL_WIDTH, res[0], res[1])
            direct = dx_ref[0:1, pl.ds(pl.multiple_of(k // 2 * GW + pair * 128, 128), 128)]
            yv[k, :, span] = intra + direct * xb.astype(F32)

        @pl.when(lax.rem(k, 2) == 1)
        def _():
            g = k // 2
            cb = cv[BLOCK : 2 * BLOCK, pl.ds(pl.multiple_of(g * STATE, STATE), STATE)]
            parts = lpv[g]
            for c in range(4):
                span = slice(c * 256, c * 256 + 256)
                at = pl.ds(pl.multiple_of(g * GW + c * 256, 256), 256)
                passed = dot(cb, shv[0, :, at]) + dot(cb, shv[1, :, at])
                yv[k, :, span] = yv[k, :, span] + dot(parts, sp[:, span]) * passed

        store(k).start()
        return 0

    lax.fori_loop(0, steps, mix, 0)
    fin_ref[...] = jnp.zeros_like(fin_ref)

    def scan(d, _):
        @pl.when(d != me)
        def _():
            for copy in out(d, d):
                copy.wait_recv()

        now = fin_ref[SEQS - 1]
        eb[d] = now.astype(BF16)

        @pl.when(d != me)
        def _():
            back(d, me).start()

        for r in range(SEQS - 1):
            fin_ref[r] = fin_ref[r] + ra[d, 1 + r : 2 + r, :] * now
        fin_ref[SEQS - 1] = ra[d, 0:1, :] * now + rs[d].astype(F32)
        return 0

    lax.fori_loop(0, n, scan, 0)
    ent_ref[:, cols(me)] = eb[me]

    def done(i, _):
        back(peer(i), peer(i)).wait_recv()
        return 0

    lax.fori_loop(1, n, done, 0)

    def drain(i, _):
        for copy in out(peer(i), me):
            copy.wait_send()
        back(peer(i), me).wait_send()
        return 0

    lax.fori_loop(1, n, drain, 0)

    def stored(k, _):
        store(k).wait()
        return 0

    lax.fori_loop(0, steps, stored, 0)


def exchange(states, aux, dx, xb, sc, cum, rt, lead, passed, c, n):
    width = D // n
    steps = xb.shape[0]
    far = pl.BlockSpec(memory_space=pl.ANY)
    vmem = pl.BlockSpec(memory_space=pltpu.VMEM)
    return pl.pallas_call(
        functools.partial(exchange_kernel, n),
        in_specs=[vmem] * 3 + [far] * 7,
        out_specs=[vmem, vmem, far],
        out_shape=[
            jax.ShapeDtypeStruct((STATE, D), BF16),
            jax.ShapeDtypeStruct((SEQS, STATE, width), F32),
            jax.ShapeDtypeStruct((steps, BLOCK, GW), F32),
        ],
        scratch_shapes=[
            pltpu.VMEM((n, STATE, width), BF16),
            pltpu.VMEM((n, 8, width), F32),
            pltpu.VMEM((n, STATE, width), BF16),
            pltpu.VMEM(xb.shape, BF16),
            pltpu.VMEM(sc.shape, F32),
            pltpu.VMEM(cum.shape, F32),
            pltpu.VMEM(rt.shape, F32),
            pltpu.VMEM(lead.shape, BF16),
            pltpu.VMEM(passed.shape, BF16),
            pltpu.VMEM(c.shape, BF16),
            pltpu.VMEM((128, GW), BF16),
            pltpu.VMEM((steps, BLOCK, GW), F32),
        ]
        + [pltpu.SemaphoreType.DMA((n,)) for _ in range(6)]
        + [pltpu.SemaphoreType.DMA((k,)) if k != 4 else pltpu.SemaphoreType.DMA((steps, 4)) for k in (4, 3, steps)],
        compiler_params=pltpu.CompilerParams(
            collective_id=0, has_side_effects=True, vmem_limit_bytes=VMEM_LIMIT
        ),
        name="exchange",
    )(states, aux, dx, xb, sc, cum, rt, lead, passed, c)


def finish_kernel(len_ref, y_ref, c_ref, e_ref, ld_ref, gate_ref, nw_ref, out_ref, rows_ref, sp, of, scales):
    g = pl.program_id(0)
    j = pl.program_id(1)

    @pl.when((g == 0) & (j == 0))
    def _():
        sp[...] = spread_matrix()

    @pl.when(j == 0)
    def _():
        rows_ref[...] = jnp.zeros_like(rows_ref)

    parts = spread_parts(ld_ref[0, 0])
    half = BLOCK // 2
    for lines in (slice(0, half), slice(half, BLOCK)):
        total = jnp.zeros((half, 128), F32)
        for cols in CHUNKS:
            v = y_ref[0, lines, cols] + dot(parts[lines], sp[:, cols]) * dot(c_ref[lines, :], e_ref[:, cols])
            v = v * halves(0.5 * gate_ref[lines, cols].astype(F32))
            of[lines, cols] = v
            total = total + v[:, :128] * v[:, :128] + v[:, 128:] * v[:, 128:]
        scale = lax.rsqrt(jnp.sum(total, axis=1, keepdims=True) * (1.0 / GW) + TINY_FLOOR)
        scales[lines, :] = jnp.broadcast_to(scale, (half, 128))
        for cols in CHUNKS:
            out_ref[lines, cols] = (of[lines, cols] * scale * nw_ref[:, cols]).astype(BF16)

    start = lax.axis_index("seq") * (pl.num_programs(1) * BLOCK) + j * BLOCK
    bounds = bounds_of(len_ref)
    for r, bound in enumerate(bounds + (bounds[2] + len_ref[0, 3],)):
        local = bound - 1 - start

        @pl.when((local >= 0) & (local < BLOCK))
        def _():
            spot = jnp.clip(local, 0, BLOCK - 1)
            line = of[pl.ds(spot, 1), :] * scales[pl.ds(spot, 1), :][:, 0:1] * nw_ref[...]
            line = line.astype(BF16).astype(F32)
            for c in range(GW // 128):
                place = c % 2 * SEQS + r
                rows_ref[c // 2, place : place + 1, :] = line[:, c * 128 : c * 128 + 128]


def finish(lengths, y, c, entering, lead, gate, norm_weight):
    length = gate.shape[0]
    blocks = length // BLOCK
    block = lambda width: pl.BlockSpec((BLOCK, width), lambda g, j: (j, g))
    return pl.pallas_call(
        finish_kernel,
        grid=(GROUPS, length // BLOCK),
        in_specs=[
            pl.BlockSpec(memory_space=pltpu.SMEM),
            pl.BlockSpec((1, BLOCK, GW), lambda g, j: (g * blocks + j, 0, 0)),
            block(STATE),
            pl.BlockSpec((STATE, GW), lambda g, j: (0, g)),
            pl.BlockSpec((1, 1, BLOCK, 128), lambda g, j: (g, j, 0, 0)),
            block(GW),
            pl.BlockSpec((1, GW), lambda g, j: (0, g)),
        ],
        out_specs=[block(GW), pl.BlockSpec((GW // 256, 8, 128), lambda g, j: (g, 0, 0))],
        out_shape=[
            jax.ShapeDtypeStruct((length, D), BF16),
            jax.ShapeDtypeStruct((D // 256, 8, 128), F32),
        ],
        scratch_shapes=[
            pltpu.VMEM((128, GW), BF16),
            pltpu.VMEM((BLOCK, GW), F32),
            pltpu.VMEM((BLOCK, 128), F32),
        ],
        compiler_params=pltpu.CompilerParams(
            vmem_limit_bytes=VMEM_LIMIT, dimension_semantics=("arbitrary", "arbitrary")
        ),
        name="finish",
    )(lengths, y, c, entering, lead, gate, norm_weight)


def tail_kernel(
    n,
    m,
    rows_ref,
    w_ref,
    tails_ref,
    reach_ref,
    resid_ref,
    gain_ref,
    vocab_ref,
    hid_ref,
    max_ref,
    fin_ref,
    vbuf,
    rrecv,
    ragg,
    wbuf,
    part,
    precv,
    h1,
    h2,
    hf,
    tv,
    mx1,
    mx2,
    p1,
    p2,
    p3,
    p4,
    vsem,
    tsem,
    rs_s,
    rs_r,
    ag_s,
    ag_r,
    w_s,
    w_r,
    pt_s,
    pt_r,
    h1_s,
    h1_r,
    h2_s,
    h2_r,
    m1_s,
    m1_r,
    m2_s,
    m2_r,
    p1_s,
    p1_r,
    p2_s,
    p2_r,
    p3_s,
    p3_r,
    p4_s,
    p4_r,
):
    s = lax.axis_index("seq")
    b = lax.axis_index("req")
    width = D // n
    depth = D // m
    w_place = 2 * b + s // 8
    w_slot = lax.rem(s, 8)
    to_self = w_place == s
    from_b = s // 2
    from_s = 8 * lax.rem(s, 2)

    load = pltpu.make_async_copy(vocab_ref, vbuf, vsem)
    tload = pltpu.make_async_copy(tails_ref, tv, tsem)
    tload.start()
    load.start()

    barrier = pltpu.get_barrier_semaphore()

    def signal(where):
        pl.semaphore_signal(barrier, inc=1, device_id=where, device_id_type=MESH)

    def seq_peer(i):
        return lax.rem(s + i, n)

    def req_peer(i):
        return lax.rem(b + i, m)

    def greet_seq(i, _):
        signal({"seq": seq_peer(i)})
        return 0

    def greet_req(i, _):
        signal({"req": req_peer(i)})
        return 0

    def greet_w(i, _):
        @pl.when(jnp.logical_not(to_self & (i == b)))
        def _():
            signal({"req": i, "seq": w_place})

        @pl.when(jnp.logical_not((from_b == b) & (from_s + i == s)))
        def _():
            signal({"req": from_b, "seq": from_s + i})

        return 0

    lax.fori_loop(1, n, greet_seq, 0)
    lax.fori_loop(1, m, greet_req, 0)
    lax.fori_loop(0, m, greet_w, 0)
    pl.semaphore_wait(barrier, (n - 1) + (m - 1) + 2 * m - 2 * to_self.astype(jnp.int32))

    def remote(src, dst, send, recv, where):
        return pltpu.make_async_remote_copy(
            src_ref=src, dst_ref=dst, send_sem=send, recv_sem=recv, device_id=where, device_id_type=MESH
        )

    def over(count, peer, copy, me):
        def start(i, _):
            copy(peer(i), me).start()
            return 0

        def arrive(i, _):
            copy(peer(i), peer(i)).wait_recv()
            return 0

        def drain(i, _):
            copy(peer(i), me).wait_send()
            return 0

        return (
            lambda: lax.fori_loop(1, count, start, 0),
            lambda: lax.fori_loop(1, count, arrive, 0),
            lambda: lax.fori_loop(1, count, drain, 0),
        )

    def rows_copy(p, slot):
        return remote(rows_ref.at[p], rrecv.at[slot], rs_s.at[p], rs_r.at[slot], {"seq": p})

    def gather_copy(p, slot):
        return remote(ragg.at[b], ragg.at[slot], ag_s.at[p], ag_r.at[slot], {"req": p})

    def part_copy(p, slot):
        cols = pl.ds(pl.multiple_of(lax.rem(p, 2) * 256, 256), 256)
        return remote(part.at[p // 2, :, cols], precv.at[slot], pt_s.at[p], pt_r.at[slot], {"seq": p})

    def h1_copy(p, slot):
        return remote(h1.at[b], h1.at[slot], h1_s.at[p], h1_r.at[slot], {"req": p})

    def h2_copy(p, slot):
        return remote(h1, h2.at[slot // 2, lax.rem(slot, 2)], h2_s.at[p], h2_r.at[slot], {"seq": p})

    def m1_copy(p, slot):
        return remote(mx1.at[b], mx1.at[slot], m1_s.at[p], m1_r.at[slot], {"req": p})

    def m2_copy(p, slot):
        return remote(mx2.at[s], mx2.at[slot], m2_s.at[p], m2_r.at[slot], {"seq": p})

    sy, sz = s // 4, lax.rem(s, 4)

    def even(c):
        return c + 1 - 2 * lax.rem(c, 2)

    def odd(c):
        return 3 - c

    orders = []
    for v in range(4):
        first_is_z = v % 2 == 0
        near, far = (even, odd) if v < 2 else (odd, even)
        c, e = (sz, sy) if first_is_z else (sy, sz)
        orders.append((first_is_z, near, far, c, e))

    def spot_of(v, c, e):
        return e * 4 + c if orders[v][0] else c * 4 + e

    def block(v, c, e):
        cols = pl.ds(pl.multiple_of(spot_of(v, c, e) * width, width), width)
        return (slice(None), pl.ds(32 * v, 32), cols)

    def stage1(v, i, q):
        _, near, far, c, _ = orders[v]
        p = near(c)
        src = tails_ref.at[block(v, p if i == 0 else far(p), q)]
        _, _, _, _, e = orders[v]
        return remote(src, p1.at[v, i, q], p1_s.at[v, i, q], p1_r.at[v, i, q], {"seq": spot_of(v, p, e)})

    def stage2(v, q):
        _, _, far, c, e = orders[v]
        return remote(
            p1.at[v, 1, q], p2.at[v, q], p2_s.at[v, q], p2_r.at[v, q], {"seq": spot_of(v, far(c), e)}
        )

    def stage3(v, i):
        _, near, far, c, e = orders[v]
        p = near(e)
        src = p2.at[v, p if i == 0 else far(p)]
        return remote(src, p3.at[v, i], p3_s.at[v, i], p3_r.at[v, i], {"seq": spot_of(v, c, p)})

    def stage4(v):
        _, _, far, c, e = orders[v]
        return remote(p3.at[v, 1], p4.at[v], p4_s.at[v], p4_r.at[v], {"seq": spot_of(v, c, far(e))})

    def each(act, one):
        for v in range(4):
            for i in range(2):
                if act == 1:

                    def step(q, _):
                        one(stage1(v, i, q))
                        return 0

                    lax.fori_loop(0, 4, step, 0)
                elif act == 2 and i == 0:

                    def step(q, _):
                        one(stage2(v, q))
                        return 0

                    lax.fori_loop(0, 4, step, 0)
                elif act == 3:
                    one(stage3(v, i))
                elif act == 4 and i == 0:
                    one(stage4(v))

    go = lambda copy: copy.start()
    got = lambda copy: copy.wait_recv()
    sent = lambda copy: copy.wait_send()

    def add1():
        for v in range(4):
            _, _, far, c, _ = orders[v]
            for i in range(2):

                def step(q, _):
                    p1[v, i, q] = p1[v, i, q] + tv[block(v, c if i == 0 else far(c), q)]
                    return 0

                lax.fori_loop(0, 4, step, 0)

    def add2():
        for v in range(4):
            p2[v] = p2[v] + p1[v, 0]

    def add3():
        for v in range(4):
            _, _, far, _, e = orders[v]
            p3[v, 0] = p3[v, 0] + p2[v, e]
            p3[v, 1] = p3[v, 1] + p2[v, far(e)]

    rows_go, rows_in, rows_out = over(n, seq_peer, rows_copy, s)
    ag_go, ag_in, ag_out = over(m, req_peer, gather_copy, b)
    part_go, part_in, part_out = over(n, seq_peer, part_copy, s)
    h1_go, h1_in, h1_out = over(m, req_peer, h1_copy, b)
    h2_go, h2_in, h2_out = over(n, seq_peer, h2_copy, s)
    m1_go, m1_in, m1_out = over(m, req_peer, m1_copy, b)
    m2_go, m2_in, m2_out = over(n, seq_peer, m2_copy, s)

    rows_go()

    def w_copy(p):
        cols = pl.ds(pl.multiple_of(p * depth, depth), depth)
        return remote(
            w_ref.at[:, cols], wbuf.at[w_slot], w_s.at[p], w_r.at[w_slot], {"req": p, "seq": w_place}
        )

    def w_start(i, _):
        p = lax.rem(b + i, m)

        @pl.when(jnp.logical_not(to_self & (p == b)))
        def _():
            w_copy(p).start()

        return 0

    lax.fori_loop(0, m, w_start, 0)

    @pl.when(to_self)
    def _():
        wbuf[w_slot] = w_ref[:, pl.ds(pl.multiple_of(b * depth, depth), depth)]

    rrecv[s] = rows_ref[s]
    each(1, go)
    rows_in()
    ragg[b] = jnp.sum(rrecv[...], axis=0)
    ag_go()
    ag_in()

    def w_arrive(i, _):
        @pl.when(jnp.logical_not((from_b == b) & (from_s + i == s)))
        def _():
            remote(
                w_ref.at[:, pl.ds(0, depth)], wbuf.at[i], w_s.at[i], w_r.at[i], {"req": i, "seq": w_place}
            ).wait_recv()

        return 0

    lax.fori_loop(0, m, w_arrive, 0)

    lhs = ragg[...].reshape(8 * m, 128).astype(BF16)
    weights = wbuf[...].reshape(m * 32, depth)
    place = lax.broadcasted_iota(jnp.int32, (8 * m, depth), 0)
    both = jnp.where(place % 8 < 4, dot(lhs, weights[0:128]), dot(lhs, weights[128:256]))
    both = both + pltpu.roll(both, 4, 0)
    part[...] = both.reshape(m, 8, depth)
    part_go()
    precv[s] = part[s // 2, :, pl.ds(pl.multiple_of(lax.rem(s, 2) * 256, 256), 256)]
    each(1, got)
    tload.wait()
    add1()
    each(2, go)
    part_in()
    cols = pl.ds(pl.multiple_of(b * depth + lax.rem(s, 2) * 256, 256), 256)
    resid = resid_ref[s // 2, :, cols].astype(F32)
    hidden = jnp.sum(precv[...], axis=0) + jnp.concatenate([resid, resid], axis=0)
    upper = pltpu.roll(hidden[:, 128:256], 4, 0)
    eight = lax.broadcasted_iota(jnp.int32, (8, 128), 0)
    h1[b] = jnp.where(eight < 4, upper, hidden[:, 0:128]).astype(BF16)
    h1_go()
    h1_in()
    h2_go()
    h2[s // 2, lax.rem(s, 2)] = h1[...]
    each(2, got)
    add2()
    each(3, go)
    h2_in()

    for k in range(m):
        for q in range(2):
            piece = h2[:, q, k].astype(F32).reshape(8 * m, 128)
            lo = k * depth + q * 256
            hf[:, lo : lo + 128] = piece
            hf[:, lo + 128 : lo + 256] = pltpu.roll(piece, 4, 0)
    h = hf[...]
    hid_ref[0] = hf[pl.ds(pl.multiple_of(b * 8, 8), 8), :].astype(BF16)[SEQS:]
    scale = lax.rsqrt(jnp.mean(h * h, axis=1, keepdims=True) + TINY_FLOOR)
    normed = (h * scale * gain_ref[...]).astype(BF16)
    load.wait()
    top = jnp.full((1, 8 * m), -jnp.inf, F32)
    chunk = 256
    for k in range(vbuf.shape[0] // chunk):
        logits = dot_nt(vbuf[k * chunk : (k + 1) * chunk, :], normed)
        top = jnp.maximum(top, jnp.max(logits, axis=0, keepdims=True))
    top = jnp.concatenate([top, top], axis=1)
    mx1[b] = jnp.broadcast_to(top, (8, 128))
    m1_go()
    each(3, got)
    add3()
    each(4, go)
    m1_in()
    mx2[s] = jnp.max(mx1[...], axis=0)
    m2_go()

    each(4, got)
    for v in range(4):
        p4[v] = p4[v] + p3[v, 0]
    for r in range(SEQS - 1):
        share = jnp.concatenate([p4[v, r].astype(F32) for v in range(4)], axis=0)
        fin_ref[r] = reach_ref[r] + share
    fin_ref[SEQS - 1] = reach_ref[SEQS - 1]
    m2_in()
    best = jnp.max(mx2[...], axis=0)[0:1]
    lanes = lax.broadcasted_iota(jnp.int32, (1, 128), 1)
    four = lax.broadcasted_iota(jnp.int32, (1, SEQS), 1)
    top = jnp.zeros((1, SEQS), F32)
    for r in range(SEQS):
        one = jnp.max(jnp.where(lanes == b * 8 + SEQS + r, best, -jnp.inf), axis=1, keepdims=True)
        top = jnp.where(four == r, one, top)
    max_ref[...] = top

    for drain in (rows_out, ag_out, part_out, h1_out, h2_out, m1_out, m2_out):
        drain()

    def w_drain(p, _):
        @pl.when(jnp.logical_not(to_self & (p == b)))
        def _():
            w_copy(p).wait_send()

        return 0

    lax.fori_loop(0, m, w_drain, 0)

    for act in range(1, 5):
        each(act, sent)


def tail(rows, out_weight, tails, reached, resid, gain, vocab, n, m):
    width = D // n
    vmem = pl.BlockSpec(memory_space=pltpu.VMEM)
    dma = pltpu.SemaphoreType.DMA
    return pl.pallas_call(
        functools.partial(tail_kernel, n, m),
        in_specs=[vmem] * 2
        + [pl.BlockSpec(memory_space=pl.ANY)]
        + [vmem] * 3
        + [pl.BlockSpec(memory_space=pl.ANY)],
        out_specs=[vmem] * 3,
        out_shape=[
            jax.ShapeDtypeStruct((1, SEQS, D), BF16),
            jax.ShapeDtypeStruct((1, SEQS), F32),
            jax.ShapeDtypeStruct((SEQS, STATE, width), F32),
        ],
        scratch_shapes=[
            pltpu.VMEM(vocab.shape, BF16),
            pltpu.VMEM((n, 8, 128), F32),
            pltpu.VMEM((m, 8, 128), F32),
            pltpu.VMEM((m, 32, D // m), BF16),
            pltpu.VMEM((m, 8, D // m), F32),
            pltpu.VMEM((n, 8, 256), F32),
            pltpu.VMEM((m, 8, 128), BF16),
            pltpu.VMEM((n // 2, 2, m, 8, 128), BF16),
            pltpu.VMEM((8 * m, D), F32),
            pltpu.VMEM(tails.shape, BF16),
            pltpu.VMEM((m, 8, 128), F32),
            pltpu.VMEM((n, 8, 128), F32),
            pltpu.VMEM((4, 2, 4, SEQS - 1, 32, width), BF16),
            pltpu.VMEM((4, 4, SEQS - 1, 32, width), BF16),
            pltpu.VMEM((4, 2, SEQS - 1, 32, width), BF16),
            pltpu.VMEM((4, SEQS - 1, 32, width), BF16),
            dma,
            dma,
            dma((n,)),
            dma((n,)),
            dma((m,)),
            dma((m,)),
            dma((m,)),
            dma((m,)),
            dma((n,)),
            dma((n,)),
            dma((m,)),
            dma((m,)),
            dma((n,)),
            dma((n,)),
            dma((m,)),
            dma((m,)),
            dma((n,)),
            dma((n,)),
            dma((4, 2, 4)),
            dma((4, 2, 4)),
            dma((4, 4)),
            dma((4, 4)),
            dma((4, 2)),
            dma((4, 2)),
            dma((4,)),
            dma((4,)),
        ],
        compiler_params=pltpu.CompilerParams(
            collective_id=1, has_side_effects=True, vmem_limit_bytes=VMEM_LIMIT
        ),
        name="tail",
    )(rows, out_weight, tails, reached, resid, gain, vocab)


def pack_kernel(fin_ref, hid_ref, top_ref, fin_out, hid_out, top_out):
    for r in range(SEQS):
        fin_out[r] = fin_ref[r].T
    hid_out[...] = hid_ref[...]
    top_out[...] = top_ref[...]


def pack(final, hid, top):
    vmem = pl.BlockSpec(memory_space=pltpu.VMEM)
    return pl.pallas_call(
        pack_kernel,
        in_specs=[vmem] * 3,
        out_specs=[vmem] * 3,
        out_shape=[
            jax.ShapeDtypeStruct((final.shape[0], final.shape[2], final.shape[1]), F32),
            jax.ShapeDtypeStruct(hid.shape, BF16),
            jax.ShapeDtypeStruct(top.shape, F32),
        ],
        name="pack",
    )(final, hid, top)


def body(
    conv_input,
    gate_projected,
    step_raw,
    step_bias,
    decay_log,
    head_direct_gain,
    conv_weight,
    convolution_bias,
    norm_weight,
    lengths,
    out_weight,
    residual_last,
    final_gain,
    vocab_weight,
):
    seq_count = lax.axis_size("seq")
    req_count = lax.axis_size("req")
    conv = conv_input[0]
    halo = halo_rows(conv, seq_count)
    lead_parts, passed, states, tails, aux, c, lead, xb, sc, cum, rt, dx = local_pass(
        lengths,
        conv,
        halo,
        conv_weight,
        convolution_bias[None],
        step_raw[0].T,
        step_bias[None],
        decay_log[None],
        head_direct_gain[None],
    )
    entering, reached, y = exchange(
        states, aux, dx, xb, sc, cum, rt, lead_parts, passed, c, seq_count
    )
    gated, rows = finish(lengths, y, c, entering, lead, gate_projected[0], norm_weight[None])
    hid, top, final = tail(
        rows, out_weight, tails, reached, residual_last, final_gain[None], vocab_weight, seq_count, req_count
    )
    final, hid, top = pack(final, hid, top)
    final_states = final.reshape(SEQS, HEADS // seq_count, CHANNEL_WIDTH, STATE)[None]
    return (gated[None], final_states, hid, top)


def solution(mesh):
    return jax.shard_map(
        body,
        mesh=mesh,
        in_specs=(
            P("req", "seq", None),
            P("req", "seq", None),
            P("req", "seq", None),
            P(),
            P(),
            P(),
            P(),
            P(),
            P(),
            P("req", None),
            P(("req", "seq"), None),
            P(),
            P(),
            P(("req", "seq"), None),
        ),
        out_specs=(
            P("req", "seq", None),
            P("req", None, "seq", None, None),
            P("req", None, None),
            P("req", None),
        ),
        check_vma=False,
    )
```
